128 devices in a mesh: dom: 64 (over y, z, x), head: 2 (over core).
Axes of the slice: x: 4, y: 4, z: 4, core: 2. Of those that a mesh axis runs over, the one named last changes fastest.
Arguments:
- vertex_state: bfloat16 [131072, 128], P('dom'), may hold values from -6 to 6
- link_state_slotted: bfloat16 [786432, 128], P('dom'), may hold values from -6 to 6
- source_vertex_ids: int32 [786432], P('dom'), may hold values from 0 to 4095
- target_vertex_ids: int32 [786432], P('dom'), may hold values from 0 to 2047
- active_link_tally: int32 [64], P('dom'), may hold values from 6144 to 12288, as said below
- halo_outgoing_ids: int32 [64, 4, 512], P('dom'), may hold values from 0 to 2047
- link_layer_alpha: bfloat16 [384, 128], replicated, may hold values from -0.3125 to 0.3125
- link_layer_beta: bfloat16 [128, 128], replicated, may hold values from -0.5 to 0.5
- link_layer_gamma: bfloat16 [128, 128], replicated, may hold values from -0.5 to 0.5
- link_scale_factor: float32 [128], replicated, may hold values from 0.25 to 1.75
- vertex_layer_alpha: bfloat16 [256, 128], replicated, may hold values from -0.375 to 0.375
- vertex_layer_beta: bfloat16 [128, 128], replicated, may hold values from -0.5 to 0.5
- vertex_layer_gamma: bfloat16 [128, 128], replicated, may hold values from -0.5 to 0.5
- vertex_scale_factor: float32 [128], replicated, may hold values from 0.25 to 1.75
- focus_scale_factor: float32 [128], replicated, may hold values from 0.25 to 1.75
- vertex_content_factor: bfloat16 [128, 128], P(None, 'head'), may hold values from -0.5 to 0.5
- cluster_affinity_factor: bfloat16 [128, 512], P(None, 'head'), may hold values from -0.5 to 0.5
- softness_level: float32 [8], P('head'), may hold values from 0.15 to 2, as said below
- cluster_probe_lookup: float32 [2, 8, 16, 16], P(None, 'head'), may hold values from -8 to 8
- cluster_content_linear: float32 [8, 16, 16], P('head'), may hold values from -1.5 to 1.5
- closing_linear_factor: bfloat16 [128, 128], P('head'), may hold values from -0.5 to 0.5
Outputs:
- result: bfloat16 [131072, 128], P('dom')
The draws below stay inside these ranges and needn't reach their ends.
Inputs may be any that keep to these rules, and one draw needn't show every extreme that they name: `active_link_tally`: each count lies between half the slots and all of them; in every draw some partition's slots are all valid. `softness_level`: positive.
All inputs are finite; a program needn't handle non-finite values.
Results may differ from the reference program's by a relative error of at most 0.0085.
Values may be sent and summed in bfloat16 or wider, within the bound.
A program may use at most 64 MiB of HBM per device.

```python
import math
import jax
import jax.numpy as jnp
from jax import lax

D = 128
FOCUS_CHANNELS = 8
HEAD_DIM = 16
GROUPS_PER_LANE = 64
LOCAL_NODES = 2048
NBRS = 4
HALO = 512
EDGE_CAP = 12288
PARTS_SIZE = 64


def draw_active_link_tally(key, part):
    counts = jax.random.randint(jax.random.fold_in(key, 11), (PARTS_SIZE,), EDGE_CAP // 2, EDGE_CAP + 1)
    fullest = jax.random.randint(jax.random.fold_in(key, 12), (), 0, PARTS_SIZE)
    return jnp.where(jnp.arange(PARTS_SIZE) == fullest, EDGE_CAP, counts).astype(jnp.int32)


def draw_softness_level(key, part):
    unit = jax.random.uniform(key, (FOCUS_CHANNELS,), jnp.float32)
    return jnp.exp(jnp.log(0.3) + unit * (jnp.log(2.0) - jnp.log(0.3)))


def draw_cluster_probe_lookup(key, part):
    return jnp.clip(jax.random.normal(key, (2, FOCUS_CHANNELS, HEAD_DIM, HEAD_DIM), jnp.float32) * 3.0, -8.0, 8.0)


def place_ends(values, key, low, top_value):
    shape = values.shape
    index_at = [jax.random.randint(jax.random.fold_in(key, axis), (), 0, shape[axis]) for axis in range(len(shape))]
    values = values.at[tuple(index_at)].set(low)
    longest = shape.index(max(shape))
    index_at[longest] = (index_at[longest] + 1) % shape[longest]
    return values.at[tuple(index_at)].set(top_value)


def levels(own_key, shape, split, smallest, high):
    factor_of = 1.0
    for position, parts in split:
        draws = jax.random.uniform(jax.random.fold_in(jax.random.fold_in(own_key, 6), position), (parts,), jnp.float32, smallest / len(split), high / len(split))
        factor_of = factor_of * jnp.repeat(jnp.exp(draws), shape[position] // parts).reshape((-1,) + (1,) * (len(shape) - 1 - position))
    return factor_of


def scatter_about(key, shape, scale, limit, cuts=(), held_as=jnp.bfloat16):
    values = scale * jax.random.normal(key, shape, jnp.float32)
    if cuts:
        values = values * levels(key, shape, cuts, -0.22, 0.18)
    return jnp.clip(values, -limit, limit).astype(held_as)


def setup_inputs(seed: int = 0) -> dict:
    splits = jax.random.split(jax.random.key(seed), 22)
    return {
        "vertex_state": scatter_about(splits[0], (PARTS_SIZE * LOCAL_NODES, D), 1.0, 6.0, ((0, 64),)),
        "link_state_slotted": scatter_about(splits[1], (PARTS_SIZE * EDGE_CAP, D), 1.0, 6.0, ((0, 64),)),
        "source_vertex_ids": place_ends(jax.random.randint(splits[2], (PARTS_SIZE * EDGE_CAP,), 0, LOCAL_NODES + NBRS * HALO), jax.random.fold_in(splits[2], 1), 0, (LOCAL_NODES + NBRS * HALO) - 1).astype(jnp.int32),
        "target_vertex_ids": place_ends(jax.random.randint(splits[3], (PARTS_SIZE * EDGE_CAP,), 0, LOCAL_NODES), jax.random.fold_in(splits[3], 1), 0, LOCAL_NODES - 1).astype(jnp.int32),
        "active_link_tally": draw_active_link_tally(jax.random.fold_in(splits[21], 71), 0),
        "halo_outgoing_ids": place_ends(jax.random.randint(splits[5], (PARTS_SIZE, NBRS, HALO), 0, LOCAL_NODES), jax.random.fold_in(splits[5], 1), 0, LOCAL_NODES - 1).astype(jnp.int32),
        "link_layer_alpha": scatter_about(splits[6], (3 * D, D), (3 * D) ** -0.5, 0.3125),
        "link_layer_beta": scatter_about(splits[7], (D, D), D ** -0.5, 0.5),
        "link_layer_gamma": scatter_about(splits[8], (D, D), D ** -0.5, 0.5),
        "link_scale_factor": jnp.clip(1.0 + 0.15 * jax.random.normal(splits[9], (D,), jnp.float32), 0.25, 1.75),
        "vertex_layer_alpha": scatter_about(splits[10], (2 * D, D), (2 * D) ** -0.5, 0.375),
        "vertex_layer_beta": scatter_about(splits[11], (D, D), D ** -0.5, 0.5),
        "vertex_layer_gamma": scatter_about(splits[12], (D, D), D ** -0.5, 0.5),
        "vertex_scale_factor": jnp.clip(1.0 + 0.15 * jax.random.normal(splits[13], (D,), jnp.float32), 0.25, 1.75),
        "focus_scale_factor": jnp.clip(1.0 + 0.15 * jax.random.normal(splits[14], (D,), jnp.float32), 0.25, 1.75),
        "vertex_content_factor": scatter_about(splits[15], (D, D), D ** -0.5, 0.5, ((1, 2),)),
        "cluster_affinity_factor": scatter_about(splits[16], (D, FOCUS_CHANNELS * GROUPS_PER_LANE), D ** -0.5, 0.5, ((1, 2),)),
        "softness_level": draw_softness_level(jax.random.fold_in(splits[21], 71), 0),
        "cluster_probe_lookup": draw_cluster_probe_lookup(jax.random.fold_in(splits[21], 71), 0),
        "cluster_content_linear": scatter_about(splits[19], (FOCUS_CHANNELS, HEAD_DIM, HEAD_DIM), HEAD_DIM ** -0.5, 1.5, ((0, 2),), jnp.float32),
        "closing_linear_factor": scatter_about(splits[20], (D, D), D ** -0.5, 0.5, ((0, 2),)),
    }


def linear_combination(left, right):
    return jnp.dot(left.astype(jnp.float32), right.astype(jnp.float32), preferred_element_type=jnp.float32)

def layer_norm(values, gain_row):
    row_mean = lax.optimization_barrier(jnp.mean(values, axis=-1, keepdims=True))
    centred = values - row_mean
    row_var = lax.optimization_barrier(jnp.mean(centred * centred, axis=-1, keepdims=True))
    return centred * lax.rsqrt(row_var + 1e-05) * gain_row.astype(jnp.float32)

def reference(vertex_state, link_state_slotted, source_vertex_ids, target_vertex_ids, active_link_tally, halo_outgoing_ids, link_layer_alpha, link_layer_beta, link_layer_gamma, link_scale_factor, vertex_layer_alpha, vertex_layer_beta, vertex_layer_gamma, vertex_scale_factor, focus_scale_factor, vertex_content_factor, cluster_affinity_factor, softness_level, cluster_probe_lookup, cluster_content_linear, closing_linear_factor):
    nodes_all = vertex_state.reshape(PARTS_SIZE, LOCAL_NODES, D)
    edges_all = link_state_slotted.reshape(PARTS_SIZE, EDGE_CAP, D)
    send_all = source_vertex_ids.reshape(PARTS_SIZE, EDGE_CAP)
    recv_all = target_vertex_ids.reshape(PARTS_SIZE, EDGE_CAP)
    offsets = (1, -1, 2, -2)

    def process(partition):
        own_rows = nodes_all[partition]
        pieces = [own_rows]
        for neighbour in range(4):
            source = partition - offsets[neighbour]
            inside = jnp.logical_and(source >= 0, source < PARTS_SIZE)
            clipped = jnp.clip(source, 0, PARTS_SIZE - 1).astype(jnp.int32)
            fetched = jnp.take(nodes_all[clipped], halo_outgoing_ids[clipped, neighbour], axis=0)
            pieces.append(jnp.where(inside, fetched, jnp.zeros_like(fetched)))
        extended = jnp.concatenate(pieces, axis=0)
        edge_rows = edges_all[partition]
        sender_rows = jnp.take(extended, send_all[partition], axis=0)
        receiver_rows = jnp.take(own_rows, recv_all[partition], axis=0)
        pre = linear_combination(jnp.concatenate([edge_rows, sender_rows, receiver_rows], axis=1), link_layer_alpha)
        first = jax.nn.silu(pre).astype(jnp.bfloat16)
        second = jax.nn.silu(linear_combination(first, link_layer_beta)).astype(jnp.bfloat16)
        edge_new = (edge_rows.astype(jnp.float32) + layer_norm(linear_combination(second, link_layer_gamma), link_scale_factor)).astype(jnp.bfloat16)
        live = jnp.arange(EDGE_CAP, dtype=jnp.int32) < active_link_tally[partition]
        messages = jnp.where(live[:, None], edge_new.astype(jnp.float32), jnp.float32(0.0))
        summed = jax.ops.segment_sum(messages, recv_all[partition], num_segments=LOCAL_NODES).astype(jnp.bfloat16)
        node_one = jax.nn.silu(linear_combination(jnp.concatenate([own_rows, summed], axis=1), vertex_layer_alpha)).astype(jnp.bfloat16)
        node_two = jax.nn.silu(linear_combination(node_one, vertex_layer_beta)).astype(jnp.bfloat16)
        refreshed_vertices = (own_rows.astype(jnp.float32) + layer_norm(linear_combination(node_two, vertex_layer_gamma), vertex_scale_factor)).astype(jnp.bfloat16)
        standardised_entries = layer_norm(refreshed_vertices.astype(jnp.float32), focus_scale_factor).astype(jnp.bfloat16)
        values = linear_combination(standardised_entries, vertex_content_factor).astype(jnp.bfloat16)
        cluster_affinities = linear_combination(standardised_entries, cluster_affinity_factor).reshape(LOCAL_NODES, FOCUS_CHANNELS, GROUPS_PER_LANE) / softness_level[None, :, None]
        weights = jax.nn.softmax(cluster_affinities, axis=-1)
        weights_b = weights.astype(jnp.bfloat16)
        numer = jnp.einsum('nhs,nhc->hsc', weights_b.astype(jnp.float32), values.reshape(LOCAL_NODES, FOCUS_CHANNELS, HEAD_DIM).astype(jnp.float32))
        denom = lax.optimization_barrier(jnp.sum(weights, axis=0))
        return (refreshed_vertices, weights_b, numer, denom)
    refreshed_vertices, weights_b, numer, denom = lax.map(process, jnp.arange(PARTS_SIZE, dtype=jnp.int32))
    tokens = lax.optimization_barrier(jnp.sum(numer, axis=0)) / lax.optimization_barrier(jnp.sum(denom, axis=0))[:, :, None]
    highest = lax.Precision.HIGHEST
    query = jnp.einsum('hsc,hcd->hsd', tokens, cluster_probe_lookup[0], precision=highest)
    keys = jnp.einsum('hsc,hcd->hsd', tokens, cluster_probe_lookup[1], precision=highest)
    carried = jnp.einsum('hsc,hcd->hsd', tokens, cluster_content_linear, precision=highest)
    scores = jnp.einsum('hsd,htd->hst', query, keys, precision=highest) / math.sqrt(HEAD_DIM)
    mixing = jax.nn.softmax(scores, axis=-1)
    slice_out = jnp.einsum('hst,htd->hsd', mixing, carried, precision=highest).astype(jnp.bfloat16)

    def finish(partition):
        attended = jnp.einsum('nhs,hsd->nhd', weights_b[partition].astype(jnp.float32), slice_out.astype(jnp.float32))
        attended = attended.reshape(LOCAL_NODES, D).astype(jnp.bfloat16)
        return (refreshed_vertices[partition].astype(jnp.float32) + linear_combination(attended, closing_linear_factor)).astype(jnp.bfloat16)
    return lax.map(finish, jnp.arange(PARTS_SIZE, dtype=jnp.int32)).reshape(PARTS_SIZE * LOCAL_NODES, D)
```

```python
import functools
import math

import jax
import jax.numpy as jnp
from jax import lax
from jax.experimental import pallas as pl
from jax.experimental.pallas import tpu as pltpu
from jax.sharding import PartitionSpec as P

HEAD_DIM = 16
GROUPS_PER_LANE = 64


def passed_along(value, axis, steps):
    count = lax.axis_size(axis)
    first, last = (max(0, -steps), min(count, count - steps))
    return lax.ppermute(value, axis, [(source, source + steps) for source in range(first, last)])


def _doubling_kernel(steps, x_ref, o_ref, inbox, send_sem, recv_sem):
    me = lax.axis_index("dom")
    partners = []
    for k in range(steps):
        span = 2**k
        bit = (me // span) % 2
        partners.append(me + span - 2 * span * bit)
    barrier = pltpu.get_barrier_semaphore()
    for partner in partners:
        pl.semaphore_signal(
            barrier, 1, device_id={"dom": partner}, device_id_type=pl.DeviceIdType.MESH
        )
    pl.semaphore_wait(barrier, steps)
    for k in range(steps):
        source = x_ref if k == 0 else o_ref
        copy = pltpu.make_async_remote_copy(
            src_ref=source,
            dst_ref=inbox.at[k],
            send_sem=send_sem.at[k],
            recv_sem=recv_sem.at[k],
            device_id={"dom": partners[k]},
            device_id_type=pl.DeviceIdType.MESH,
        )
        copy.start()
        copy.wait()
        o_ref[...] = source[...] + inbox[k]


def dom_sum(flat):
    count = lax.axis_size("dom")
    steps = count.bit_length() - 1
    return pl.pallas_call(
        functools.partial(_doubling_kernel, steps),
        out_shape=jax.ShapeDtypeStruct(flat.shape, flat.dtype),
        in_specs=[pl.BlockSpec(memory_space=pltpu.VMEM)],
        out_specs=pl.BlockSpec(memory_space=pltpu.VMEM),
        scratch_shapes=[
            pltpu.VMEM((steps,) + flat.shape, flat.dtype),
            pltpu.SemaphoreType.DMA((steps,)),
            pltpu.SemaphoreType.DMA((steps,)),
        ],
        compiler_params=pltpu.CompilerParams(collective_id=0, has_side_effects=True),
    )(flat)


def psum_slices(numer, denom):
    joined = jnp.concatenate([numer.reshape(-1), denom.reshape(-1)])
    rows = -(-joined.shape[0] // 1024) * 8
    padded = jnp.zeros((rows * 128,), joined.dtype).at[: joined.shape[0]].set(joined)
    total = dom_sum(padded.reshape(rows, 128)).reshape(-1)
    numer_size = numer.size
    return (
        total[:numer_size].reshape(numer.shape),
        total[numer_size : numer_size + denom.size].reshape(denom.shape),
    )


def layer_norm(values, gain_row):
    row_mean = jnp.mean(values, axis=-1, keepdims=True)
    centred = values - row_mean
    row_var = jnp.mean(centred * centred, axis=-1, keepdims=True)
    return centred * lax.rsqrt(row_var + 1e-05) * gain_row


def node_section(
    own_rows,
    summed_b,
    vertex_layer_alpha,
    vertex_layer_beta,
    vertex_layer_gamma,
    vertex_scale_factor,
):
    feature_width = own_rows.shape[1]
    node_pre = jnp.dot(
        own_rows, vertex_layer_alpha[:feature_width], preferred_element_type=jnp.float32
    )
    node_pre = node_pre + jnp.dot(
        summed_b, vertex_layer_alpha[feature_width:], preferred_element_type=jnp.float32
    )
    node_one = jax.nn.silu(node_pre).astype(jnp.bfloat16)
    node_two = jax.nn.silu(
        jnp.dot(node_one, vertex_layer_beta, preferred_element_type=jnp.float32)
    ).astype(jnp.bfloat16)
    node_three = jnp.dot(node_two, vertex_layer_gamma, preferred_element_type=jnp.float32)
    return (own_rows.astype(jnp.float32) + layer_norm(node_three, vertex_scale_factor)).astype(
        jnp.bfloat16
    )


def slice_partial_terms(
    refreshed_vertices,
    focus_scale_factor,
    vertex_content_factor,
    cluster_affinity_factor,
    softness_level,
):
    count_of_rows = refreshed_vertices.shape[0]
    domain_channel_split = softness_level.shape[0]
    standardised_entries = layer_norm(
        refreshed_vertices.astype(jnp.float32), focus_scale_factor
    ).astype(jnp.bfloat16)
    values = jnp.dot(
        standardised_entries, vertex_content_factor, preferred_element_type=jnp.float32
    ).astype(jnp.bfloat16)
    cluster_affinities = jnp.dot(
        standardised_entries, cluster_affinity_factor, preferred_element_type=jnp.float32
    )
    cluster_affinities = (
        cluster_affinities.reshape(count_of_rows, domain_channel_split, GROUPS_PER_LANE)
        / softness_level[None, :, None]
    )
    weights = jax.nn.softmax(cluster_affinities, axis=-1)
    weights_b = weights.astype(jnp.bfloat16)
    numer = jnp.einsum(
        "nhs,nhc->hsc",
        weights_b,
        values.reshape(count_of_rows, domain_channel_split, HEAD_DIM),
        preferred_element_type=jnp.float32,
    )
    denom = jnp.sum(weights, axis=0)
    return (weights_b, numer, denom)


def slice_mixing(numer, denom, cluster_probe_lookup, cluster_content_linear):
    tokens = numer / denom[:, :, None]
    highest = lax.Precision.HIGHEST
    query = jnp.einsum("hsc,hcd->hsd", tokens, cluster_probe_lookup[0], precision=highest)
    keys = jnp.einsum("hsc,hcd->hsd", tokens, cluster_probe_lookup[1], precision=highest)
    carried = jnp.einsum("hsc,hcd->hsd", tokens, cluster_content_linear, precision=highest)
    scores = jnp.einsum("hsd,htd->hst", query, keys, precision=highest) / math.sqrt(HEAD_DIM)
    mixing = jax.nn.softmax(scores, axis=-1)
    return jnp.einsum("hst,htd->hsd", mixing, carried, precision=highest).astype(jnp.bfloat16)


def attend_rows(weights_b, slice_out):
    count_of_rows = weights_b.shape[0]
    domain_channel_split = weights_b.shape[1]
    attended = jnp.einsum("nhs,hsd->nhd", weights_b, slice_out, preferred_element_type=jnp.float32)
    return attended.reshape(count_of_rows, domain_channel_split * HEAD_DIM).astype(jnp.bfloat16)


def pick_rows(table, row_ids):
    table_ids = jnp.arange(table.shape[0], dtype=jnp.int32)
    selector = (row_ids[:, None] == table_ids[None, :]).astype(jnp.bfloat16)
    return jnp.dot(selector, table, preferred_element_type=jnp.float32).astype(jnp.bfloat16)


def body(
    vertex_state,
    link_state_slotted,
    source_vertex_ids,
    target_vertex_ids,
    active_link_tally,
    halo_outgoing_ids,
    link_layer_alpha,
    link_layer_beta,
    link_layer_gamma,
    link_scale_factor,
    vertex_layer_alpha,
    vertex_layer_beta,
    vertex_layer_gamma,
    vertex_scale_factor,
    focus_scale_factor,
    vertex_content_factor,
    cluster_affinity_factor,
    softness_level,
    cluster_probe_lookup,
    cluster_content_linear,
    closing_linear_factor,
):
    node_count = vertex_state.shape[0]
    feature_width = vertex_state.shape[1]
    capacity = link_state_slotted.shape[0]
    offsets = (1, -1, 2, -2)
    pieces = [vertex_state]
    for neighbour in range(4):
        outgoing = pick_rows(vertex_state, halo_outgoing_ids[0, neighbour])
        pieces.append(passed_along(outgoing, "dom", offsets[neighbour]))
    extended = jnp.concatenate(pieces, axis=0)
    extended_ids = jnp.arange(extended.shape[0], dtype=jnp.int32)
    node_ids = jnp.arange(node_count, dtype=jnp.int32)
    block_rows = min(node_count, 1024)
    share = capacity // lax.axis_size("head")
    first_row = lax.axis_index("head") * share
    edge_rows = lax.dynamic_slice_in_dim(link_state_slotted, first_row, share, 0)
    send_rows = lax.dynamic_slice_in_dim(source_vertex_ids, first_row, share, 0)
    recv_rows = lax.dynamic_slice_in_dim(target_vertex_ids, first_row, share, 0)
    turns = edge_rows.shape[0] // block_rows
    edge_blocks = edge_rows.reshape(turns, block_rows, feature_width)
    send_blocks = send_rows.reshape(turns, block_rows)
    recv_blocks = recv_rows.reshape(turns, block_rows)

    def step(total, item):
        edge_part, send_part, recv_part, turn = item
        send_hot = (send_part[:, None] == extended_ids[None, :]).astype(jnp.bfloat16)
        recv_hot = (recv_part[:, None] == node_ids[None, :]).astype(jnp.bfloat16)
        sender_rows = jnp.dot(send_hot, extended, preferred_element_type=jnp.float32).astype(
            jnp.bfloat16
        )
        receiver_rows = jnp.dot(recv_hot, vertex_state, preferred_element_type=jnp.float32).astype(
            jnp.bfloat16
        )
        pre = jnp.dot(
            edge_part, link_layer_alpha[:feature_width], preferred_element_type=jnp.float32
        )
        pre = pre + jnp.dot(
            sender_rows,
            link_layer_alpha[feature_width : 2 * feature_width],
            preferred_element_type=jnp.float32,
        )
        pre = pre + jnp.dot(
            receiver_rows, link_layer_alpha[2 * feature_width :], preferred_element_type=jnp.float32
        )
        first = jax.nn.silu(pre).astype(jnp.bfloat16)
        second = jax.nn.silu(
            jnp.dot(first, link_layer_beta, preferred_element_type=jnp.float32)
        ).astype(jnp.bfloat16)
        third = jnp.dot(second, link_layer_gamma, preferred_element_type=jnp.float32)
        edge_new = (edge_part.astype(jnp.float32) + layer_norm(third, link_scale_factor)).astype(
            jnp.bfloat16
        )
        position = first_row + turn * block_rows + jnp.arange(block_rows, dtype=jnp.int32)
        live = position < active_link_tally[0]
        messages = jnp.where(live[:, None], edge_new, jnp.zeros_like(edge_new))
        gathered = lax.dot_general(
            recv_hot, messages, (((0,), (0,)), ((), ())), preferred_element_type=jnp.float32
        )
        return (total + gathered, None)

    start = jnp.zeros((node_count, feature_width), jnp.float32)
    total, unused = lax.scan(
        step, start, (edge_blocks, send_blocks, recv_blocks, jnp.arange(turns, dtype=jnp.int32))
    )
    summed = lax.psum(total, "head")
    refreshed_vertices = node_section(
        vertex_state,
        summed.astype(jnp.bfloat16),
        vertex_layer_alpha,
        vertex_layer_beta,
        vertex_layer_gamma,
        vertex_scale_factor,
    )
    weights_b, numer, denom = slice_partial_terms(
        refreshed_vertices,
        focus_scale_factor,
        vertex_content_factor,
        cluster_affinity_factor,
        softness_level,
    )
    numer, denom = psum_slices(numer, denom)
    slice_out = slice_mixing(numer, denom, cluster_probe_lookup, cluster_content_linear)
    attended = attend_rows(weights_b, slice_out)
    projected = lax.psum(
        jnp.dot(attended, closing_linear_factor, preferred_element_type=jnp.float32).astype(
            jnp.bfloat16
        ),
        "head",
    ).astype(jnp.float32)
    return (refreshed_vertices.astype(jnp.float32) + projected).astype(jnp.bfloat16)


def solution(mesh):
    in_specs = (
        P("dom", None),
        P("dom", None),
        P("dom"),
        P("dom"),
        P("dom"),
        P("dom", None, None),
        P(),
        P(),
        P(),
        P(),
        P(),
        P(),
        P(),
        P(),
        P(),
        P(None, "head"),
        P(None, "head"),
        P("head"),
        P(None, "head", None, None),
        P("head", None, None),
        P("head", None),
    )
    out_specs = P("dom", None)
    return jax.shard_map(body, mesh=mesh, in_specs=in_specs, out_specs=out_specs, check_vma=False)
```

```python
import functools
import math

import jax
import jax.numpy as jnp
from jax import lax
from jax.experimental import pallas as pl
from jax.experimental.pallas import tpu as pltpu
from jax.sharding import PartitionSpec as P

HEAD_DIM = 16
GROUPS_PER_LANE = 64


def passed_along(value, axis, steps):
    count = lax.axis_size(axis)
    first, last = (max(0, -steps), min(count, count - steps))
    return lax.ppermute(value, axis, [(source, source + steps) for source in range(first, last)])


def _doubling_kernel(steps, x_ref, o_ref, inbox, send_sem, recv_sem):
    me = lax.axis_index("dom")
    partners = []
    for k in range(steps):
        span = 2**k
        bit = (me // span) % 2
        partners.append(me + span - 2 * span * bit)
    barrier = pltpu.get_barrier_semaphore()
    for partner in partners:
        pl.semaphore_signal(
            barrier, 1, device_id={"dom": partner}, device_id_type=pl.DeviceIdType.MESH
        )
    pl.semaphore_wait(barrier, steps)
    for k in range(steps):
        source = x_ref if k == 0 else o_ref
        copy = pltpu.make_async_remote_copy(
            src_ref=source,
            dst_ref=inbox.at[k],
            send_sem=send_sem.at[k],
            recv_sem=recv_sem.at[k],
            device_id={"dom": partners[k]},
            device_id_type=pl.DeviceIdType.MESH,
        )
        copy.start()
        copy.wait()
        o_ref[...] = source[...] + inbox[k]


def dom_sum(flat):
    count = lax.axis_size("dom")
    steps = count.bit_length() - 1
    return pl.pallas_call(
        functools.partial(_doubling_kernel, steps),
        out_shape=jax.ShapeDtypeStruct(flat.shape, flat.dtype),
        in_specs=[pl.BlockSpec(memory_space=pltpu.VMEM)],
        out_specs=pl.BlockSpec(memory_space=pltpu.VMEM),
        scratch_shapes=[
            pltpu.VMEM((steps,) + flat.shape, flat.dtype),
            pltpu.SemaphoreType.DMA((steps,)),
            pltpu.SemaphoreType.DMA((steps,)),
        ],
        compiler_params=pltpu.CompilerParams(collective_id=0, has_side_effects=True),
    )(flat)


def psum_slices(numer, denom):
    joined = jnp.concatenate([numer.reshape(-1), denom.reshape(-1)])
    rows = -(-joined.shape[0] // 1024) * 8
    padded = jnp.zeros((rows * 128,), joined.dtype).at[: joined.shape[0]].set(joined)
    total = dom_sum(padded.reshape(rows, 128)).reshape(-1)
    numer_size = numer.size
    return (
        total[:numer_size].reshape(numer.shape),
        total[numer_size : numer_size + denom.size].reshape(denom.shape),
    )


def layer_norm(values, gain_row):
    row_mean = jnp.mean(values, axis=-1, keepdims=True)
    centred = values - row_mean
    row_var = jnp.mean(centred * centred, axis=-1, keepdims=True)
    return centred * lax.rsqrt(row_var + 1e-05) * gain_row


def node_section(
    own_rows,
    summed_b,
    vertex_layer_alpha,
    vertex_layer_beta,
    vertex_layer_gamma,
    vertex_scale_factor,
):
    feature_width = own_rows.shape[1]
    node_pre = jnp.dot(
        own_rows, vertex_layer_alpha[:feature_width], preferred_element_type=jnp.float32
    )
    node_pre = node_pre + jnp.dot(
        summed_b, vertex_layer_alpha[feature_width:], preferred_element_type=jnp.float32
    )
    node_one = jax.nn.silu(node_pre).astype(jnp.bfloat16)
    node_two = jax.nn.silu(
        jnp.dot(node_one, vertex_layer_beta, preferred_element_type=jnp.float32)
    ).astype(jnp.bfloat16)
    node_three = jnp.dot(node_two, vertex_layer_gamma, preferred_element_type=jnp.float32)
    return (own_rows.astype(jnp.float32) + layer_norm(node_three, vertex_scale_factor)).astype(
        jnp.bfloat16
    )


def slice_partial_terms(
    refreshed_vertices,
    focus_scale_factor,
    vertex_content_factor,
    cluster_affinity_factor,
    softness_level,
):
    count_of_rows = refreshed_vertices.shape[0]
    domain_channel_split = softness_level.shape[0]
    standardised_entries = layer_norm(
        refreshed_vertices.astype(jnp.float32), focus_scale_factor
    ).astype(jnp.bfloat16)
    values = jnp.dot(
        standardised_entries, vertex_content_factor, preferred_element_type=jnp.float32
    ).astype(jnp.bfloat16)
    cluster_affinities = jnp.dot(
        standardised_entries, cluster_affinity_factor, preferred_element_type=jnp.float32
    )
    cluster_affinities = (
        cluster_affinities.reshape(count_of_rows, domain_channel_split, GROUPS_PER_LANE)
        / softness_level[None, :, None]
    )
    weights = jax.nn.softmax(cluster_affinities, axis=-1)
    weights_b = weights.astype(jnp.bfloat16)
    numer = jnp.einsum(
        "nhs,nhc->hsc",
        weights_b,
        values.reshape(count_of_rows, domain_channel_split, HEAD_DIM),
        preferred_element_type=jnp.float32,
    )
    denom = jnp.sum(weights, axis=0)
    return (weights_b, numer, denom)


def slice_mixing(numer, denom, cluster_probe_lookup, cluster_content_linear):
    tokens = numer / denom[:, :, None]
    highest = lax.Precision.HIGHEST
    query = jnp.einsum("hsc,hcd->hsd", tokens, cluster_probe_lookup[0], precision=highest)
    keys = jnp.einsum("hsc,hcd->hsd", tokens, cluster_probe_lookup[1], precision=highest)
    carried = jnp.einsum("hsc,hcd->hsd", tokens, cluster_content_linear, precision=highest)
    scores = jnp.einsum("hsd,htd->hst", query, keys, precision=highest) / math.sqrt(HEAD_DIM)
    mixing = jax.nn.softmax(scores, axis=-1)
    return jnp.einsum("hst,htd->hsd", mixing, carried, precision=highest).astype(jnp.bfloat16)


def attend_rows(weights_b, slice_out):
    count_of_rows = weights_b.shape[0]
    domain_channel_split = weights_b.shape[1]
    attended = jnp.einsum("nhs,hsd->nhd", weights_b, slice_out, preferred_element_type=jnp.float32)
    return attended.reshape(count_of_rows, domain_channel_split * HEAD_DIM).astype(jnp.bfloat16)


def pick_rows(table, row_ids):
    table_ids = jnp.arange(table.shape[0], dtype=jnp.int32)
    selector = (row_ids[:, None] == table_ids[None, :]).astype(jnp.bfloat16)
    return jnp.dot(selector, table, preferred_element_type=jnp.float32).astype(jnp.bfloat16)


def body(
    vertex_state,
    link_state_slotted,
    source_vertex_ids,
    target_vertex_ids,
    active_link_tally,
    halo_outgoing_ids,
    link_layer_alpha,
    link_layer_beta,
    link_layer_gamma,
    link_scale_factor,
    vertex_layer_alpha,
    vertex_layer_beta,
    vertex_layer_gamma,
    vertex_scale_factor,
    focus_scale_factor,
    vertex_content_factor,
    cluster_affinity_factor,
    softness_level,
    cluster_probe_lookup,
    cluster_content_linear,
    closing_linear_factor,
):
    node_count = vertex_state.shape[0]
    feature_width = vertex_state.shape[1]
    capacity = link_state_slotted.shape[0]
    offsets = (1, -1, 2, -2)
    pieces = [vertex_state]
    for neighbour in range(4):
        outgoing = pick_rows(vertex_state, halo_outgoing_ids[0, neighbour])
        pieces.append(passed_along(outgoing, "dom", offsets[neighbour]))
    extended = jnp.concatenate(pieces, axis=0)
    extended_ids = jnp.arange(extended.shape[0], dtype=jnp.int32)
    node_ids = jnp.arange(node_count, dtype=jnp.int32)
    block_rows = min(node_count, 1024)
    share = capacity // lax.axis_size("head")
    first_row = lax.axis_index("head") * share
    edge_rows = lax.dynamic_slice_in_dim(link_state_slotted, first_row, share, 0)
    send_rows = lax.dynamic_slice_in_dim(source_vertex_ids, first_row, share, 0)
    recv_rows = lax.dynamic_slice_in_dim(target_vertex_ids, first_row, share, 0)
    turns = edge_rows.shape[0] // block_rows
    edge_blocks = edge_rows.reshape(turns, block_rows, feature_width)
    send_blocks = send_rows.reshape(turns, block_rows)
    recv_blocks = recv_rows.reshape(turns, block_rows)

    def step(total, item):
        edge_part, send_part, recv_part, turn = item
        send_hot = (send_part[:, None] == extended_ids[None, :]).astype(jnp.bfloat16)
        recv_hot = (recv_part[:, None] == node_ids[None, :]).astype(jnp.bfloat16)
        sender_rows = jnp.dot(send_hot, extended, preferred_element_type=jnp.float32).astype(
            jnp.bfloat16
        )
        receiver_rows = jnp.dot(recv_hot, vertex_state, preferred_element_type=jnp.float32).astype(
            jnp.bfloat16
        )
        pre = jnp.dot(
            edge_part, link_layer_alpha[:feature_width], preferred_element_type=jnp.float32
        )
        pre = pre + jnp.dot(
            sender_rows,
            link_layer_alpha[feature_width : 2 * feature_width],
            preferred_element_type=jnp.float32,
        )
        pre = pre + jnp.dot(
            receiver_rows, link_layer_alpha[2 * feature_width :], preferred_element_type=jnp.float32
        )
        first = jax.nn.silu(pre).astype(jnp.bfloat16)
        second = jax.nn.silu(
            jnp.dot(first, link_layer_beta, preferred_element_type=jnp.float32)
        ).astype(jnp.bfloat16)
        third = jnp.dot(second, link_layer_gamma, preferred_element_type=jnp.float32)
        edge_new = (edge_part.astype(jnp.float32) + layer_norm(third, link_scale_factor)).astype(
            jnp.bfloat16
        )
        position = first_row + turn * block_rows + jnp.arange(block_rows, dtype=jnp.int32)
        live = position < active_link_tally[0]
        messages = jnp.where(live[:, None], edge_new, jnp.zeros_like(edge_new))
        gathered = lax.dot_general(
            recv_hot, messages, (((0,), (0,)), ((), ())), preferred_element_type=jnp.float32
        )
        return (total + gathered, None)

    start = jnp.zeros((node_count, feature_width), jnp.float32)
    total, unused = lax.scan(
        step, start, (edge_blocks, send_blocks, recv_blocks, jnp.arange(turns, dtype=jnp.int32))
    )
    summed = lax.psum(total, "head")
    refreshed_vertices = node_section(
        vertex_state,
        summed.astype(jnp.bfloat16),
        vertex_layer_alpha,
        vertex_layer_beta,
        vertex_layer_gamma,
        vertex_scale_factor,
    )
    weights_b, numer, denom = slice_partial_terms(
        refreshed_vertices,
        focus_scale_factor,
        vertex_content_factor,
        cluster_affinity_factor,
        softness_level,
    )
    numer, denom = psum_slices(numer, denom)
    slice_out = slice_mixing(numer, denom, cluster_probe_lookup, cluster_content_linear)
    attended = attend_rows(weights_b, slice_out)
    projected = jnp.dot(attended, closing_linear_factor, preferred_element_type=jnp.float32)
    return (refreshed_vertices.astype(jnp.float32) + projected).astype(jnp.bfloat16)


def solution(mesh):
    in_specs = (
        P("dom", None),
        P("dom", None),
        P("dom"),
        P("dom"),
        P("dom"),
        P("dom", None, None),
        P(),
        P(),
        P(),
        P(),
        P(),
        P(),
        P(),
        P(),
        P(),
        P(),
        P(),
        P(),
        P(),
        P(),
        P(),
    )
    out_specs = P("dom", None)
    return jax.shard_map(body, mesh=mesh, in_specs=in_specs, out_specs=out_specs, check_vma=False)
```

```python
import functools
import math

import jax
import jax.numpy as jnp
from jax import lax
from jax.experimental import pallas as pl
from jax.experimental.pallas import tpu as pltpu
from jax.sharding import PartitionSpec as P

HEAD_DIM = 16
GROUPS_PER_LANE = 64


def passed_along(value, axis, steps):
    count = lax.axis_size(axis)
    first, last = (max(0, -steps), min(count, count - steps))
    return lax.ppermute(value, axis, [(source, source + steps) for source in range(first, last)])


def _doubling_kernel(steps, x_ref, o_ref, inbox, send_sem, recv_sem):
    me = lax.axis_index("dom")
    partners = []
    for k in range(steps):
        span = 2**k
        bit = (me // span) % 2
        partners.append(me + span - 2 * span * bit)
    barrier = pltpu.get_barrier_semaphore()
    for partner in partners:
        pl.semaphore_signal(
            barrier, 1, device_id={"dom": partner}, device_id_type=pl.DeviceIdType.MESH
        )
    pl.semaphore_wait(barrier, steps)
    for k in range(steps):
        source = x_ref if k == 0 else o_ref
        copy = pltpu.make_async_remote_copy(
            src_ref=source,
            dst_ref=inbox.at[k],
            send_sem=send_sem.at[k],
            recv_sem=recv_sem.at[k],
            device_id={"dom": partners[k]},
            device_id_type=pl.DeviceIdType.MESH,
        )
        copy.start()
        copy.wait()
        o_ref[...] = source[...] + inbox[k]


def dom_sum(flat):
    count = lax.axis_size("dom")
    steps = count.bit_length() - 1
    return pl.pallas_call(
        functools.partial(_doubling_kernel, steps),
        out_shape=jax.ShapeDtypeStruct(flat.shape, flat.dtype),
        in_specs=[pl.BlockSpec(memory_space=pltpu.VMEM)],
        out_specs=pl.BlockSpec(memory_space=pltpu.VMEM),
        scratch_shapes=[
            pltpu.VMEM((steps,) + flat.shape, flat.dtype),
            pltpu.SemaphoreType.DMA((steps,)),
            pltpu.SemaphoreType.DMA((steps,)),
        ],
        compiler_params=pltpu.CompilerParams(collective_id=0, has_side_effects=True),
    )(flat)


def psum_slices(numer, denom):
    joined = jnp.concatenate([numer.reshape(-1), denom.reshape(-1)])
    rows = -(-joined.shape[0] // 1024) * 8
    padded = jnp.zeros((rows * 128,), joined.dtype).at[: joined.shape[0]].set(joined)
    total = dom_sum(padded.reshape(rows, 128)).reshape(-1)
    numer_size = numer.size
    return (
        total[:numer_size].reshape(numer.shape),
        total[numer_size : numer_size + denom.size].reshape(denom.shape),
    )


def layer_norm(values, gain_row):
    row_mean = jnp.mean(values, axis=-1, keepdims=True)
    centred = values - row_mean
    row_var = jnp.mean(centred * centred, axis=-1, keepdims=True)
    return centred * lax.rsqrt(row_var + 1e-05) * gain_row


def node_section(
    own_rows,
    summed_b,
    vertex_layer_alpha,
    vertex_layer_beta,
    vertex_layer_gamma,
    vertex_scale_factor,
):
    feature_width = own_rows.shape[1]
    node_pre = jnp.dot(
        own_rows, vertex_layer_alpha[:feature_width], preferred_element_type=jnp.float32
    )
    node_pre = node_pre + jnp.dot(
        summed_b, vertex_layer_alpha[feature_width:], preferred_element_type=jnp.float32
    )
    node_one = jax.nn.silu(node_pre).astype(jnp.bfloat16)
    node_two = jax.nn.silu(
        jnp.dot(node_one, vertex_layer_beta, preferred_element_type=jnp.float32)
    ).astype(jnp.bfloat16)
    node_three = jnp.dot(node_two, vertex_layer_gamma, preferred_element_type=jnp.float32)
    return (own_rows.astype(jnp.float32) + layer_norm(node_three, vertex_scale_factor)).astype(
        jnp.bfloat16
    )


def slice_partial_terms(
    refreshed_vertices,
    focus_scale_factor,
    vertex_content_factor,
    cluster_affinity_factor,
    softness_level,
):
    count_of_rows = refreshed_vertices.shape[0]
    domain_channel_split = softness_level.shape[0]
    standardised_entries = layer_norm(
        refreshed_vertices.astype(jnp.float32), focus_scale_factor
    ).astype(jnp.bfloat16)
    values = jnp.dot(
        standardised_entries, vertex_content_factor, preferred_element_type=jnp.float32
    ).astype(jnp.bfloat16)
    cluster_affinities = jnp.dot(
        standardised_entries, cluster_affinity_factor, preferred_element_type=jnp.float32
    )
    cluster_affinities = (
        cluster_affinities.reshape(count_of_rows, domain_channel_split, GROUPS_PER_LANE)
        / softness_level[None, :, None]
    )
    weights = jax.nn.softmax(cluster_affinities, axis=-1)
    weights_b = weights.astype(jnp.bfloat16)
    numer = jnp.einsum(
        "nhs,nhc->hsc",
        weights_b,
        values.reshape(count_of_rows, domain_channel_split, HEAD_DIM),
        preferred_element_type=jnp.float32,
    )
    denom = jnp.sum(weights, axis=0)
    return (weights_b, numer, denom)


def slice_mixing(numer, denom, cluster_probe_lookup, cluster_content_linear):
    tokens = numer / denom[:, :, None]
    highest = lax.Precision.HIGHEST
    query = jnp.einsum("hsc,hcd->hsd", tokens, cluster_probe_lookup[0], precision=highest)
    keys = jnp.einsum("hsc,hcd->hsd", tokens, cluster_probe_lookup[1], precision=highest)
    carried = jnp.einsum("hsc,hcd->hsd", tokens, cluster_content_linear, precision=highest)
    scores = jnp.einsum("hsd,htd->hst", query, keys, precision=highest) / math.sqrt(HEAD_DIM)
    mixing = jax.nn.softmax(scores, axis=-1)
    return jnp.einsum("hst,htd->hsd", mixing, carried, precision=highest).astype(jnp.bfloat16)


def attend_rows(weights_b, slice_out):
    count_of_rows = weights_b.shape[0]
    domain_channel_split = weights_b.shape[1]
    attended = jnp.einsum("nhs,hsd->nhd", weights_b, slice_out, preferred_element_type=jnp.float32)
    return attended.reshape(count_of_rows, domain_channel_split * HEAD_DIM).astype(jnp.bfloat16)


def pick_rows(table, row_ids):
    table_ids = jnp.arange(table.shape[0], dtype=jnp.int32)
    selector = (row_ids[:, None] == table_ids[None, :]).astype(jnp.bfloat16)
    return jnp.dot(selector, table, preferred_element_type=jnp.float32).astype(jnp.bfloat16)


def body(
    vertex_state,
    link_state_slotted,
    source_vertex_ids,
    target_vertex_ids,
    active_link_tally,
    halo_outgoing_ids,
    link_layer_alpha,
    link_layer_beta,
    link_layer_gamma,
    link_scale_factor,
    vertex_layer_alpha,
    vertex_layer_beta,
    vertex_layer_gamma,
    vertex_scale_factor,
    focus_scale_factor,
    vertex_content_factor,
    cluster_affinity_factor,
    softness_level,
    cluster_probe_lookup,
    cluster_content_linear,
    closing_linear_factor,
):
    node_count = vertex_state.shape[0]
    feature_width = vertex_state.shape[1]
    capacity = link_state_slotted.shape[0]
    offsets = (1, -1, 2, -2)
    pieces = [vertex_state]
    for neighbour in range(4):
        outgoing = pick_rows(vertex_state, halo_outgoing_ids[0, neighbour])
        pieces.append(passed_along(outgoing, "dom", offsets[neighbour]))
    extended = jnp.concatenate(pieces, axis=0)
    extended_ids = jnp.arange(extended.shape[0], dtype=jnp.int32)
    node_ids = jnp.arange(node_count, dtype=jnp.int32)
    block_rows = capacity // lax.axis_size("head")
    share = capacity // lax.axis_size("head")
    first_row = lax.axis_index("head") * share
    edge_rows = lax.dynamic_slice_in_dim(link_state_slotted, first_row, share, 0)
    send_rows = lax.dynamic_slice_in_dim(source_vertex_ids, first_row, share, 0)
    recv_rows = lax.dynamic_slice_in_dim(target_vertex_ids, first_row, share, 0)
    turns = edge_rows.shape[0] // block_rows
    edge_blocks = edge_rows.reshape(turns, block_rows, feature_width)
    send_blocks = send_rows.reshape(turns, block_rows)
    recv_blocks = recv_rows.reshape(turns, block_rows)

    def step(total, item):
        edge_part, send_part, recv_part, turn = item
        send_hot = (send_part[:, None] == extended_ids[None, :]).astype(jnp.bfloat16)
        recv_hot = (recv_part[:, None] == node_ids[None, :]).astype(jnp.bfloat16)
        sender_rows = jnp.dot(send_hot, extended, preferred_element_type=jnp.float32).astype(
            jnp.bfloat16
        )
        receiver_rows = jnp.dot(recv_hot, vertex_state, preferred_element_type=jnp.float32).astype(
            jnp.bfloat16
        )
        pre = jnp.dot(
            edge_part, link_layer_alpha[:feature_width], preferred_element_type=jnp.float32
        )
        pre = pre + jnp.dot(
            sender_rows,
            link_layer_alpha[feature_width : 2 * feature_width],
            preferred_element_type=jnp.float32,
        )
        pre = pre + jnp.dot(
            receiver_rows, link_layer_alpha[2 * feature_width :], preferred_element_type=jnp.float32
        )
        first = jax.nn.silu(pre).astype(jnp.bfloat16)
        second = jax.nn.silu(
            jnp.dot(first, link_layer_beta, preferred_element_type=jnp.float32)
        ).astype(jnp.bfloat16)
        third = jnp.dot(second, link_layer_gamma, preferred_element_type=jnp.float32)
        edge_new = (edge_part.astype(jnp.float32) + layer_norm(third, link_scale_factor)).astype(
            jnp.bfloat16
        )
        position = first_row + turn * block_rows + jnp.arange(block_rows, dtype=jnp.int32)
        live = position < active_link_tally[0]
        messages = jnp.where(live[:, None], edge_new, jnp.zeros_like(edge_new))
        gathered = lax.dot_general(
            recv_hot, messages, (((0,), (0,)), ((), ())), preferred_element_type=jnp.float32
        )
        return (total + gathered, None)

    start = jnp.zeros((node_count, feature_width), jnp.float32)
    total, unused = lax.scan(
        step, start, (edge_blocks, send_blocks, recv_blocks, jnp.arange(turns, dtype=jnp.int32))
    )
    summed = lax.psum(total, "head")
    refreshed_vertices = node_section(
        vertex_state,
        summed.astype(jnp.bfloat16),
        vertex_layer_alpha,
        vertex_layer_beta,
        vertex_layer_gamma,
        vertex_scale_factor,
    )
    weights_b, numer, denom = slice_partial_terms(
        refreshed_vertices,
        focus_scale_factor,
        vertex_content_factor,
        cluster_affinity_factor,
        softness_level,
    )
    numer, denom = psum_slices(numer, denom)
    slice_out = slice_mixing(numer, denom, cluster_probe_lookup, cluster_content_linear)
    attended = attend_rows(weights_b, slice_out)
    projected = jnp.dot(attended, closing_linear_factor, preferred_element_type=jnp.float32)
    return (refreshed_vertices.astype(jnp.float32) + projected).astype(jnp.bfloat16)


def solution(mesh):
    in_specs = (
        P("dom", None),
        P("dom", None),
        P("dom"),
        P("dom"),
        P("dom"),
        P("dom", None, None),
        P(),
        P(),
        P(),
        P(),
        P(),
        P(),
        P(),
        P(),
        P(),
        P(),
        P(),
        P(),
        P(),
        P(),
        P(),
    )
    out_specs = P("dom", None)
    return jax.shard_map(body, mesh=mesh, in_specs=in_specs, out_specs=out_specs, check_vma=False)
```

```python
import functools
import math

import jax
import jax.numpy as jnp
from jax import lax
from jax.experimental import pallas as pl
from jax.experimental.pallas import tpu as pltpu
from jax.sharding import PartitionSpec as P

HEAD_DIM = 16
GROUPS_PER_LANE = 64


def passed_along(value, axis, steps):
    count = lax.axis_size(axis)
    first, last = (max(0, -steps), min(count, count - steps))
    return lax.ppermute(value, axis, [(source, source + steps) for source in range(first, last)])


def _doubling_kernel(steps, x_ref, o_ref, inbox, send_sem, recv_sem):
    me = lax.axis_index("dom")
    partners = []
    for k in range(steps):
        span = 2**k
        bit = (me // span) % 2
        partners.append(me + span - 2 * span * bit)
    barrier = pltpu.get_barrier_semaphore()
    for partner in partners:
        pl.semaphore_signal(
            barrier, 1, device_id={"dom": partner}, device_id_type=pl.DeviceIdType.MESH
        )
    pl.semaphore_wait(barrier, steps)
    for k in range(steps):
        source = x_ref if k == 0 else o_ref
        copy = pltpu.make_async_remote_copy(
            src_ref=source,
            dst_ref=inbox.at[k],
            send_sem=send_sem.at[k],
            recv_sem=recv_sem.at[k],
            device_id={"dom": partners[k]},
            device_id_type=pl.DeviceIdType.MESH,
        )
        copy.start()
        copy.wait()
        o_ref[...] = source[...] + inbox[k]


def dom_sum(flat):
    count = lax.axis_size("dom")
    steps = count.bit_length() - 1
    return pl.pallas_call(
        functools.partial(_doubling_kernel, steps),
        out_shape=jax.ShapeDtypeStruct(flat.shape, flat.dtype),
        in_specs=[pl.BlockSpec(memory_space=pltpu.VMEM)],
        out_specs=pl.BlockSpec(memory_space=pltpu.VMEM),
        scratch_shapes=[
            pltpu.VMEM((steps,) + flat.shape, flat.dtype),
            pltpu.SemaphoreType.DMA((steps,)),
            pltpu.SemaphoreType.DMA((steps,)),
        ],
        compiler_params=pltpu.CompilerParams(collective_id=0, has_side_effects=True),
    )(flat)


def psum_slices(numer, denom):
    joined = jnp.concatenate([numer.reshape(-1), denom.reshape(-1)])
    rows = -(-joined.shape[0] // 1024) * 8
    padded = jnp.zeros((rows * 128,), joined.dtype).at[: joined.shape[0]].set(joined)
    total = dom_sum(padded.reshape(rows, 128)).reshape(-1)
    numer_size = numer.size
    return (
        total[:numer_size].reshape(numer.shape),
        total[numer_size : numer_size + denom.size].reshape(denom.shape),
    )


def layer_norm(values, gain_row):
    row_mean = jnp.mean(values, axis=-1, keepdims=True)
    centred = values - row_mean
    row_var = jnp.mean(centred * centred, axis=-1, keepdims=True)
    return centred * lax.rsqrt(row_var + 1e-05) * gain_row


def node_section(
    own_rows,
    summed_b,
    vertex_layer_alpha,
    vertex_layer_beta,
    vertex_layer_gamma,
    vertex_scale_factor,
):
    feature_width = own_rows.shape[1]
    node_pre = jnp.dot(
        own_rows, vertex_layer_alpha[:feature_width], preferred_element_type=jnp.float32
    )
    node_pre = node_pre + jnp.dot(
        summed_b, vertex_layer_alpha[feature_width:], preferred_element_type=jnp.float32
    )
    node_one = jax.nn.silu(node_pre).astype(jnp.bfloat16)
    node_two = jax.nn.silu(
        jnp.dot(node_one, vertex_layer_beta, preferred_element_type=jnp.float32)
    ).astype(jnp.bfloat16)
    node_three = jnp.dot(node_two, vertex_layer_gamma, preferred_element_type=jnp.float32)
    return (own_rows.astype(jnp.float32) + layer_norm(node_three, vertex_scale_factor)).astype(
        jnp.bfloat16
    )


def slice_partial_terms(
    refreshed_vertices,
    focus_scale_factor,
    vertex_content_factor,
    cluster_affinity_factor,
    softness_level,
):
    count_of_rows = refreshed_vertices.shape[0]
    domain_channel_split = softness_level.shape[0]
    standardised_entries = layer_norm(
        refreshed_vertices.astype(jnp.float32), focus_scale_factor
    ).astype(jnp.bfloat16)
    values = jnp.dot(
        standardised_entries, vertex_content_factor, preferred_element_type=jnp.float32
    ).astype(jnp.bfloat16)
    cluster_affinities = jnp.dot(
        standardised_entries, cluster_affinity_factor, preferred_element_type=jnp.float32
    )
    cluster_affinities = (
        cluster_affinities.reshape(count_of_rows, domain_channel_split, GROUPS_PER_LANE)
        / softness_level[None, :, None]
    )
    weights = jax.nn.softmax(cluster_affinities, axis=-1)
    weights_b = weights.astype(jnp.bfloat16)
    numer = jnp.einsum(
        "nhs,nhc->hsc",
        weights_b,
        values.reshape(count_of_rows, domain_channel_split, HEAD_DIM),
        preferred_element_type=jnp.float32,
    )
    denom = jnp.sum(weights, axis=0)
    return (weights_b, numer, denom)


def slice_mixing(numer, denom, cluster_probe_lookup, cluster_content_linear):
    tokens = numer / denom[:, :, None]
    highest = lax.Precision.HIGHEST
    query = jnp.einsum("hsc,hcd->hsd", tokens, cluster_probe_lookup[0], precision=highest)
    keys = jnp.einsum("hsc,hcd->hsd", tokens, cluster_probe_lookup[1], precision=highest)
    carried = jnp.einsum("hsc,hcd->hsd", tokens, cluster_content_linear, precision=highest)
    scores = jnp.einsum("hsd,htd->hst", query, keys, precision=highest) / math.sqrt(HEAD_DIM)
    mixing = jax.nn.softmax(scores, axis=-1)
    return jnp.einsum("hst,htd->hsd", mixing, carried, precision=highest).astype(jnp.bfloat16)


def attend_rows(weights_b, slice_out):
    count_of_rows = weights_b.shape[0]
    domain_channel_split = weights_b.shape[1]
    attended = jnp.einsum("nhs,hsd->nhd", weights_b, slice_out, preferred_element_type=jnp.float32)
    return attended.reshape(count_of_rows, domain_channel_split * HEAD_DIM).astype(jnp.bfloat16)


def pick_rows(table, row_ids):
    table_ids = jnp.arange(table.shape[0], dtype=jnp.int32)
    selector = (row_ids[:, None] == table_ids[None, :]).astype(jnp.bfloat16)
    return jnp.dot(selector, table, preferred_element_type=jnp.float32).astype(jnp.bfloat16)


def gather_heads(parts, joins):
    flat = jnp.concatenate([part.astype(jnp.float32).reshape(-1) for part in parts])
    other = lax.ppermute(flat, "head", [(0, 1), (1, 0)])
    first = lax.axis_index("head") == 0
    low = jnp.where(first, flat, other)
    high = jnp.where(first, other, flat)
    wholes = []
    start = 0
    for part, axis in zip(parts, joins):
        size = part.size
        pieces = [
            half[start : start + size].reshape(part.shape).astype(part.dtype)
            for half in (low, high)
        ]
        wholes.append(jnp.concatenate(pieces, axis=axis))
        start += size
    return wholes


def body(
    vertex_state,
    link_state_slotted,
    source_vertex_ids,
    target_vertex_ids,
    active_link_tally,
    halo_outgoing_ids,
    link_layer_alpha,
    link_layer_beta,
    link_layer_gamma,
    link_scale_factor,
    vertex_layer_alpha,
    vertex_layer_beta,
    vertex_layer_gamma,
    vertex_scale_factor,
    focus_scale_factor,
    vertex_content_factor,
    cluster_affinity_factor,
    softness_level,
    cluster_probe_lookup,
    cluster_content_linear,
    closing_linear_factor,
):
    (
        vertex_content_factor,
        cluster_affinity_factor,
        softness_level,
        cluster_probe_lookup,
        cluster_content_linear,
        closing_linear_factor,
    ) = gather_heads(
        (
            vertex_content_factor,
            cluster_affinity_factor,
            softness_level,
            cluster_probe_lookup,
            cluster_content_linear,
            closing_linear_factor,
        ),
        (1, 1, 0, 1, 0, 0),
    )
    node_count = vertex_state.shape[0]
    feature_width = vertex_state.shape[1]
    capacity = link_state_slotted.shape[0]
    offsets = (1, -1, 2, -2)
    pieces = [vertex_state]
    for neighbour in range(4):
        outgoing = pick_rows(vertex_state, halo_outgoing_ids[0, neighbour])
        pieces.append(passed_along(outgoing, "dom", offsets[neighbour]))
    extended = jnp.concatenate(pieces, axis=0)
    extended_ids = jnp.arange(extended.shape[0], dtype=jnp.int32)
    node_ids = jnp.arange(node_count, dtype=jnp.int32)
    block_rows = capacity // lax.axis_size("head")
    share = capacity // lax.axis_size("head")
    first_row = lax.axis_index("head") * share
    edge_rows = lax.dynamic_slice_in_dim(link_state_slotted, first_row, share, 0)
    send_rows = lax.dynamic_slice_in_dim(source_vertex_ids, first_row, share, 0)
    recv_rows = lax.dynamic_slice_in_dim(target_vertex_ids, first_row, share, 0)
    turns = edge_rows.shape[0] // block_rows
    edge_blocks = edge_rows.reshape(turns, block_rows, feature_width)
    send_blocks = send_rows.reshape(turns, block_rows)
    recv_blocks = recv_rows.reshape(turns, block_rows)

    def step(total, item):
        edge_part, send_part, recv_part, turn = item
        send_hot = (send_part[:, None] == extended_ids[None, :]).astype(jnp.bfloat16)
        recv_hot = (recv_part[:, None] == node_ids[None, :]).astype(jnp.bfloat16)
        sender_rows = jnp.dot(send_hot, extended, preferred_element_type=jnp.float32).astype(
            jnp.bfloat16
        )
        receiver_rows = jnp.dot(recv_hot, vertex_state, preferred_element_type=jnp.float32).astype(
            jnp.bfloat16
        )
        pre = jnp.dot(
            edge_part, link_layer_alpha[:feature_width], preferred_element_type=jnp.float32
        )
        pre = pre + jnp.dot(
            sender_rows,
            link_layer_alpha[feature_width : 2 * feature_width],
            preferred_element_type=jnp.float32,
        )
        pre = pre + jnp.dot(
            receiver_rows, link_layer_alpha[2 * feature_width :], preferred_element_type=jnp.float32
        )
        first = jax.nn.silu(pre).astype(jnp.bfloat16)
        second = jax.nn.silu(
            jnp.dot(first, link_layer_beta, preferred_element_type=jnp.float32)
        ).astype(jnp.bfloat16)
        third = jnp.dot(second, link_layer_gamma, preferred_element_type=jnp.float32)
        edge_new = (edge_part.astype(jnp.float32) + layer_norm(third, link_scale_factor)).astype(
            jnp.bfloat16
        )
        position = first_row + turn * block_rows + jnp.arange(block_rows, dtype=jnp.int32)
        live = position < active_link_tally[0]
        messages = jnp.where(live[:, None], edge_new, jnp.zeros_like(edge_new))
        gathered = lax.dot_general(
            recv_hot, messages, (((0,), (0,)), ((), ())), preferred_element_type=jnp.float32
        )
        return (total + gathered, None)

    start = jnp.zeros((node_count, feature_width), jnp.float32)
    total, unused = lax.scan(
        step, start, (edge_blocks, send_blocks, recv_blocks, jnp.arange(turns, dtype=jnp.int32))
    )
    summed = lax.psum(total, "head")
    refreshed_vertices = node_section(
        vertex_state,
        summed.astype(jnp.bfloat16),
        vertex_layer_alpha,
        vertex_layer_beta,
        vertex_layer_gamma,
        vertex_scale_factor,
    )
    weights_b, numer, denom = slice_partial_terms(
        refreshed_vertices,
        focus_scale_factor,
        vertex_content_factor,
        cluster_affinity_factor,
        softness_level,
    )
    numer, denom = psum_slices(numer, denom)
    slice_out = slice_mixing(numer, denom, cluster_probe_lookup, cluster_content_linear)
    attended = attend_rows(weights_b, slice_out)
    projected = jnp.dot(attended, closing_linear_factor, preferred_element_type=jnp.float32)
    return (refreshed_vertices.astype(jnp.float32) + projected).astype(jnp.bfloat16)


def solution(mesh):
    in_specs = (
        P("dom", None),
        P("dom", None),
        P("dom"),
        P("dom"),
        P("dom"),
        P("dom", None, None),
        P(),
        P(),
        P(),
        P(),
        P(),
        P(),
        P(),
        P(),
        P(),
        P(None, "head"),
        P(None, "head"),
        P("head"),
        P(None, "head", None, None),
        P("head", None, None),
        P("head", None),
    )
    out_specs = P("dom", None)
    return jax.shard_map(body, mesh=mesh, in_specs=in_specs, out_specs=out_specs, check_vma=False)
```

```python
import functools
import math

import jax
import jax.numpy as jnp
from jax import lax
from jax.experimental import pallas as pl
from jax.experimental.pallas import tpu as pltpu
from jax.sharding import PartitionSpec as P

HEAD_DIM = 16
GROUPS_PER_LANE = 64


def passed_along(value, axis, steps):
    count = lax.axis_size(axis)
    first, last = (max(0, -steps), min(count, count - steps))
    return lax.ppermute(value, axis, [(source, source + steps) for source in range(first, last)])


def _radix_kernel(radix, steps, x_ref, o_ref, inbox, send_sem, recv_sem):
    me = lax.axis_index("dom")
    spans = [radix**s for s in range(steps)]
    digits = [(me // span) % radix for span in spans]
    partners = [
        [me + ((digit + j) % radix - digit) * span for j in range(1, radix)]
        for digit, span in zip(digits, spans)
    ]
    barrier = pltpu.get_barrier_semaphore()
    for group in partners:
        for partner in group:
            pl.semaphore_signal(
                barrier, 1, device_id={"dom": partner}, device_id_type=pl.DeviceIdType.MESH
            )
    pl.semaphore_wait(barrier, steps * (radix - 1))
    for s in range(steps):
        source = x_ref if s == 0 else o_ref
        copies = []
        for j, partner in enumerate(partners[s]):
            copy = pltpu.make_async_remote_copy(
                src_ref=source,
                dst_ref=inbox.at[s, digits[s]],
                send_sem=send_sem.at[s, j],
                recv_sem=recv_sem.at[s, digits[s]],
                device_id={"dom": partner},
                device_id_type=pl.DeviceIdType.MESH,
            )
            copy.start()
            copies.append(copy)
        inbox[s, digits[s]] = source[...]
        for copy in copies:
            copy.wait_send()
        for j, partner in enumerate(partners[s]):
            slot = (digits[s] + j + 1) % radix
            pltpu.make_async_remote_copy(
                src_ref=source,
                dst_ref=inbox.at[s, slot],
                send_sem=send_sem.at[s, j],
                recv_sem=recv_sem.at[s, slot],
                device_id={"dom": partner},
                device_id_type=pl.DeviceIdType.MESH,
            ).wait_recv()
        total = inbox[s, 0]
        for d in range(1, radix):
            total = total + inbox[s, d]
        o_ref[...] = total


def dom_sum(flat):
    count = lax.axis_size("dom")
    radix = 4
    steps = 0
    while radix ** (steps + 1) <= count:
        steps += 1
    assert radix**steps == count
    return pl.pallas_call(
        functools.partial(_radix_kernel, radix, steps),
        out_shape=jax.ShapeDtypeStruct(flat.shape, flat.dtype),
        in_specs=[pl.BlockSpec(memory_space=pltpu.VMEM)],
        out_specs=pl.BlockSpec(memory_space=pltpu.VMEM),
        scratch_shapes=[
            pltpu.VMEM((steps, radix) + flat.shape, flat.dtype),
            pltpu.SemaphoreType.DMA((steps, radix - 1)),
            pltpu.SemaphoreType.DMA((steps, radix)),
        ],
        compiler_params=pltpu.CompilerParams(collective_id=0, has_side_effects=True),
    )(flat)


def psum_slices(numer, denom):
    joined = jnp.concatenate([numer.reshape(-1), denom.reshape(-1)])
    rows = -(-joined.shape[0] // 1024) * 8
    padded = jnp.zeros((rows * 128,), joined.dtype).at[: joined.shape[0]].set(joined)
    total = dom_sum(padded.reshape(rows, 128)).reshape(-1)
    numer_size = numer.size
    return (
        total[:numer_size].reshape(numer.shape),
        total[numer_size : numer_size + denom.size].reshape(denom.shape),
    )


def layer_norm(values, gain_row):
    row_mean = jnp.mean(values, axis=-1, keepdims=True)
    centred = values - row_mean
    row_var = jnp.mean(centred * centred, axis=-1, keepdims=True)
    return centred * lax.rsqrt(row_var + 1e-05) * gain_row


def node_section(
    own_rows,
    summed_b,
    vertex_layer_alpha,
    vertex_layer_beta,
    vertex_layer_gamma,
    vertex_scale_factor,
):
    feature_width = own_rows.shape[1]
    node_pre = jnp.dot(
        own_rows, vertex_layer_alpha[:feature_width], preferred_element_type=jnp.float32
    )
    node_pre = node_pre + jnp.dot(
        summed_b, vertex_layer_alpha[feature_width:], preferred_element_type=jnp.float32
    )
    node_one = jax.nn.silu(node_pre).astype(jnp.bfloat16)
    node_two = jax.nn.silu(
        jnp.dot(node_one, vertex_layer_beta, preferred_element_type=jnp.float32)
    ).astype(jnp.bfloat16)
    node_three = jnp.dot(node_two, vertex_layer_gamma, preferred_element_type=jnp.float32)
    return (own_rows.astype(jnp.float32) + layer_norm(node_three, vertex_scale_factor)).astype(
        jnp.bfloat16
    )


def slice_partial_terms(
    refreshed_vertices,
    focus_scale_factor,
    vertex_content_factor,
    cluster_affinity_factor,
    softness_level,
):
    count_of_rows = refreshed_vertices.shape[0]
    domain_channel_split = softness_level.shape[0]
    standardised_entries = layer_norm(
        refreshed_vertices.astype(jnp.float32), focus_scale_factor
    ).astype(jnp.bfloat16)
    values = jnp.dot(
        standardised_entries, vertex_content_factor, preferred_element_type=jnp.float32
    ).astype(jnp.bfloat16)
    cluster_affinities = jnp.dot(
        standardised_entries, cluster_affinity_factor, preferred_element_type=jnp.float32
    )
    cluster_affinities = (
        cluster_affinities.reshape(count_of_rows, domain_channel_split, GROUPS_PER_LANE)
        / softness_level[None, :, None]
    )
    weights = jax.nn.softmax(cluster_affinities, axis=-1)
    weights_b = weights.astype(jnp.bfloat16)
    numer = jnp.einsum(
        "nhs,nhc->hsc",
        weights_b,
        values.reshape(count_of_rows, domain_channel_split, HEAD_DIM),
        preferred_element_type=jnp.float32,
    )
    denom = jnp.sum(weights, axis=0)
    return (weights_b, numer, denom)


def slice_mixing(numer, denom, cluster_probe_lookup, cluster_content_linear):
    tokens = numer / denom[:, :, None]
    highest = lax.Precision.HIGHEST
    query = jnp.einsum("hsc,hcd->hsd", tokens, cluster_probe_lookup[0], precision=highest)
    keys = jnp.einsum("hsc,hcd->hsd", tokens, cluster_probe_lookup[1], precision=highest)
    carried = jnp.einsum("hsc,hcd->hsd", tokens, cluster_content_linear, precision=highest)
    scores = jnp.einsum("hsd,htd->hst", query, keys, precision=highest) / math.sqrt(HEAD_DIM)
    mixing = jax.nn.softmax(scores, axis=-1)
    return jnp.einsum("hst,htd->hsd", mixing, carried, precision=highest).astype(jnp.bfloat16)


def attend_rows(weights_b, slice_out):
    count_of_rows = weights_b.shape[0]
    domain_channel_split = weights_b.shape[1]
    attended = jnp.einsum("nhs,hsd->nhd", weights_b, slice_out, preferred_element_type=jnp.float32)
    return attended.reshape(count_of_rows, domain_channel_split * HEAD_DIM).astype(jnp.bfloat16)


def pick_rows(table, row_ids):
    table_ids = jnp.arange(table.shape[0], dtype=jnp.int32)
    selector = (row_ids[:, None] == table_ids[None, :]).astype(jnp.bfloat16)
    return jnp.dot(selector, table, preferred_element_type=jnp.float32).astype(jnp.bfloat16)


def body(
    vertex_state,
    link_state_slotted,
    source_vertex_ids,
    target_vertex_ids,
    active_link_tally,
    halo_outgoing_ids,
    link_layer_alpha,
    link_layer_beta,
    link_layer_gamma,
    link_scale_factor,
    vertex_layer_alpha,
    vertex_layer_beta,
    vertex_layer_gamma,
    vertex_scale_factor,
    focus_scale_factor,
    vertex_content_factor,
    cluster_affinity_factor,
    softness_level,
    cluster_probe_lookup,
    cluster_content_linear,
    closing_linear_factor,
):
    node_count = vertex_state.shape[0]
    feature_width = vertex_state.shape[1]
    capacity = link_state_slotted.shape[0]
    offsets = (1, -1, 2, -2)
    pieces = [vertex_state]
    for neighbour in range(4):
        outgoing = pick_rows(vertex_state, halo_outgoing_ids[0, neighbour])
        pieces.append(passed_along(outgoing, "dom", offsets[neighbour]))
    extended = jnp.concatenate(pieces, axis=0)
    extended_ids = jnp.arange(extended.shape[0], dtype=jnp.int32)
    node_ids = jnp.arange(node_count, dtype=jnp.int32)
    block_rows = capacity // lax.axis_size("head")
    share = capacity // lax.axis_size("head")
    first_row = lax.axis_index("head") * share
    edge_rows = lax.dynamic_slice_in_dim(link_state_slotted, first_row, share, 0)
    send_rows = lax.dynamic_slice_in_dim(source_vertex_ids, first_row, share, 0)
    recv_rows = lax.dynamic_slice_in_dim(target_vertex_ids, first_row, share, 0)
    turns = edge_rows.shape[0] // block_rows
    edge_blocks = edge_rows.reshape(turns, block_rows, feature_width)
    send_blocks = send_rows.reshape(turns, block_rows)
    recv_blocks = recv_rows.reshape(turns, block_rows)

    def step(total, item):
        edge_part, send_part, recv_part, turn = item
        send_hot = (send_part[:, None] == extended_ids[None, :]).astype(jnp.bfloat16)
        recv_hot = (recv_part[:, None] == node_ids[None, :]).astype(jnp.bfloat16)
        sender_rows = jnp.dot(send_hot, extended, preferred_element_type=jnp.float32).astype(
            jnp.bfloat16
        )
        receiver_rows = jnp.dot(recv_hot, vertex_state, preferred_element_type=jnp.float32).astype(
            jnp.bfloat16
        )
        pre = jnp.dot(
            edge_part, link_layer_alpha[:feature_width], preferred_element_type=jnp.float32
        )
        pre = pre + jnp.dot(
            sender_rows,
            link_layer_alpha[feature_width : 2 * feature_width],
            preferred_element_type=jnp.float32,
        )
        pre = pre + jnp.dot(
            receiver_rows, link_layer_alpha[2 * feature_width :], preferred_element_type=jnp.float32
        )
        first = jax.nn.silu(pre).astype(jnp.bfloat16)
        second = jax.nn.silu(
            jnp.dot(first, link_layer_beta, preferred_element_type=jnp.float32)
        ).astype(jnp.bfloat16)
        third = jnp.dot(second, link_layer_gamma, preferred_element_type=jnp.float32)
        edge_new = (edge_part.astype(jnp.float32) + layer_norm(third, link_scale_factor)).astype(
            jnp.bfloat16
        )
        position = first_row + turn * block_rows + jnp.arange(block_rows, dtype=jnp.int32)
        live = position < active_link_tally[0]
        messages = jnp.where(live[:, None], edge_new, jnp.zeros_like(edge_new))
        gathered = lax.dot_general(
            recv_hot, messages, (((0,), (0,)), ((), ())), preferred_element_type=jnp.float32
        )
        return (total + gathered, None)

    start = jnp.zeros((node_count, feature_width), jnp.float32)
    total, unused = lax.scan(
        step, start, (edge_blocks, send_blocks, recv_blocks, jnp.arange(turns, dtype=jnp.int32))
    )
    summed = lax.psum(total, "head")
    refreshed_vertices = node_section(
        vertex_state,
        summed.astype(jnp.bfloat16),
        vertex_layer_alpha,
        vertex_layer_beta,
        vertex_layer_gamma,
        vertex_scale_factor,
    )
    weights_b, numer, denom = slice_partial_terms(
        refreshed_vertices,
        focus_scale_factor,
        vertex_content_factor,
        cluster_affinity_factor,
        softness_level,
    )
    numer, denom = psum_slices(numer, denom)
    slice_out = slice_mixing(numer, denom, cluster_probe_lookup, cluster_content_linear)
    attended = attend_rows(weights_b, slice_out)
    projected = jnp.dot(attended, closing_linear_factor, preferred_element_type=jnp.float32)
    return (refreshed_vertices.astype(jnp.float32) + projected).astype(jnp.bfloat16)


def solution(mesh):
    in_specs = (
        P("dom", None),
        P("dom", None),
        P("dom"),
        P("dom"),
        P("dom"),
        P("dom", None, None),
        P(),
        P(),
        P(),
        P(),
        P(),
        P(),
        P(),
        P(),
        P(),
        P(),
        P(),
        P(),
        P(),
        P(),
        P(),
    )
    out_specs = P("dom", None)
    return jax.shard_map(body, mesh=mesh, in_specs=in_specs, out_specs=out_specs, check_vma=False)
```

```python
import functools
import math

import jax
import jax.numpy as jnp
from jax import lax
from jax.experimental import pallas as pl
from jax.experimental.pallas import tpu as pltpu
from jax.sharding import PartitionSpec as P

HEAD_DIM = 16
GROUPS_PER_LANE = 64


def passed_along(value, axis, steps):
    count = lax.axis_size(axis)
    first, last = (max(0, -steps), min(count, count - steps))
    return lax.ppermute(value, axis, [(source, source + steps) for source in range(first, last)])


def _radix_kernel(radix, steps, x_ref, o_ref, inbox, send_sem, recv_sem):
    me = lax.axis_index("dom")
    spans = [radix**s for s in range(steps)]
    digits = [(me // span) % radix for span in spans]
    partners = [
        [me + ((digit + j) % radix - digit) * span for j in range(1, radix)]
        for digit, span in zip(digits, spans)
    ]
    barrier = pltpu.get_barrier_semaphore()
    for group in partners:
        for partner in group:
            pl.semaphore_signal(
                barrier, 1, device_id={"dom": partner}, device_id_type=pl.DeviceIdType.MESH
            )
    pl.semaphore_wait(barrier, steps * (radix - 1))
    for s in range(steps):
        source = x_ref if s == 0 else o_ref
        copies = []
        for j, partner in enumerate(partners[s]):
            copy = pltpu.make_async_remote_copy(
                src_ref=source,
                dst_ref=inbox.at[s, digits[s]],
                send_sem=send_sem.at[s, j],
                recv_sem=recv_sem.at[s, digits[s]],
                device_id={"dom": partner},
                device_id_type=pl.DeviceIdType.MESH,
            )
            copy.start()
            copies.append(copy)
        inbox[s, digits[s]] = source[...]
        for copy in copies:
            copy.wait_send()
        for j, partner in enumerate(partners[s]):
            slot = (digits[s] + j + 1) % radix
            pltpu.make_async_remote_copy(
                src_ref=source,
                dst_ref=inbox.at[s, slot],
                send_sem=send_sem.at[s, j],
                recv_sem=recv_sem.at[s, slot],
                device_id={"dom": partner},
                device_id_type=pl.DeviceIdType.MESH,
            ).wait_recv()
        total = inbox[s, 0]
        for d in range(1, radix):
            total = total + inbox[s, d]
        o_ref[...] = total


def dom_sum(flat):
    count = lax.axis_size("dom")
    radix = 4
    steps = 0
    while radix ** (steps + 1) <= count:
        steps += 1
    assert radix**steps == count
    return pl.pallas_call(
        functools.partial(_radix_kernel, radix, steps),
        out_shape=jax.ShapeDtypeStruct(flat.shape, flat.dtype),
        in_specs=[pl.BlockSpec(memory_space=pltpu.VMEM)],
        out_specs=pl.BlockSpec(memory_space=pltpu.VMEM),
        scratch_shapes=[
            pltpu.VMEM((steps, radix) + flat.shape, flat.dtype),
            pltpu.SemaphoreType.DMA((steps, radix - 1)),
            pltpu.SemaphoreType.DMA((steps, radix)),
        ],
        compiler_params=pltpu.CompilerParams(collective_id=0, has_side_effects=True),
    )(flat)


def _halo_kernel(offsets, own_ref, out_ref, ext_ref, send_sem, recv_sem):
    me = lax.axis_index("dom")
    count = lax.axis_size("dom")
    rows = own_ref.shape[0]
    halo = out_ref.shape[1]
    barrier = pltpu.get_barrier_semaphore()
    for offset in offsets:
        pl.semaphore_signal(
            barrier,
            1,
            device_id={"dom": (me + offset + count) % count},
            device_id_type=pl.DeviceIdType.MESH,
        )
    pl.semaphore_wait(barrier, len(offsets))
    copies = []
    for k, offset in enumerate(offsets):
        copy = pltpu.make_async_remote_copy(
            src_ref=out_ref.at[k],
            dst_ref=ext_ref.at[pl.ds(rows + k * halo, halo)],
            send_sem=send_sem.at[k],
            recv_sem=recv_sem.at[k],
            device_id={"dom": (me + offset + count) % count},
            device_id_type=pl.DeviceIdType.MESH,
        )
        copy.start()
        copies.append(copy)
    ext_ref[pl.ds(0, rows)] = own_ref[...]
    for copy in copies:
        copy.wait()
    for k, offset in enumerate(offsets):
        if offset > 0:
            inside = (me + count - offset) // count
        else:
            inside = (2 * count - 1 + offset - me) // count
        slot = pl.ds(rows + k * halo, halo)
        ext_ref[slot] = ext_ref[slot] * inside.astype(ext_ref.dtype)


def exchange_halos(own_rows, outgoing, offsets):
    rows = own_rows.shape[0]
    total = rows + outgoing.shape[0] * outgoing.shape[1]
    return pl.pallas_call(
        functools.partial(_halo_kernel, offsets),
        out_shape=jax.ShapeDtypeStruct((total, own_rows.shape[1]), own_rows.dtype),
        in_specs=[pl.BlockSpec(memory_space=pltpu.VMEM)] * 2,
        out_specs=pl.BlockSpec(memory_space=pltpu.VMEM),
        scratch_shapes=[
            pltpu.SemaphoreType.DMA((len(offsets),)),
            pltpu.SemaphoreType.DMA((len(offsets),)),
        ],
        compiler_params=pltpu.CompilerParams(collective_id=1, has_side_effects=True),
    )(own_rows, outgoing)


def psum_slices(numer, denom):
    joined = jnp.concatenate([numer.reshape(-1), denom.reshape(-1)])
    rows = -(-joined.shape[0] // 1024) * 8
    padded = jnp.zeros((rows * 128,), joined.dtype).at[: joined.shape[0]].set(joined)
    total = dom_sum(padded.reshape(rows, 128)).reshape(-1)
    numer_size = numer.size
    return (
        total[:numer_size].reshape(numer.shape),
        total[numer_size : numer_size + denom.size].reshape(denom.shape),
    )


def layer_norm(values, gain_row):
    row_mean = jnp.mean(values, axis=-1, keepdims=True)
    centred = values - row_mean
    row_var = jnp.mean(centred * centred, axis=-1, keepdims=True)
    return centred * lax.rsqrt(row_var + 1e-05) * gain_row


def node_section(
    own_rows,
    summed_b,
    vertex_layer_alpha,
    vertex_layer_beta,
    vertex_layer_gamma,
    vertex_scale_factor,
):
    feature_width = own_rows.shape[1]
    node_pre = jnp.dot(
        own_rows, vertex_layer_alpha[:feature_width], preferred_element_type=jnp.float32
    )
    node_pre = node_pre + jnp.dot(
        summed_b, vertex_layer_alpha[feature_width:], preferred_element_type=jnp.float32
    )
    node_one = jax.nn.silu(node_pre).astype(jnp.bfloat16)
    node_two = jax.nn.silu(
        jnp.dot(node_one, vertex_layer_beta, preferred_element_type=jnp.float32)
    ).astype(jnp.bfloat16)
    node_three = jnp.dot(node_two, vertex_layer_gamma, preferred_element_type=jnp.float32)
    return (own_rows.astype(jnp.float32) + layer_norm(node_three, vertex_scale_factor)).astype(
        jnp.bfloat16
    )


def slice_partial_terms(
    refreshed_vertices,
    focus_scale_factor,
    vertex_content_factor,
    cluster_affinity_factor,
    softness_level,
):
    count_of_rows = refreshed_vertices.shape[0]
    domain_channel_split = softness_level.shape[0]
    standardised_entries = layer_norm(
        refreshed_vertices.astype(jnp.float32), focus_scale_factor
    ).astype(jnp.bfloat16)
    values = jnp.dot(
        standardised_entries, vertex_content_factor, preferred_element_type=jnp.float32
    ).astype(jnp.bfloat16)
    cluster_affinities = jnp.dot(
        standardised_entries, cluster_affinity_factor, preferred_element_type=jnp.float32
    )
    cluster_affinities = (
        cluster_affinities.reshape(count_of_rows, domain_channel_split, GROUPS_PER_LANE)
        / softness_level[None, :, None]
    )
    weights = jax.nn.softmax(cluster_affinities, axis=-1)
    weights_b = weights.astype(jnp.bfloat16)
    numer = jnp.einsum(
        "nhs,nhc->hsc",
        weights_b,
        values.reshape(count_of_rows, domain_channel_split, HEAD_DIM),
        preferred_element_type=jnp.float32,
    )
    denom = jnp.sum(weights, axis=0)
    return (weights_b, numer, denom)


def slice_mixing(numer, denom, cluster_probe_lookup, cluster_content_linear):
    tokens = numer / denom[:, :, None]
    highest = lax.Precision.HIGHEST
    query = jnp.einsum("hsc,hcd->hsd", tokens, cluster_probe_lookup[0], precision=highest)
    keys = jnp.einsum("hsc,hcd->hsd", tokens, cluster_probe_lookup[1], precision=highest)
    carried = jnp.einsum("hsc,hcd->hsd", tokens, cluster_content_linear, precision=highest)
    scores = jnp.einsum("hsd,htd->hst", query, keys, precision=highest) / math.sqrt(HEAD_DIM)
    mixing = jax.nn.softmax(scores, axis=-1)
    return jnp.einsum("hst,htd->hsd", mixing, carried, precision=highest).astype(jnp.bfloat16)


def attend_rows(weights_b, slice_out):
    count_of_rows = weights_b.shape[0]
    domain_channel_split = weights_b.shape[1]
    attended = jnp.einsum("nhs,hsd->nhd", weights_b, slice_out, preferred_element_type=jnp.float32)
    return attended.reshape(count_of_rows, domain_channel_split * HEAD_DIM).astype(jnp.bfloat16)


def pick_rows(table, row_ids):
    table_ids = jnp.arange(table.shape[0], dtype=jnp.int32)
    selector = (row_ids[:, None] == table_ids[None, :]).astype(jnp.bfloat16)
    return jnp.dot(selector, table, preferred_element_type=jnp.float32).astype(jnp.bfloat16)


def body(
    vertex_state,
    link_state_slotted,
    source_vertex_ids,
    target_vertex_ids,
    active_link_tally,
    halo_outgoing_ids,
    link_layer_alpha,
    link_layer_beta,
    link_layer_gamma,
    link_scale_factor,
    vertex_layer_alpha,
    vertex_layer_beta,
    vertex_layer_gamma,
    vertex_scale_factor,
    focus_scale_factor,
    vertex_content_factor,
    cluster_affinity_factor,
    softness_level,
    cluster_probe_lookup,
    cluster_content_linear,
    closing_linear_factor,
):
    node_count = vertex_state.shape[0]
    feature_width = vertex_state.shape[1]
    capacity = link_state_slotted.shape[0]
    offsets = (1, -1, 2, -2)
    outgoing = pick_rows(vertex_state, halo_outgoing_ids[0].reshape(-1))
    extended = exchange_halos(
        vertex_state, outgoing.reshape(halo_outgoing_ids.shape[1:] + (feature_width,)), offsets
    )
    extended_ids = jnp.arange(extended.shape[0], dtype=jnp.int32)
    node_ids = jnp.arange(node_count, dtype=jnp.int32)
    block_rows = capacity // lax.axis_size("head")
    share = capacity // lax.axis_size("head")
    first_row = lax.axis_index("head") * share
    edge_rows = lax.dynamic_slice_in_dim(link_state_slotted, first_row, share, 0)
    send_rows = lax.dynamic_slice_in_dim(source_vertex_ids, first_row, share, 0)
    recv_rows = lax.dynamic_slice_in_dim(target_vertex_ids, first_row, share, 0)
    turns = edge_rows.shape[0] // block_rows
    edge_blocks = edge_rows.reshape(turns, block_rows, feature_width)
    send_blocks = send_rows.reshape(turns, block_rows)
    recv_blocks = recv_rows.reshape(turns, block_rows)

    def step(total, item):
        edge_part, send_part, recv_part, turn = item
        send_hot = (send_part[:, None] == extended_ids[None, :]).astype(jnp.bfloat16)
        recv_hot = (recv_part[:, None] == node_ids[None, :]).astype(jnp.bfloat16)
        sender_rows = jnp.dot(send_hot, extended, preferred_element_type=jnp.float32).astype(
            jnp.bfloat16
        )
        receiver_rows = jnp.dot(recv_hot, vertex_state, preferred_element_type=jnp.float32).astype(
            jnp.bfloat16
        )
        pre = jnp.dot(
            edge_part, link_layer_alpha[:feature_width], preferred_element_type=jnp.float32
        )
        pre = pre + jnp.dot(
            sender_rows,
            link_layer_alpha[feature_width : 2 * feature_width],
            preferred_element_type=jnp.float32,
        )
        pre = pre + jnp.dot(
            receiver_rows, link_layer_alpha[2 * feature_width :], preferred_element_type=jnp.float32
        )
        first = jax.nn.silu(pre).astype(jnp.bfloat16)
        second = jax.nn.silu(
            jnp.dot(first, link_layer_beta, preferred_element_type=jnp.float32)
        ).astype(jnp.bfloat16)
        third = jnp.dot(second, link_layer_gamma, preferred_element_type=jnp.float32)
        edge_new = (edge_part.astype(jnp.float32) + layer_norm(third, link_scale_factor)).astype(
            jnp.bfloat16
        )
        position = first_row + turn * block_rows + jnp.arange(block_rows, dtype=jnp.int32)
        live = position < active_link_tally[0]
        messages = jnp.where(live[:, None], edge_new, jnp.zeros_like(edge_new))
        gathered = lax.dot_general(
            recv_hot, messages, (((0,), (0,)), ((), ())), preferred_element_type=jnp.float32
        )
        return (total + gathered, None)

    start = jnp.zeros((node_count, feature_width), jnp.float32)
    total, unused = lax.scan(
        step, start, (edge_blocks, send_blocks, recv_blocks, jnp.arange(turns, dtype=jnp.int32))
    )
    summed = lax.psum(total, "head")
    refreshed_vertices = node_section(
        vertex_state,
        summed.astype(jnp.bfloat16),
        vertex_layer_alpha,
        vertex_layer_beta,
        vertex_layer_gamma,
        vertex_scale_factor,
    )
    weights_b, numer, denom = slice_partial_terms(
        refreshed_vertices,
        focus_scale_factor,
        vertex_content_factor,
        cluster_affinity_factor,
        softness_level,
    )
    numer, denom = psum_slices(numer, denom)
    slice_out = slice_mixing(numer, denom, cluster_probe_lookup, cluster_content_linear)
    attended = attend_rows(weights_b, slice_out)
    projected = jnp.dot(attended, closing_linear_factor, preferred_element_type=jnp.float32)
    return (refreshed_vertices.astype(jnp.float32) + projected).astype(jnp.bfloat16)


def solution(mesh):
    in_specs = (
        P("dom", None),
        P("dom", None),
        P("dom"),
        P("dom"),
        P("dom"),
        P("dom", None, None),
        P(),
        P(),
        P(),
        P(),
        P(),
        P(),
        P(),
        P(),
        P(),
        P(),
        P(),
        P(),
        P(),
        P(),
        P(),
    )
    out_specs = P("dom", None)
    return jax.shard_map(body, mesh=mesh, in_specs=in_specs, out_specs=out_specs, check_vma=False)
```

```python
import functools
import math

import jax
import jax.numpy as jnp
from jax import lax
from jax.experimental import pallas as pl
from jax.experimental.pallas import tpu as pltpu
from jax.sharding import PartitionSpec as P

HEAD_DIM = 16
GROUPS_PER_LANE = 64
FOLD = 4


def passed_along(value, axis, steps):
    count = lax.axis_size(axis)
    first, last = (max(0, -steps), min(count, count - steps))
    return lax.ppermute(value, axis, [(source, source + steps) for source in range(first, last)])


def _radix_kernel(radix, steps, x_ref, o_ref, inbox, send_sem, recv_sem):
    me = lax.axis_index("dom")
    spans = [radix**s for s in range(steps)]
    digits = [(me // span) % radix for span in spans]
    partners = [
        [me + ((digit + j) % radix - digit) * span for j in range(1, radix)]
        for digit, span in zip(digits, spans)
    ]
    barrier = pltpu.get_barrier_semaphore()
    for group in partners:
        for partner in group:
            pl.semaphore_signal(
                barrier, 1, device_id={"dom": partner}, device_id_type=pl.DeviceIdType.MESH
            )
    pl.semaphore_wait(barrier, steps * (radix - 1))
    for s in range(steps):
        source = x_ref if s == 0 else o_ref
        copies = []
        for j, partner in enumerate(partners[s]):
            copy = pltpu.make_async_remote_copy(
                src_ref=source,
                dst_ref=inbox.at[s, digits[s]],
                send_sem=send_sem.at[s, j],
                recv_sem=recv_sem.at[s, digits[s]],
                device_id={"dom": partner},
                device_id_type=pl.DeviceIdType.MESH,
            )
            copy.start()
            copies.append(copy)
        inbox[s, digits[s]] = source[...]
        for copy in copies:
            copy.wait_send()
        for j, partner in enumerate(partners[s]):
            slot = (digits[s] + j + 1) % radix
            pltpu.make_async_remote_copy(
                src_ref=source,
                dst_ref=inbox.at[s, slot],
                send_sem=send_sem.at[s, j],
                recv_sem=recv_sem.at[s, slot],
                device_id={"dom": partner},
                device_id_type=pl.DeviceIdType.MESH,
            ).wait_recv()
        total = inbox[s, 0]
        for d in range(1, radix):
            total = total + inbox[s, d]
        o_ref[...] = total


def dom_sum(flat):
    count = lax.axis_size("dom")
    radix = 4
    steps = 0
    while radix ** (steps + 1) <= count:
        steps += 1
    assert radix**steps == count
    return pl.pallas_call(
        functools.partial(_radix_kernel, radix, steps),
        out_shape=jax.ShapeDtypeStruct(flat.shape, flat.dtype),
        in_specs=[pl.BlockSpec(memory_space=pltpu.VMEM)],
        out_specs=pl.BlockSpec(memory_space=pltpu.VMEM),
        scratch_shapes=[
            pltpu.VMEM((steps, radix) + flat.shape, flat.dtype),
            pltpu.SemaphoreType.DMA((steps, radix - 1)),
            pltpu.SemaphoreType.DMA((steps, radix)),
        ],
        compiler_params=pltpu.CompilerParams(collective_id=0, has_side_effects=True),
    )(flat)


def _halo_kernel(offsets, own_ref, out_ref, ext_ref, send_sem, recv_sem):
    me = lax.axis_index("dom")
    count = lax.axis_size("dom")
    rows = own_ref.shape[0]
    halo = out_ref.shape[1]
    barrier = pltpu.get_barrier_semaphore()
    for offset in offsets:
        pl.semaphore_signal(
            barrier,
            1,
            device_id={"dom": (me + offset + count) % count},
            device_id_type=pl.DeviceIdType.MESH,
        )
    pl.semaphore_wait(barrier, len(offsets))
    copies = []
    for k, offset in enumerate(offsets):
        copy = pltpu.make_async_remote_copy(
            src_ref=out_ref.at[k],
            dst_ref=ext_ref.at[pl.ds(rows + k * halo, halo)],
            send_sem=send_sem.at[k],
            recv_sem=recv_sem.at[k],
            device_id={"dom": (me + offset + count) % count},
            device_id_type=pl.DeviceIdType.MESH,
        )
        copy.start()
        copies.append(copy)
    ext_ref[pl.ds(0, rows)] = own_ref[...]
    for copy in copies:
        copy.wait()
    for k, offset in enumerate(offsets):
        if offset > 0:
            inside = (me + count - offset) // count
        else:
            inside = (2 * count - 1 + offset - me) // count
        slot = pl.ds(rows + k * halo, halo)
        ext_ref[slot] = ext_ref[slot] * inside.astype(ext_ref.dtype)


def exchange_halos(own_rows, outgoing, offsets):
    rows = own_rows.shape[0]
    total = rows + outgoing.shape[0] * outgoing.shape[1]
    return pl.pallas_call(
        functools.partial(_halo_kernel, offsets),
        out_shape=jax.ShapeDtypeStruct((total, own_rows.shape[1]), own_rows.dtype),
        in_specs=[pl.BlockSpec(memory_space=pltpu.VMEM)] * 2,
        out_specs=pl.BlockSpec(memory_space=pltpu.VMEM),
        scratch_shapes=[
            pltpu.SemaphoreType.DMA((len(offsets),)),
            pltpu.SemaphoreType.DMA((len(offsets),)),
        ],
        compiler_params=pltpu.CompilerParams(collective_id=1, has_side_effects=True),
    )(own_rows, outgoing)


def psum_slices(numer, denom):
    joined = jnp.concatenate([numer.reshape(-1), denom.reshape(-1)])
    rows = -(-joined.shape[0] // 1024) * 8
    padded = jnp.zeros((rows * 128,), joined.dtype).at[: joined.shape[0]].set(joined)
    total = dom_sum(padded.reshape(rows, 128)).reshape(-1)
    numer_size = numer.size
    return (
        total[:numer_size].reshape(numer.shape),
        total[numer_size : numer_size + denom.size].reshape(denom.shape),
    )


def layer_norm(values, gain_row):
    row_mean = jnp.mean(values, axis=-1, keepdims=True)
    centred = values - row_mean
    row_var = jnp.mean(centred * centred, axis=-1, keepdims=True)
    return centred * lax.rsqrt(row_var + 1e-05) * gain_row


def node_section(
    own_rows,
    summed_b,
    vertex_layer_alpha,
    vertex_layer_beta,
    vertex_layer_gamma,
    vertex_scale_factor,
):
    feature_width = own_rows.shape[1]
    node_pre = jnp.dot(
        own_rows, vertex_layer_alpha[:feature_width], preferred_element_type=jnp.float32
    )
    node_pre = node_pre + jnp.dot(
        summed_b, vertex_layer_alpha[feature_width:], preferred_element_type=jnp.float32
    )
    node_one = jax.nn.silu(node_pre).astype(jnp.bfloat16)
    node_two = jax.nn.silu(
        jnp.dot(node_one, vertex_layer_beta, preferred_element_type=jnp.float32)
    ).astype(jnp.bfloat16)
    node_three = jnp.dot(node_two, vertex_layer_gamma, preferred_element_type=jnp.float32)
    return (own_rows.astype(jnp.float32) + layer_norm(node_three, vertex_scale_factor)).astype(
        jnp.bfloat16
    )


def slice_partial_terms(
    refreshed_vertices,
    focus_scale_factor,
    vertex_content_factor,
    cluster_affinity_factor,
    softness_level,
):
    count_of_rows = refreshed_vertices.shape[0]
    domain_channel_split = softness_level.shape[0]
    standardised_entries = layer_norm(
        refreshed_vertices.astype(jnp.float32), focus_scale_factor
    ).astype(jnp.bfloat16)
    values = jnp.dot(
        standardised_entries, vertex_content_factor, preferred_element_type=jnp.float32
    ).astype(jnp.bfloat16)
    cluster_affinities = jnp.dot(
        standardised_entries, cluster_affinity_factor, preferred_element_type=jnp.float32
    )
    cluster_affinities = (
        cluster_affinities.reshape(count_of_rows, domain_channel_split, GROUPS_PER_LANE)
        / softness_level[None, :, None]
    )
    weights = jax.nn.softmax(cluster_affinities, axis=-1)
    weights_b = weights.astype(jnp.bfloat16)
    numer = jnp.einsum(
        "nhs,nhc->hsc",
        weights_b,
        values.reshape(count_of_rows, domain_channel_split, HEAD_DIM),
        preferred_element_type=jnp.float32,
    )
    denom = jnp.sum(weights, axis=0)
    return (weights_b, numer, denom)


def slice_mixing(numer, denom, cluster_probe_lookup, cluster_content_linear):
    tokens = numer / denom[:, :, None]
    highest = lax.Precision.HIGHEST
    query = jnp.einsum("hsc,hcd->hsd", tokens, cluster_probe_lookup[0], precision=highest)
    keys = jnp.einsum("hsc,hcd->hsd", tokens, cluster_probe_lookup[1], precision=highest)
    carried = jnp.einsum("hsc,hcd->hsd", tokens, cluster_content_linear, precision=highest)
    scores = jnp.einsum("hsd,htd->hst", query, keys, precision=highest) / math.sqrt(HEAD_DIM)
    mixing = jax.nn.softmax(scores, axis=-1)
    return jnp.einsum("hst,htd->hsd", mixing, carried, precision=highest).astype(jnp.bfloat16)


def attend_rows(weights_b, slice_out):
    count_of_rows = weights_b.shape[0]
    domain_channel_split = weights_b.shape[1]
    attended = jnp.einsum("nhs,hsd->nhd", weights_b, slice_out, preferred_element_type=jnp.float32)
    return attended.reshape(count_of_rows, domain_channel_split * HEAD_DIM).astype(jnp.bfloat16)


def pick_rows(table, row_ids):
    table_ids = jnp.arange(table.shape[0], dtype=jnp.int32)
    selector = (row_ids[:, None] == table_ids[None, :]).astype(jnp.bfloat16)
    return jnp.dot(selector, table, preferred_element_type=jnp.float32).astype(jnp.bfloat16)


def gather_rows(table, row_ids, fold):
    count, width = table.shape
    wide = table.reshape(count // fold, fold * width)
    hot = (row_ids[:, None] // fold == jnp.arange(count // fold, dtype=jnp.int32)[None, :]).astype(
        jnp.bfloat16
    )
    picked = jnp.dot(hot, wide, preferred_element_type=jnp.float32)
    lane = row_ids % fold
    rows = picked[:, :width]
    for j in range(1, fold):
        rows = jnp.where((lane == j)[:, None], picked[:, j * width : (j + 1) * width], rows)
    return rows.astype(jnp.bfloat16)


def scatter_rows(messages, row_ids, count, fold):
    width = messages.shape[1]
    lane = row_ids % fold
    spread = jnp.concatenate(
        [jnp.where((lane == j)[:, None], messages, jnp.zeros_like(messages)) for j in range(fold)],
        axis=1,
    )
    hot = (row_ids[:, None] // fold == jnp.arange(count // fold, dtype=jnp.int32)[None, :]).astype(
        jnp.bfloat16
    )
    total = lax.dot_general(
        hot, spread, (((0,), (0,)), ((), ())), preferred_element_type=jnp.float32
    )
    return total.reshape(count, width)


def body(
    vertex_state,
    link_state_slotted,
    source_vertex_ids,
    target_vertex_ids,
    active_link_tally,
    halo_outgoing_ids,
    link_layer_alpha,
    link_layer_beta,
    link_layer_gamma,
    link_scale_factor,
    vertex_layer_alpha,
    vertex_layer_beta,
    vertex_layer_gamma,
    vertex_scale_factor,
    focus_scale_factor,
    vertex_content_factor,
    cluster_affinity_factor,
    softness_level,
    cluster_probe_lookup,
    cluster_content_linear,
    closing_linear_factor,
):
    node_count = vertex_state.shape[0]
    feature_width = vertex_state.shape[1]
    capacity = link_state_slotted.shape[0]
    offsets = (1, -1, 2, -2)
    outgoing = pick_rows(vertex_state, halo_outgoing_ids[0].reshape(-1))
    extended = exchange_halos(
        vertex_state, outgoing.reshape(halo_outgoing_ids.shape[1:] + (feature_width,)), offsets
    )
    extended_ids = jnp.arange(extended.shape[0], dtype=jnp.int32)
    node_ids = jnp.arange(node_count, dtype=jnp.int32)
    block_rows = capacity // lax.axis_size("head")
    share = capacity // lax.axis_size("head")
    first_row = lax.axis_index("head") * share
    edge_rows = lax.dynamic_slice_in_dim(link_state_slotted, first_row, share, 0)
    send_rows = lax.dynamic_slice_in_dim(source_vertex_ids, first_row, share, 0)
    recv_rows = lax.dynamic_slice_in_dim(target_vertex_ids, first_row, share, 0)
    turns = edge_rows.shape[0] // block_rows
    edge_blocks = edge_rows.reshape(turns, block_rows, feature_width)
    send_blocks = send_rows.reshape(turns, block_rows)
    recv_blocks = recv_rows.reshape(turns, block_rows)

    def step(total, item):
        edge_part, send_part, recv_part, turn = item
        sender_rows = gather_rows(extended, send_part, FOLD)
        receiver_rows = gather_rows(vertex_state, recv_part, FOLD)
        pre = jnp.dot(
            edge_part, link_layer_alpha[:feature_width], preferred_element_type=jnp.float32
        )
        pre = pre + jnp.dot(
            sender_rows,
            link_layer_alpha[feature_width : 2 * feature_width],
            preferred_element_type=jnp.float32,
        )
        pre = pre + jnp.dot(
            receiver_rows, link_layer_alpha[2 * feature_width :], preferred_element_type=jnp.float32
        )
        first = jax.nn.silu(pre).astype(jnp.bfloat16)
        second = jax.nn.silu(
            jnp.dot(first, link_layer_beta, preferred_element_type=jnp.float32)
        ).astype(jnp.bfloat16)
        third = jnp.dot(second, link_layer_gamma, preferred_element_type=jnp.float32)
        edge_new = (edge_part.astype(jnp.float32) + layer_norm(third, link_scale_factor)).astype(
            jnp.bfloat16
        )
        position = first_row + turn * block_rows + jnp.arange(block_rows, dtype=jnp.int32)
        live = position < active_link_tally[0]
        messages = jnp.where(live[:, None], edge_new, jnp.zeros_like(edge_new))
        gathered = scatter_rows(messages, recv_part, node_count, FOLD)
        return (total + gathered, None)

    start = jnp.zeros((node_count, feature_width), jnp.float32)
    total, unused = lax.scan(
        step, start, (edge_blocks, send_blocks, recv_blocks, jnp.arange(turns, dtype=jnp.int32))
    )
    summed = lax.psum(total, "head")
    refreshed_vertices = node_section(
        vertex_state,
        summed.astype(jnp.bfloat16),
        vertex_layer_alpha,
        vertex_layer_beta,
        vertex_layer_gamma,
        vertex_scale_factor,
    )
    weights_b, numer, denom = slice_partial_terms(
        refreshed_vertices,
        focus_scale_factor,
        vertex_content_factor,
        cluster_affinity_factor,
        softness_level,
    )
    numer, denom = psum_slices(numer, denom)
    slice_out = slice_mixing(numer, denom, cluster_probe_lookup, cluster_content_linear)
    attended = attend_rows(weights_b, slice_out)
    projected = jnp.dot(attended, closing_linear_factor, preferred_element_type=jnp.float32)
    return (refreshed_vertices.astype(jnp.float32) + projected).astype(jnp.bfloat16)


def solution(mesh):
    in_specs = (
        P("dom", None),
        P("dom", None),
        P("dom"),
        P("dom"),
        P("dom"),
        P("dom", None, None),
        P(),
        P(),
        P(),
        P(),
        P(),
        P(),
        P(),
        P(),
        P(),
        P(),
        P(),
        P(),
        P(),
        P(),
        P(),
    )
    out_specs = P("dom", None)
    return jax.shard_map(body, mesh=mesh, in_specs=in_specs, out_specs=out_specs, check_vma=False)
```

```python
import functools
import math

import jax
import jax.numpy as jnp
from jax import lax
from jax.experimental import pallas as pl
from jax.experimental.pallas import tpu as pltpu
from jax.sharding import PartitionSpec as P

HEAD_DIM = 16
GROUPS_PER_LANE = 64
FOLD = 4


def passed_along(value, axis, steps):
    count = lax.axis_size(axis)
    first, last = (max(0, -steps), min(count, count - steps))
    return lax.ppermute(value, axis, [(source, source + steps) for source in range(first, last)])


def _radix_kernel(radix, steps, x_ref, o_ref, inbox, send_sem, recv_sem):
    me = lax.axis_index("dom")
    spans = [radix**s for s in range(steps)]
    digits = [(me // span) % radix for span in spans]
    partners = [
        [me + ((digit + j) % radix - digit) * span for j in range(1, radix)]
        for digit, span in zip(digits, spans)
    ]
    barrier = pltpu.get_barrier_semaphore()
    for group in partners:
        for partner in group:
            pl.semaphore_signal(
                barrier, 1, device_id={"dom": partner}, device_id_type=pl.DeviceIdType.MESH
            )
    pl.semaphore_wait(barrier, steps * (radix - 1))
    for s in range(steps):
        source = x_ref if s == 0 else o_ref
        copies = []
        for j, partner in enumerate(partners[s]):
            copy = pltpu.make_async_remote_copy(
                src_ref=source,
                dst_ref=inbox.at[s, digits[s]],
                send_sem=send_sem.at[s, j],
                recv_sem=recv_sem.at[s, digits[s]],
                device_id={"dom": partner},
                device_id_type=pl.DeviceIdType.MESH,
            )
            copy.start()
            copies.append(copy)
        inbox[s, digits[s]] = source[...]
        for copy in copies:
            copy.wait_send()
        for j, partner in enumerate(partners[s]):
            slot = (digits[s] + j + 1) % radix
            pltpu.make_async_remote_copy(
                src_ref=source,
                dst_ref=inbox.at[s, slot],
                send_sem=send_sem.at[s, j],
                recv_sem=recv_sem.at[s, slot],
                device_id={"dom": partner},
                device_id_type=pl.DeviceIdType.MESH,
            ).wait_recv()
        total = inbox[s, 0]
        for d in range(1, radix):
            total = total + inbox[s, d]
        o_ref[...] = total


def dom_sum(flat):
    count = lax.axis_size("dom")
    radix = 4
    steps = 0
    while radix ** (steps + 1) <= count:
        steps += 1
    assert radix**steps == count
    return pl.pallas_call(
        functools.partial(_radix_kernel, radix, steps),
        out_shape=jax.ShapeDtypeStruct(flat.shape, flat.dtype),
        in_specs=[pl.BlockSpec(memory_space=pltpu.VMEM)],
        out_specs=pl.BlockSpec(memory_space=pltpu.VMEM),
        scratch_shapes=[
            pltpu.VMEM((steps, radix) + flat.shape, flat.dtype),
            pltpu.SemaphoreType.DMA((steps, radix - 1)),
            pltpu.SemaphoreType.DMA((steps, radix)),
        ],
        compiler_params=pltpu.CompilerParams(collective_id=0, has_side_effects=True),
    )(flat)


def _halo_kernel(offsets, own_ref, out_ref, ext_ref, send_sem, recv_sem, pass_sem, land_sem):
    me = lax.axis_index("dom")
    count = lax.axis_size("dom")
    core = lax.axis_index("head")
    sibling = 1 - core
    rows = own_ref.shape[0]
    halo = out_ref.shape[1]
    half = halo // 2
    mesh_ids = pl.DeviceIdType.MESH
    barrier = pltpu.get_barrier_semaphore()
    for offset in offsets:
        pl.semaphore_signal(
            barrier, 1, device_id={"dom": (me + offset + count) % count}, device_id_type=mesh_ids
        )
    pl.semaphore_signal(barrier, 1, device_id={"head": sibling}, device_id_type=mesh_ids)
    pl.semaphore_wait(barrier, len(offsets) + 1)
    sends = []
    for k, offset in enumerate(offsets):
        copy = pltpu.make_async_remote_copy(
            src_ref=out_ref.at[k, pl.ds(core * half, half)],
            dst_ref=ext_ref.at[pl.ds(rows + k * halo + core * half, half)],
            send_sem=send_sem.at[k],
            recv_sem=recv_sem.at[k],
            device_id={"dom": (me + offset + count) % count},
            device_id_type=mesh_ids,
        )
        copy.start()
        sends.append(copy)
    ext_ref[pl.ds(0, rows)] = own_ref[...]
    passes = []
    for k in range(len(offsets)):
        sends[k].wait_recv()
        forward = pltpu.make_async_remote_copy(
            src_ref=ext_ref.at[pl.ds(rows + k * halo + core * half, half)],
            dst_ref=ext_ref.at[pl.ds(rows + k * halo + core * half, half)],
            send_sem=pass_sem.at[k],
            recv_sem=land_sem.at[k],
            device_id={"head": sibling},
            device_id_type=mesh_ids,
        )
        forward.start()
        passes.append(forward)
    for copy in sends:
        copy.wait_send()
    for forward in passes:
        forward.wait()
    for k, offset in enumerate(offsets):
        if offset > 0:
            inside = (me + count - offset) // count
        else:
            inside = (2 * count - 1 + offset - me) // count
        slot = pl.ds(rows + k * halo, halo)
        ext_ref[slot] = ext_ref[slot] * inside.astype(ext_ref.dtype)


def exchange_halos(own_rows, outgoing, offsets):
    rows = own_rows.shape[0]
    total = rows + outgoing.shape[0] * outgoing.shape[1]
    return pl.pallas_call(
        functools.partial(_halo_kernel, offsets),
        out_shape=jax.ShapeDtypeStruct((total, own_rows.shape[1]), own_rows.dtype),
        in_specs=[pl.BlockSpec(memory_space=pltpu.VMEM)] * 2,
        out_specs=pl.BlockSpec(memory_space=pltpu.VMEM),
        scratch_shapes=[pltpu.SemaphoreType.DMA((len(offsets),))] * 4,
        compiler_params=pltpu.CompilerParams(collective_id=1, has_side_effects=True),
    )(own_rows, outgoing)


def psum_slices(numer, denom):
    joined = jnp.concatenate([numer.reshape(-1), denom.reshape(-1)])
    rows = -(-joined.shape[0] // 1024) * 8
    padded = jnp.zeros((rows * 128,), joined.dtype).at[: joined.shape[0]].set(joined)
    total = dom_sum(padded.reshape(rows, 128)).reshape(-1)
    numer_size = numer.size
    return (
        total[:numer_size].reshape(numer.shape),
        total[numer_size : numer_size + denom.size].reshape(denom.shape),
    )


def layer_norm(values, gain_row):
    row_mean = jnp.mean(values, axis=-1, keepdims=True)
    centred = values - row_mean
    row_var = jnp.mean(centred * centred, axis=-1, keepdims=True)
    return centred * lax.rsqrt(row_var + 1e-05) * gain_row


def node_section(
    own_rows,
    summed_b,
    vertex_layer_alpha,
    vertex_layer_beta,
    vertex_layer_gamma,
    vertex_scale_factor,
):
    feature_width = own_rows.shape[1]
    node_pre = jnp.dot(
        own_rows, vertex_layer_alpha[:feature_width], preferred_element_type=jnp.float32
    )
    node_pre = node_pre + jnp.dot(
        summed_b, vertex_layer_alpha[feature_width:], preferred_element_type=jnp.float32
    )
    node_one = jax.nn.silu(node_pre).astype(jnp.bfloat16)
    node_two = jax.nn.silu(
        jnp.dot(node_one, vertex_layer_beta, preferred_element_type=jnp.float32)
    ).astype(jnp.bfloat16)
    node_three = jnp.dot(node_two, vertex_layer_gamma, preferred_element_type=jnp.float32)
    return (own_rows.astype(jnp.float32) + layer_norm(node_three, vertex_scale_factor)).astype(
        jnp.bfloat16
    )


def slice_partial_terms(
    refreshed_vertices,
    focus_scale_factor,
    vertex_content_factor,
    cluster_affinity_factor,
    softness_level,
):
    count_of_rows = refreshed_vertices.shape[0]
    domain_channel_split = softness_level.shape[0]
    standardised_entries = layer_norm(
        refreshed_vertices.astype(jnp.float32), focus_scale_factor
    ).astype(jnp.bfloat16)
    values = jnp.dot(
        standardised_entries, vertex_content_factor, preferred_element_type=jnp.float32
    ).astype(jnp.bfloat16)
    cluster_affinities = jnp.dot(
        standardised_entries, cluster_affinity_factor, preferred_element_type=jnp.float32
    )
    cluster_affinities = (
        cluster_affinities.reshape(count_of_rows, domain_channel_split, GROUPS_PER_LANE)
        / softness_level[None, :, None]
    )
    weights = jax.nn.softmax(cluster_affinities, axis=-1)
    weights_b = weights.astype(jnp.bfloat16)
    numer = jnp.einsum(
        "nhs,nhc->hsc",
        weights_b,
        values.reshape(count_of_rows, domain_channel_split, HEAD_DIM),
        preferred_element_type=jnp.float32,
    )
    denom = jnp.sum(weights, axis=0)
    return (weights_b, numer, denom)


def slice_mixing(numer, denom, cluster_probe_lookup, cluster_content_linear):
    tokens = numer / denom[:, :, None]
    highest = lax.Precision.HIGHEST
    query = jnp.einsum("hsc,hcd->hsd", tokens, cluster_probe_lookup[0], precision=highest)
    keys = jnp.einsum("hsc,hcd->hsd", tokens, cluster_probe_lookup[1], precision=highest)
    carried = jnp.einsum("hsc,hcd->hsd", tokens, cluster_content_linear, precision=highest)
    scores = jnp.einsum("hsd,htd->hst", query, keys, precision=highest) / math.sqrt(HEAD_DIM)
    mixing = jax.nn.softmax(scores, axis=-1)
    return jnp.einsum("hst,htd->hsd", mixing, carried, precision=highest).astype(jnp.bfloat16)


def attend_rows(weights_b, slice_out):
    count_of_rows = weights_b.shape[0]
    domain_channel_split = weights_b.shape[1]
    attended = jnp.einsum("nhs,hsd->nhd", weights_b, slice_out, preferred_element_type=jnp.float32)
    return attended.reshape(count_of_rows, domain_channel_split * HEAD_DIM).astype(jnp.bfloat16)


def pick_rows(table, row_ids):
    table_ids = jnp.arange(table.shape[0], dtype=jnp.int32)
    selector = (row_ids[:, None] == table_ids[None, :]).astype(jnp.bfloat16)
    return jnp.dot(selector, table, preferred_element_type=jnp.float32).astype(jnp.bfloat16)


def gather_rows(table, row_ids, fold):
    count, width = table.shape
    wide = table.reshape(count // fold, fold * width)
    hot = (row_ids[:, None] // fold == jnp.arange(count // fold, dtype=jnp.int32)[None, :]).astype(
        jnp.bfloat16
    )
    picked = jnp.dot(hot, wide, preferred_element_type=jnp.float32)
    lane = row_ids % fold
    rows = picked[:, :width]
    for j in range(1, fold):
        rows = jnp.where((lane == j)[:, None], picked[:, j * width : (j + 1) * width], rows)
    return rows.astype(jnp.bfloat16)


def scatter_rows(messages, row_ids, count, fold):
    width = messages.shape[1]
    lane = row_ids % fold
    spread = jnp.concatenate(
        [jnp.where((lane == j)[:, None], messages, jnp.zeros_like(messages)) for j in range(fold)],
        axis=1,
    )
    hot = (row_ids[:, None] // fold == jnp.arange(count // fold, dtype=jnp.int32)[None, :]).astype(
        jnp.bfloat16
    )
    total = lax.dot_general(
        hot, spread, (((0,), (0,)), ((), ())), preferred_element_type=jnp.float32
    )
    return total.reshape(count, width)


def body(
    vertex_state,
    link_state_slotted,
    source_vertex_ids,
    target_vertex_ids,
    active_link_tally,
    halo_outgoing_ids,
    link_layer_alpha,
    link_layer_beta,
    link_layer_gamma,
    link_scale_factor,
    vertex_layer_alpha,
    vertex_layer_beta,
    vertex_layer_gamma,
    vertex_scale_factor,
    focus_scale_factor,
    vertex_content_factor,
    cluster_affinity_factor,
    softness_level,
    cluster_probe_lookup,
    cluster_content_linear,
    closing_linear_factor,
):
    node_count = vertex_state.shape[0]
    feature_width = vertex_state.shape[1]
    capacity = link_state_slotted.shape[0]
    offsets = (1, -1, 2, -2)
    outgoing = pick_rows(vertex_state, halo_outgoing_ids[0].reshape(-1))
    extended = exchange_halos(
        vertex_state, outgoing.reshape(halo_outgoing_ids.shape[1:] + (feature_width,)), offsets
    )
    extended_ids = jnp.arange(extended.shape[0], dtype=jnp.int32)
    node_ids = jnp.arange(node_count, dtype=jnp.int32)
    block_rows = capacity // lax.axis_size("head")
    share = capacity // lax.axis_size("head")
    first_row = lax.axis_index("head") * share
    edge_rows = lax.dynamic_slice_in_dim(link_state_slotted, first_row, share, 0)
    send_rows = lax.dynamic_slice_in_dim(source_vertex_ids, first_row, share, 0)
    recv_rows = lax.dynamic_slice_in_dim(target_vertex_ids, first_row, share, 0)
    turns = edge_rows.shape[0] // block_rows
    edge_blocks = edge_rows.reshape(turns, block_rows, feature_width)
    send_blocks = send_rows.reshape(turns, block_rows)
    recv_blocks = recv_rows.reshape(turns, block_rows)

    def step(total, item):
        edge_part, send_part, recv_part, turn = item
        sender_rows = gather_rows(extended, send_part, FOLD)
        receiver_rows = gather_rows(vertex_state, recv_part, FOLD)
        pre = jnp.dot(
            edge_part, link_layer_alpha[:feature_width], preferred_element_type=jnp.float32
        )
        pre = pre + jnp.dot(
            sender_rows,
            link_layer_alpha[feature_width : 2 * feature_width],
            preferred_element_type=jnp.float32,
        )
        pre = pre + jnp.dot(
            receiver_rows, link_layer_alpha[2 * feature_width :], preferred_element_type=jnp.float32
        )
        first = jax.nn.silu(pre).astype(jnp.bfloat16)
        second = jax.nn.silu(
            jnp.dot(first, link_layer_beta, preferred_element_type=jnp.float32)
        ).astype(jnp.bfloat16)
        third = jnp.dot(second, link_layer_gamma, preferred_element_type=jnp.float32)
        edge_new = (edge_part.astype(jnp.float32) + layer_norm(third, link_scale_factor)).astype(
            jnp.bfloat16
        )
        position = first_row + turn * block_rows + jnp.arange(block_rows, dtype=jnp.int32)
        live = position < active_link_tally[0]
        messages = jnp.where(live[:, None], edge_new, jnp.zeros_like(edge_new))
        gathered = scatter_rows(messages, recv_part, node_count, FOLD)
        return (total + gathered, None)

    start = jnp.zeros((node_count, feature_width), jnp.float32)
    total, unused = lax.scan(
        step, start, (edge_blocks, send_blocks, recv_blocks, jnp.arange(turns, dtype=jnp.int32))
    )
    summed = lax.psum(total, "head")
    refreshed_vertices = node_section(
        vertex_state,
        summed.astype(jnp.bfloat16),
        vertex_layer_alpha,
        vertex_layer_beta,
        vertex_layer_gamma,
        vertex_scale_factor,
    )
    weights_b, numer, denom = slice_partial_terms(
        refreshed_vertices,
        focus_scale_factor,
        vertex_content_factor,
        cluster_affinity_factor,
        softness_level,
    )
    numer, denom = psum_slices(numer, denom)
    slice_out = slice_mixing(numer, denom, cluster_probe_lookup, cluster_content_linear)
    attended = attend_rows(weights_b, slice_out)
    projected = jnp.dot(attended, closing_linear_factor, preferred_element_type=jnp.float32)
    return (refreshed_vertices.astype(jnp.float32) + projected).astype(jnp.bfloat16)


def solution(mesh):
    in_specs = (
        P("dom", None),
        P("dom", None),
        P("dom"),
        P("dom"),
        P("dom"),
        P("dom", None, None),
        P(),
        P(),
        P(),
        P(),
        P(),
        P(),
        P(),
        P(),
        P(),
        P(),
        P(),
        P(),
        P(),
        P(),
        P(),
    )
    out_specs = P("dom", None)
    return jax.shard_map(body, mesh=mesh, in_specs=in_specs, out_specs=out_specs, check_vma=False)
```

```python
import functools
import math

import jax
import jax.numpy as jnp
from jax import lax
from jax.experimental import pallas as pl
from jax.experimental.pallas import tpu as pltpu
from jax.sharding import PartitionSpec as P

HEAD_DIM = 16
GROUPS_PER_LANE = 64
FOLD = 4


def passed_along(value, axis, steps):
    count = lax.axis_size(axis)
    first, last = (max(0, -steps), min(count, count - steps))
    return lax.ppermute(value, axis, [(source, source + steps) for source in range(first, last)])


def _radix_kernel(radix, steps, x_ref, o_ref, inbox, send_sem, recv_sem):
    me = lax.axis_index("dom")
    spans = [radix**s for s in range(steps)]
    digits = [(me // span) % radix for span in spans]
    partners = [
        [me + ((digit + j) % radix - digit) * span for j in range(1, radix)]
        for digit, span in zip(digits, spans)
    ]
    barrier = pltpu.get_barrier_semaphore()
    for group in partners:
        for partner in group:
            pl.semaphore_signal(
                barrier, 1, device_id={"dom": partner}, device_id_type=pl.DeviceIdType.MESH
            )
    pl.semaphore_wait(barrier, steps * (radix - 1))
    for s in range(steps):
        source = x_ref if s == 0 else o_ref
        copies = []
        for j, partner in enumerate(partners[s]):
            copy = pltpu.make_async_remote_copy(
                src_ref=source,
                dst_ref=inbox.at[s, digits[s]],
                send_sem=send_sem.at[s, j],
                recv_sem=recv_sem.at[s, digits[s]],
                device_id={"dom": partner},
                device_id_type=pl.DeviceIdType.MESH,
            )
            copy.start()
            copies.append(copy)
        inbox[s, digits[s]] = source[...]
        for copy in copies:
            copy.wait_send()
        for j, partner in enumerate(partners[s]):
            slot = (digits[s] + j + 1) % radix
            pltpu.make_async_remote_copy(
                src_ref=source,
                dst_ref=inbox.at[s, slot],
                send_sem=send_sem.at[s, j],
                recv_sem=recv_sem.at[s, slot],
                device_id={"dom": partner},
                device_id_type=pl.DeviceIdType.MESH,
            ).wait_recv()
        total = inbox[s, 0]
        for d in range(1, radix):
            total = total + inbox[s, d]
        o_ref[...] = total


def dom_sum(flat):
    count = lax.axis_size("dom")
    radix = 4
    steps = 0
    while radix ** (steps + 1) <= count:
        steps += 1
    assert radix**steps == count
    return pl.pallas_call(
        functools.partial(_radix_kernel, radix, steps),
        out_shape=jax.ShapeDtypeStruct(flat.shape, flat.dtype),
        in_specs=[pl.BlockSpec(memory_space=pltpu.VMEM)],
        out_specs=pl.BlockSpec(memory_space=pltpu.VMEM),
        scratch_shapes=[
            pltpu.VMEM((steps, radix) + flat.shape, flat.dtype),
            pltpu.SemaphoreType.DMA((steps, radix - 1)),
            pltpu.SemaphoreType.DMA((steps, radix)),
        ],
        compiler_params=pltpu.CompilerParams(collective_id=0, has_side_effects=True),
    )(flat)


def _halo_kernel(offsets, own_ref, out_ref, ext_ref, send_sem, recv_sem, pass_sem, land_sem):
    me = lax.axis_index("dom")
    count = lax.axis_size("dom")
    core = lax.axis_index("head")
    sibling = 1 - core
    rows = own_ref.shape[0]
    halo = out_ref.shape[1]
    half = halo // 2
    mesh_ids = pl.DeviceIdType.MESH
    barrier = pltpu.get_barrier_semaphore()
    for offset in offsets:
        pl.semaphore_signal(
            barrier, 1, device_id={"dom": (me + offset + count) % count}, device_id_type=mesh_ids
        )
    pl.semaphore_signal(barrier, 1, device_id={"head": sibling}, device_id_type=mesh_ids)
    pl.semaphore_wait(barrier, len(offsets) + 1)
    sends = []
    for k, offset in enumerate(offsets):
        copy = pltpu.make_async_remote_copy(
            src_ref=out_ref.at[k, pl.ds(core * half, half)],
            dst_ref=ext_ref.at[pl.ds(rows + k * halo + core * half, half)],
            send_sem=send_sem.at[k],
            recv_sem=recv_sem.at[k],
            device_id={"dom": (me + offset + count) % count},
            device_id_type=mesh_ids,
        )
        copy.start()
        sends.append(copy)
    ext_ref[pl.ds(0, rows)] = own_ref[...]
    passes = []
    for k in range(len(offsets)):
        sends[k].wait_recv()
        forward = pltpu.make_async_remote_copy(
            src_ref=ext_ref.at[pl.ds(rows + k * halo + core * half, half)],
            dst_ref=ext_ref.at[pl.ds(rows + k * halo + core * half, half)],
            send_sem=pass_sem.at[k],
            recv_sem=land_sem.at[k],
            device_id={"head": sibling},
            device_id_type=mesh_ids,
        )
        forward.start()
        passes.append(forward)
    for copy in sends:
        copy.wait_send()
    for forward in passes:
        forward.wait()
    for k, offset in enumerate(offsets):
        if offset > 0:
            inside = (me + count - offset) // count
        else:
            inside = (2 * count - 1 + offset - me) // count
        slot = pl.ds(rows + k * halo, halo)
        ext_ref[slot] = ext_ref[slot] * inside.astype(ext_ref.dtype)


def exchange_halos(own_rows, outgoing, offsets):
    rows = own_rows.shape[0]
    total = rows + outgoing.shape[0] * outgoing.shape[1]
    return pl.pallas_call(
        functools.partial(_halo_kernel, offsets),
        out_shape=jax.ShapeDtypeStruct((total, own_rows.shape[1]), own_rows.dtype),
        in_specs=[pl.BlockSpec(memory_space=pltpu.VMEM)] * 2,
        out_specs=pl.BlockSpec(memory_space=pltpu.VMEM),
        scratch_shapes=[pltpu.SemaphoreType.DMA((len(offsets),))] * 4,
        compiler_params=pltpu.CompilerParams(collective_id=1, has_side_effects=True),
    )(own_rows, outgoing)


def _sibling_kernel(x_ref, o_ref, inbox, send_sem, recv_sem):
    sibling = 1 - lax.axis_index("head")
    mesh_ids = pl.DeviceIdType.MESH
    barrier = pltpu.get_barrier_semaphore()
    pl.semaphore_signal(barrier, 1, device_id={"head": sibling}, device_id_type=mesh_ids)
    pl.semaphore_wait(barrier, 1)
    copy = pltpu.make_async_remote_copy(
        src_ref=x_ref,
        dst_ref=inbox,
        send_sem=send_sem,
        recv_sem=recv_sem,
        device_id={"head": sibling},
        device_id_type=mesh_ids,
    )
    copy.start()
    copy.wait()
    o_ref[...] = x_ref[...] + inbox[...]


def sibling_sum(x, collective_id):
    return pl.pallas_call(
        _sibling_kernel,
        out_shape=jax.ShapeDtypeStruct(x.shape, x.dtype),
        in_specs=[pl.BlockSpec(memory_space=pltpu.VMEM)],
        out_specs=pl.BlockSpec(memory_space=pltpu.VMEM),
        scratch_shapes=[
            pltpu.VMEM(x.shape, x.dtype),
            pltpu.SemaphoreType.DMA(()),
            pltpu.SemaphoreType.DMA(()),
        ],
        compiler_params=pltpu.CompilerParams(
            collective_id=collective_id, has_side_effects=True
        ),
    )(x)


def psum_slices(numer, denom):
    joined = jnp.concatenate([numer.reshape(-1), denom.reshape(-1)])
    rows = -(-joined.shape[0] // 1024) * 8
    padded = jnp.zeros((rows * 128,), joined.dtype).at[: joined.shape[0]].set(joined)
    total = dom_sum(padded.reshape(rows, 128)).reshape(-1)
    numer_size = numer.size
    return (
        total[:numer_size].reshape(numer.shape),
        total[numer_size : numer_size + denom.size].reshape(denom.shape),
    )


def layer_norm(values, gain_row):
    row_mean = jnp.mean(values, axis=-1, keepdims=True)
    centred = values - row_mean
    row_var = jnp.mean(centred * centred, axis=-1, keepdims=True)
    return centred * lax.rsqrt(row_var + 1e-05) * gain_row


def node_section(
    own_rows,
    summed_b,
    vertex_layer_alpha,
    vertex_layer_beta,
    vertex_layer_gamma,
    vertex_scale_factor,
):
    feature_width = own_rows.shape[1]
    node_pre = jnp.dot(
        own_rows, vertex_layer_alpha[:feature_width], preferred_element_type=jnp.float32
    )
    node_pre = node_pre + jnp.dot(
        summed_b, vertex_layer_alpha[feature_width:], preferred_element_type=jnp.float32
    )
    node_one = jax.nn.silu(node_pre).astype(jnp.bfloat16)
    node_two = jax.nn.silu(
        jnp.dot(node_one, vertex_layer_beta, preferred_element_type=jnp.float32)
    ).astype(jnp.bfloat16)
    node_three = jnp.dot(node_two, vertex_layer_gamma, preferred_element_type=jnp.float32)
    return (own_rows.astype(jnp.float32) + layer_norm(node_three, vertex_scale_factor)).astype(
        jnp.bfloat16
    )


def slice_partial_terms(
    refreshed_vertices,
    focus_scale_factor,
    vertex_content_factor,
    cluster_affinity_factor,
    softness_level,
):
    count_of_rows = refreshed_vertices.shape[0]
    domain_channel_split = softness_level.shape[0]
    standardised_entries = layer_norm(
        refreshed_vertices.astype(jnp.float32), focus_scale_factor
    ).astype(jnp.bfloat16)
    values = jnp.dot(
        standardised_entries, vertex_content_factor, preferred_element_type=jnp.float32
    ).astype(jnp.bfloat16)
    cluster_affinities = jnp.dot(
        standardised_entries, cluster_affinity_factor, preferred_element_type=jnp.float32
    )
    cluster_affinities = (
        cluster_affinities.reshape(count_of_rows, domain_channel_split, GROUPS_PER_LANE)
        / softness_level[None, :, None]
    )
    weights = jax.nn.softmax(cluster_affinities, axis=-1)
    weights_b = weights.astype(jnp.bfloat16)
    numer = jnp.einsum(
        "nhs,nhc->hsc",
        weights_b,
        values.reshape(count_of_rows, domain_channel_split, HEAD_DIM),
        preferred_element_type=jnp.float32,
    )
    denom = jnp.sum(weights, axis=0)
    return (weights_b, numer, denom)


def slice_mixing(numer, denom, cluster_probe_lookup, cluster_content_linear):
    tokens = numer / denom[:, :, None]
    highest = lax.Precision.HIGHEST
    query = jnp.einsum("hsc,hcd->hsd", tokens, cluster_probe_lookup[0], precision=highest)
    keys = jnp.einsum("hsc,hcd->hsd", tokens, cluster_probe_lookup[1], precision=highest)
    carried = jnp.einsum("hsc,hcd->hsd", tokens, cluster_content_linear, precision=highest)
    scores = jnp.einsum("hsd,htd->hst", query, keys, precision=highest) / math.sqrt(HEAD_DIM)
    mixing = jax.nn.softmax(scores, axis=-1)
    return jnp.einsum("hst,htd->hsd", mixing, carried, precision=highest).astype(jnp.bfloat16)


def attend_rows(weights_b, slice_out):
    count_of_rows = weights_b.shape[0]
    domain_channel_split = weights_b.shape[1]
    attended = jnp.einsum("nhs,hsd->nhd", weights_b, slice_out, preferred_element_type=jnp.float32)
    return attended.reshape(count_of_rows, domain_channel_split * HEAD_DIM).astype(jnp.bfloat16)


def pick_rows(table, row_ids):
    table_ids = jnp.arange(table.shape[0], dtype=jnp.int32)
    selector = (row_ids[:, None] == table_ids[None, :]).astype(jnp.bfloat16)
    return jnp.dot(selector, table, preferred_element_type=jnp.float32).astype(jnp.bfloat16)


def gather_rows(table, row_ids, fold):
    count, width = table.shape
    wide = table.reshape(count // fold, fold * width)
    hot = (row_ids[:, None] // fold == jnp.arange(count // fold, dtype=jnp.int32)[None, :]).astype(
        jnp.bfloat16
    )
    picked = jnp.dot(hot, wide, preferred_element_type=jnp.float32)
    lane = row_ids % fold
    rows = picked[:, :width]
    for j in range(1, fold):
        rows = jnp.where((lane == j)[:, None], picked[:, j * width : (j + 1) * width], rows)
    return rows.astype(jnp.bfloat16)


def scatter_rows(messages, row_ids, count, fold):
    width = messages.shape[1]
    lane = row_ids % fold
    spread = jnp.concatenate(
        [jnp.where((lane == j)[:, None], messages, jnp.zeros_like(messages)) for j in range(fold)],
        axis=1,
    )
    hot = (row_ids[:, None] // fold == jnp.arange(count // fold, dtype=jnp.int32)[None, :]).astype(
        jnp.bfloat16
    )
    total = lax.dot_general(
        hot, spread, (((0,), (0,)), ((), ())), preferred_element_type=jnp.float32
    )
    return total.reshape(count, width)


def body(
    vertex_state,
    link_state_slotted,
    source_vertex_ids,
    target_vertex_ids,
    active_link_tally,
    halo_outgoing_ids,
    link_layer_alpha,
    link_layer_beta,
    link_layer_gamma,
    link_scale_factor,
    vertex_layer_alpha,
    vertex_layer_beta,
    vertex_layer_gamma,
    vertex_scale_factor,
    focus_scale_factor,
    vertex_content_factor,
    cluster_affinity_factor,
    softness_level,
    cluster_probe_lookup,
    cluster_content_linear,
    closing_linear_factor,
):
    node_count = vertex_state.shape[0]
    feature_width = vertex_state.shape[1]
    capacity = link_state_slotted.shape[0]
    offsets = (1, -1, 2, -2)
    outgoing = pick_rows(vertex_state, halo_outgoing_ids[0].reshape(-1))
    extended = exchange_halos(
        vertex_state, outgoing.reshape(halo_outgoing_ids.shape[1:] + (feature_width,)), offsets
    )
    extended_ids = jnp.arange(extended.shape[0], dtype=jnp.int32)
    node_ids = jnp.arange(node_count, dtype=jnp.int32)
    block_rows = capacity // lax.axis_size("head")
    share = capacity // lax.axis_size("head")
    first_row = lax.axis_index("head") * share
    edge_rows = lax.dynamic_slice_in_dim(link_state_slotted, first_row, share, 0)
    send_rows = lax.dynamic_slice_in_dim(source_vertex_ids, first_row, share, 0)
    recv_rows = lax.dynamic_slice_in_dim(target_vertex_ids, first_row, share, 0)
    turns = edge_rows.shape[0] // block_rows
    edge_blocks = edge_rows.reshape(turns, block_rows, feature_width)
    send_blocks = send_rows.reshape(turns, block_rows)
    recv_blocks = recv_rows.reshape(turns, block_rows)

    def step(total, item):
        edge_part, send_part, recv_part, turn = item
        sender_rows = gather_rows(extended, send_part, FOLD)
        receiver_rows = gather_rows(vertex_state, recv_part, FOLD)
        pre = jnp.dot(
            edge_part, link_layer_alpha[:feature_width], preferred_element_type=jnp.float32
        )
        pre = pre + jnp.dot(
            sender_rows,
            link_layer_alpha[feature_width : 2 * feature_width],
            preferred_element_type=jnp.float32,
        )
        pre = pre + jnp.dot(
            receiver_rows, link_layer_alpha[2 * feature_width :], preferred_element_type=jnp.float32
        )
        first = jax.nn.silu(pre).astype(jnp.bfloat16)
        second = jax.nn.silu(
            jnp.dot(first, link_layer_beta, preferred_element_type=jnp.float32)
        ).astype(jnp.bfloat16)
        third = jnp.dot(second, link_layer_gamma, preferred_element_type=jnp.float32)
        edge_new = (edge_part.astype(jnp.float32) + layer_norm(third, link_scale_factor)).astype(
            jnp.bfloat16
        )
        position = first_row + turn * block_rows + jnp.arange(block_rows, dtype=jnp.int32)
        live = position < active_link_tally[0]
        messages = jnp.where(live[:, None], edge_new, jnp.zeros_like(edge_new))
        gathered = scatter_rows(messages, recv_part, node_count, FOLD)
        return (total + gathered, None)

    start = jnp.zeros((node_count, feature_width), jnp.float32)
    total, unused = lax.scan(
        step, start, (edge_blocks, send_blocks, recv_blocks, jnp.arange(turns, dtype=jnp.int32))
    )
    summed = sibling_sum(total, 2)
    refreshed_vertices = node_section(
        vertex_state,
        summed.astype(jnp.bfloat16),
        vertex_layer_alpha,
        vertex_layer_beta,
        vertex_layer_gamma,
        vertex_scale_factor,
    )
    weights_b, numer, denom = slice_partial_terms(
        refreshed_vertices,
        focus_scale_factor,
        vertex_content_factor,
        cluster_affinity_factor,
        softness_level,
    )
    numer, denom = psum_slices(numer, denom)
    slice_out = slice_mixing(numer, denom, cluster_probe_lookup, cluster_content_linear)
    attended = attend_rows(weights_b, slice_out)
    projected = sibling_sum(
        jnp.dot(attended, closing_linear_factor, preferred_element_type=jnp.float32), 3
    )
    return (refreshed_vertices.astype(jnp.float32) + projected).astype(jnp.bfloat16)


def solution(mesh):
    in_specs = (
        P("dom", None),
        P("dom", None),
        P("dom"),
        P("dom"),
        P("dom"),
        P("dom", None, None),
        P(),
        P(),
        P(),
        P(),
        P(),
        P(),
        P(),
        P(),
        P(),
        P(None, "head"),
        P(None, "head"),
        P("head"),
        P(None, "head", None, None),
        P("head", None, None),
        P("head", None),
    )
    out_specs = P("dom", None)
    return jax.shard_map(body, mesh=mesh, in_specs=in_specs, out_specs=out_specs, check_vma=False)
```

```python
import functools
import math

import jax
import jax.numpy as jnp
from jax import lax
from jax.experimental import pallas as pl
from jax.experimental.pallas import tpu as pltpu
from jax.sharding import PartitionSpec as P

HEAD_DIM = 16
GROUPS_PER_LANE = 64
FOLD = 4


def passed_along(value, axis, steps):
    count = lax.axis_size(axis)
    first, last = (max(0, -steps), min(count, count - steps))
    return lax.ppermute(value, axis, [(source, source + steps) for source in range(first, last)])


def _radix_kernel(radix, steps, x_ref, o_ref, inbox, send_sem, recv_sem):
    me = lax.axis_index("dom")
    spans = [radix**s for s in range(steps)]
    digits = [(me // span) % radix for span in spans]
    partners = [
        [me + ((digit + j) % radix - digit) * span for j in range(1, radix)]
        for digit, span in zip(digits, spans)
    ]
    barrier = pltpu.get_barrier_semaphore()
    for group in partners:
        for partner in group:
            pl.semaphore_signal(
                barrier, 1, device_id={"dom": partner}, device_id_type=pl.DeviceIdType.MESH
            )
    pl.semaphore_wait(barrier, steps * (radix - 1))
    for s in range(steps):
        source = x_ref if s == 0 else o_ref
        copies = []
        for j, partner in enumerate(partners[s]):
            copy = pltpu.make_async_remote_copy(
                src_ref=source,
                dst_ref=inbox.at[s, digits[s]],
                send_sem=send_sem.at[s, j],
                recv_sem=recv_sem.at[s, digits[s]],
                device_id={"dom": partner},
                device_id_type=pl.DeviceIdType.MESH,
            )
            copy.start()
            copies.append(copy)
        inbox[s, digits[s]] = source[...]
        for copy in copies:
            copy.wait_send()
        for j, partner in enumerate(partners[s]):
            slot = (digits[s] + j + 1) % radix
            pltpu.make_async_remote_copy(
                src_ref=source,
                dst_ref=inbox.at[s, slot],
                send_sem=send_sem.at[s, j],
                recv_sem=recv_sem.at[s, slot],
                device_id={"dom": partner},
                device_id_type=pl.DeviceIdType.MESH,
            ).wait_recv()
        total = inbox[s, 0]
        for d in range(1, radix):
            total = total + inbox[s, d]
        o_ref[...] = total


def dom_sum(flat):
    count = lax.axis_size("dom")
    radix = 4
    steps = 0
    while radix ** (steps + 1) <= count:
        steps += 1
    assert radix**steps == count
    return pl.pallas_call(
        functools.partial(_radix_kernel, radix, steps),
        out_shape=jax.ShapeDtypeStruct(flat.shape, flat.dtype),
        in_specs=[pl.BlockSpec(memory_space=pltpu.VMEM)],
        out_specs=pl.BlockSpec(memory_space=pltpu.VMEM),
        scratch_shapes=[
            pltpu.VMEM((steps, radix) + flat.shape, flat.dtype),
            pltpu.SemaphoreType.DMA((steps, radix - 1)),
            pltpu.SemaphoreType.DMA((steps, radix)),
        ],
        compiler_params=pltpu.CompilerParams(collective_id=0, has_side_effects=True),
    )(flat)


def _halo_kernel(offsets, own_ref, out_ref, ext_ref, send_sem, recv_sem, pass_sem, land_sem):
    me = lax.axis_index("dom")
    count = lax.axis_size("dom")
    core = lax.axis_index("head")
    sibling = 1 - core
    rows = own_ref.shape[0]
    halo = out_ref.shape[1]
    half = halo // 2
    mesh_ids = pl.DeviceIdType.MESH
    barrier = pltpu.get_barrier_semaphore()
    for offset in offsets:
        pl.semaphore_signal(
            barrier, 1, device_id={"dom": (me + offset + count) % count}, device_id_type=mesh_ids
        )
    pl.semaphore_signal(barrier, 1, device_id={"head": sibling}, device_id_type=mesh_ids)
    pl.semaphore_wait(barrier, len(offsets) + 1)
    sends = []
    for k, offset in enumerate(offsets):
        copy = pltpu.make_async_remote_copy(
            src_ref=out_ref.at[k, pl.ds(core * half, half)],
            dst_ref=ext_ref.at[pl.ds(rows + k * halo + core * half, half)],
            send_sem=send_sem.at[k],
            recv_sem=recv_sem.at[k],
            device_id={"dom": (me + offset + count) % count},
            device_id_type=mesh_ids,
        )
        copy.start()
        sends.append(copy)
    ext_ref[pl.ds(0, rows)] = own_ref[...]
    passes = []
    for k in range(len(offsets)):
        sends[k].wait_recv()
        forward = pltpu.make_async_remote_copy(
            src_ref=ext_ref.at[pl.ds(rows + k * halo + core * half, half)],
            dst_ref=ext_ref.at[pl.ds(rows + k * halo + core * half, half)],
            send_sem=pass_sem.at[k],
            recv_sem=land_sem.at[k],
            device_id={"head": sibling},
            device_id_type=mesh_ids,
        )
        forward.start()
        passes.append(forward)
    for copy in sends:
        copy.wait_send()
    for forward in passes:
        forward.wait()
    for k, offset in enumerate(offsets):
        if offset > 0:
            inside = (me + count - offset) // count
        else:
            inside = (2 * count - 1 + offset - me) // count
        slot = pl.ds(rows + k * halo, halo)
        ext_ref[slot] = ext_ref[slot] * inside.astype(ext_ref.dtype)


def exchange_halos(own_rows, outgoing, offsets):
    rows = own_rows.shape[0]
    total = rows + outgoing.shape[0] * outgoing.shape[1]
    return pl.pallas_call(
        functools.partial(_halo_kernel, offsets),
        out_shape=jax.ShapeDtypeStruct((total, own_rows.shape[1]), own_rows.dtype),
        in_specs=[pl.BlockSpec(memory_space=pltpu.VMEM)] * 2,
        out_specs=pl.BlockSpec(memory_space=pltpu.VMEM),
        scratch_shapes=[pltpu.SemaphoreType.DMA((len(offsets),))] * 4,
        compiler_params=pltpu.CompilerParams(collective_id=1, has_side_effects=True),
    )(own_rows, outgoing)


def _sibling_kernel(x_ref, o_ref, inbox, send_sem, recv_sem):
    sibling = 1 - lax.axis_index("head")
    mesh_ids = pl.DeviceIdType.MESH
    barrier = pltpu.get_barrier_semaphore()
    pl.semaphore_signal(barrier, 1, device_id={"head": sibling}, device_id_type=mesh_ids)
    pl.semaphore_wait(barrier, 1)
    copy = pltpu.make_async_remote_copy(
        src_ref=x_ref,
        dst_ref=inbox,
        send_sem=send_sem,
        recv_sem=recv_sem,
        device_id={"head": sibling},
        device_id_type=mesh_ids,
    )
    copy.start()
    copy.wait()
    o_ref[...] = x_ref[...] + inbox[...]


def sibling_sum(x, collective_id):
    return pl.pallas_call(
        _sibling_kernel,
        out_shape=jax.ShapeDtypeStruct(x.shape, x.dtype),
        in_specs=[pl.BlockSpec(memory_space=pltpu.VMEM)],
        out_specs=pl.BlockSpec(memory_space=pltpu.VMEM),
        scratch_shapes=[
            pltpu.VMEM(x.shape, x.dtype),
            pltpu.SemaphoreType.DMA(()),
            pltpu.SemaphoreType.DMA(()),
        ],
        compiler_params=pltpu.CompilerParams(
            collective_id=collective_id, has_side_effects=True
        ),
    )(x)


def _silu(values):
    return values * (1.0 / (1.0 + jnp.exp(-values)))


def _fold_pick(table_ref, ids, fold):
    chunk = ids.shape[0]
    groups = table_ref.shape[0]
    width = table_ref.shape[1] // fold
    shift = fold.bit_length() - 1
    hot = (
        lax.shift_right_logical(ids, shift) == lax.broadcasted_iota(jnp.int32, (chunk, groups), 1)
    ).astype(jnp.bfloat16)
    picked = jnp.dot(hot, table_ref[...], preferred_element_type=jnp.float32)
    lane = jnp.bitwise_and(ids, fold - 1)
    rows = picked[:, :width]
    for j in range(1, fold):
        rows = jnp.where(lane == j, picked[:, j * width : (j + 1) * width], rows)
    return rows.astype(jnp.bfloat16)


def _edge_kernel(fold, scalars, edge_ref, src_ref, dst_ref, dst_row_ref, ext_ref, own_ref,
                 alpha_ref, beta_ref, gamma_ref, gain_ref, out_ref):
    step = pl.program_id(0)
    chunk, width = edge_ref.shape

    @pl.when(step == 0)
    def _():
        out_ref[...] = jnp.zeros_like(out_ref)

    edge = edge_ref[...]
    dst = dst_ref[...]
    sender = _fold_pick(ext_ref, src_ref[...], fold)
    receiver = _fold_pick(own_ref, dst, fold)
    pre = jnp.dot(edge, alpha_ref[0:width], preferred_element_type=jnp.float32)
    pre = pre + jnp.dot(sender, alpha_ref[width : 2 * width], preferred_element_type=jnp.float32)
    pre = pre + jnp.dot(receiver, alpha_ref[2 * width :], preferred_element_type=jnp.float32)
    first = _silu(pre).astype(jnp.bfloat16)
    second = _silu(jnp.dot(first, beta_ref[...], preferred_element_type=jnp.float32)).astype(
        jnp.bfloat16
    )
    third = jnp.dot(second, gamma_ref[...], preferred_element_type=jnp.float32)
    row_mean = jnp.mean(third, axis=-1, keepdims=True)
    centred = third - row_mean
    row_var = jnp.mean(centred * centred, axis=-1, keepdims=True)
    normed = centred * lax.rsqrt(row_var + 1e-05) * gain_ref[...]
    edge_new = (edge.astype(jnp.float32) + normed).astype(jnp.bfloat16)
    position = scalars[1] + step * chunk + lax.broadcasted_iota(jnp.int32, (chunk, 1), 0)
    live = position < scalars[2]
    messages = jnp.where(live, edge_new, jnp.zeros_like(edge_new))
    lane = jnp.bitwise_and(dst, fold - 1)
    spread = jnp.concatenate(
        [jnp.where(lane == j, messages, jnp.zeros_like(messages)) for j in range(fold)], axis=1
    )
    groups = out_ref.shape[0]
    shift = fold.bit_length() - 1
    hot_t = (
        lax.broadcasted_iota(jnp.int32, (groups, chunk), 0)
        == lax.shift_right_logical(dst_row_ref[0], shift)
    ).astype(jnp.bfloat16)
    out_ref[...] += jnp.dot(hot_t, spread, preferred_element_type=jnp.float32)


def edge_messages(edges, send_ids, recv_ids, extended, own_rows, alpha, beta, gamma, gain,
                  first_row, share, tally, chunk=512, fold=FOLD):
    slots, width = edges.shape
    nodes = own_rows.shape[0]
    turns = share // chunk
    scalars = jnp.stack([first_row // chunk, first_row, tally]).astype(jnp.int32)
    ext_wide = extended.reshape(extended.shape[0] // fold, fold * width)
    own_wide = own_rows.reshape(nodes // fold, fold * width)
    full = lambda shape: pl.BlockSpec(shape, lambda i, s: (0,) * len(shape))
    grid_spec = pltpu.PrefetchScalarGridSpec(
        num_scalar_prefetch=1,
        grid=(turns,),
        in_specs=[
            pl.BlockSpec((chunk, width), lambda i, s: (s[0] + i, 0)),
            pl.BlockSpec((chunk, 1), lambda i, s: (s[0] + i, 0)),
            pl.BlockSpec((chunk, 1), lambda i, s: (s[0] + i, 0)),
            pl.BlockSpec((1, 1, chunk), lambda i, s: (s[0] + i, 0, 0)),
            full(ext_wide.shape),
            full(own_wide.shape),
            full(alpha.shape),
            full(beta.shape),
            full(gamma.shape),
            full((1, width)),
        ],
        out_specs=full((nodes // fold, fold * width)),
    )
    total = pl.pallas_call(
        functools.partial(_edge_kernel, fold),
        out_shape=jax.ShapeDtypeStruct((nodes // fold, fold * width), jnp.float32),
        grid_spec=grid_spec,
    )(
        scalars,
        edges,
        send_ids.reshape(slots, 1),
        recv_ids.reshape(slots, 1),
        recv_ids.reshape(slots // chunk, 1, chunk),
        ext_wide,
        own_wide,
        alpha,
        beta,
        gamma,
        gain.reshape(1, width).astype(jnp.float32),
    )
    return total.reshape(nodes, width)


def psum_slices(numer, denom):
    joined = jnp.concatenate([numer.reshape(-1), denom.reshape(-1)])
    rows = -(-joined.shape[0] // 1024) * 8
    padded = jnp.zeros((rows * 128,), joined.dtype).at[: joined.shape[0]].set(joined)
    total = dom_sum(padded.reshape(rows, 128)).reshape(-1)
    numer_size = numer.size
    return (
        total[:numer_size].reshape(numer.shape),
        total[numer_size : numer_size + denom.size].reshape(denom.shape),
    )


def layer_norm(values, gain_row):
    row_mean = jnp.mean(values, axis=-1, keepdims=True)
    centred = values - row_mean
    row_var = jnp.mean(centred * centred, axis=-1, keepdims=True)
    return centred * lax.rsqrt(row_var + 1e-05) * gain_row


def node_section(
    own_rows,
    summed_b,
    vertex_layer_alpha,
    vertex_layer_beta,
    vertex_layer_gamma,
    vertex_scale_factor,
):
    feature_width = own_rows.shape[1]
    node_pre = jnp.dot(
        own_rows, vertex_layer_alpha[:feature_width], preferred_element_type=jnp.float32
    )
    node_pre = node_pre + jnp.dot(
        summed_b, vertex_layer_alpha[feature_width:], preferred_element_type=jnp.float32
    )
    node_one = jax.nn.silu(node_pre).astype(jnp.bfloat16)
    node_two = jax.nn.silu(
        jnp.dot(node_one, vertex_layer_beta, preferred_element_type=jnp.float32)
    ).astype(jnp.bfloat16)
    node_three = jnp.dot(node_two, vertex_layer_gamma, preferred_element_type=jnp.float32)
    return (own_rows.astype(jnp.float32) + layer_norm(node_three, vertex_scale_factor)).astype(
        jnp.bfloat16
    )


def slice_partial_terms(
    refreshed_vertices,
    focus_scale_factor,
    vertex_content_factor,
    cluster_affinity_factor,
    softness_level,
):
    count_of_rows = refreshed_vertices.shape[0]
    domain_channel_split = softness_level.shape[0]
    standardised_entries = layer_norm(
        refreshed_vertices.astype(jnp.float32), focus_scale_factor
    ).astype(jnp.bfloat16)
    values = jnp.dot(
        standardised_entries, vertex_content_factor, preferred_element_type=jnp.float32
    ).astype(jnp.bfloat16)
    cluster_affinities = jnp.dot(
        standardised_entries, cluster_affinity_factor, preferred_element_type=jnp.float32
    )
    cluster_affinities = (
        cluster_affinities.reshape(count_of_rows, domain_channel_split, GROUPS_PER_LANE)
        / softness_level[None, :, None]
    )
    weights = jax.nn.softmax(cluster_affinities, axis=-1)
    weights_b = weights.astype(jnp.bfloat16)
    numer = jnp.einsum(
        "nhs,nhc->hsc",
        weights_b,
        values.reshape(count_of_rows, domain_channel_split, HEAD_DIM),
        preferred_element_type=jnp.float32,
    )
    denom = jnp.sum(weights, axis=0)
    return (weights_b, numer, denom)


def slice_mixing(numer, denom, cluster_probe_lookup, cluster_content_linear):
    tokens = numer / denom[:, :, None]
    highest = lax.Precision.HIGHEST
    query = jnp.einsum("hsc,hcd->hsd", tokens, cluster_probe_lookup[0], precision=highest)
    keys = jnp.einsum("hsc,hcd->hsd", tokens, cluster_probe_lookup[1], precision=highest)
    carried = jnp.einsum("hsc,hcd->hsd", tokens, cluster_content_linear, precision=highest)
    scores = jnp.einsum("hsd,htd->hst", query, keys, precision=highest) / math.sqrt(HEAD_DIM)
    mixing = jax.nn.softmax(scores, axis=-1)
    return jnp.einsum("hst,htd->hsd", mixing, carried, precision=highest).astype(jnp.bfloat16)


def attend_rows(weights_b, slice_out):
    count_of_rows = weights_b.shape[0]
    domain_channel_split = weights_b.shape[1]
    attended = jnp.einsum("nhs,hsd->nhd", weights_b, slice_out, preferred_element_type=jnp.float32)
    return attended.reshape(count_of_rows, domain_channel_split * HEAD_DIM).astype(jnp.bfloat16)


def pick_rows(table, row_ids):
    table_ids = jnp.arange(table.shape[0], dtype=jnp.int32)
    selector = (row_ids[:, None] == table_ids[None, :]).astype(jnp.bfloat16)
    return jnp.dot(selector, table, preferred_element_type=jnp.float32).astype(jnp.bfloat16)


def gather_rows(table, row_ids, fold):
    count, width = table.shape
    wide = table.reshape(count // fold, fold * width)
    hot = (row_ids[:, None] // fold == jnp.arange(count // fold, dtype=jnp.int32)[None, :]).astype(
        jnp.bfloat16
    )
    picked = jnp.dot(hot, wide, preferred_element_type=jnp.float32)
    lane = row_ids % fold
    rows = picked[:, :width]
    for j in range(1, fold):
        rows = jnp.where((lane == j)[:, None], picked[:, j * width : (j + 1) * width], rows)
    return rows.astype(jnp.bfloat16)


def scatter_rows(messages, row_ids, count, fold):
    width = messages.shape[1]
    lane = row_ids % fold
    spread = jnp.concatenate(
        [jnp.where((lane == j)[:, None], messages, jnp.zeros_like(messages)) for j in range(fold)],
        axis=1,
    )
    hot = (row_ids[:, None] // fold == jnp.arange(count // fold, dtype=jnp.int32)[None, :]).astype(
        jnp.bfloat16
    )
    total = lax.dot_general(
        hot, spread, (((0,), (0,)), ((), ())), preferred_element_type=jnp.float32
    )
    return total.reshape(count, width)


def body(
    vertex_state,
    link_state_slotted,
    source_vertex_ids,
    target_vertex_ids,
    active_link_tally,
    halo_outgoing_ids,
    link_layer_alpha,
    link_layer_beta,
    link_layer_gamma,
    link_scale_factor,
    vertex_layer_alpha,
    vertex_layer_beta,
    vertex_layer_gamma,
    vertex_scale_factor,
    focus_scale_factor,
    vertex_content_factor,
    cluster_affinity_factor,
    softness_level,
    cluster_probe_lookup,
    cluster_content_linear,
    closing_linear_factor,
):
    node_count = vertex_state.shape[0]
    feature_width = vertex_state.shape[1]
    capacity = link_state_slotted.shape[0]
    offsets = (1, -1, 2, -2)
    outgoing = pick_rows(vertex_state, halo_outgoing_ids[0].reshape(-1))
    extended = exchange_halos(
        vertex_state, outgoing.reshape(halo_outgoing_ids.shape[1:] + (feature_width,)), offsets
    )
    share = capacity // lax.axis_size("head")
    first_row = lax.axis_index("head") * share
    total = edge_messages(
        link_state_slotted,
        source_vertex_ids,
        target_vertex_ids,
        extended,
        vertex_state,
        link_layer_alpha,
        link_layer_beta,
        link_layer_gamma,
        link_scale_factor,
        first_row,
        share,
        active_link_tally[0],
    )
    summed = sibling_sum(total, 2)
    refreshed_vertices = node_section(
        vertex_state,
        summed.astype(jnp.bfloat16),
        vertex_layer_alpha,
        vertex_layer_beta,
        vertex_layer_gamma,
        vertex_scale_factor,
    )
    weights_b, numer, denom = slice_partial_terms(
        refreshed_vertices,
        focus_scale_factor,
        vertex_content_factor,
        cluster_affinity_factor,
        softness_level,
    )
    numer, denom = psum_slices(numer, denom)
    slice_out = slice_mixing(numer, denom, cluster_probe_lookup, cluster_content_linear)
    attended = attend_rows(weights_b, slice_out)
    projected = sibling_sum(
        jnp.dot(attended, closing_linear_factor, preferred_element_type=jnp.float32), 3
    )
    return (refreshed_vertices.astype(jnp.float32) + projected).astype(jnp.bfloat16)


def solution(mesh):
    in_specs = (
        P("dom", None),
        P("dom", None),
        P("dom"),
        P("dom"),
        P("dom"),
        P("dom", None, None),
        P(),
        P(),
        P(),
        P(),
        P(),
        P(),
        P(),
        P(),
        P(),
        P(None, "head"),
        P(None, "head"),
        P("head"),
        P(None, "head", None, None),
        P("head", None, None),
        P("head", None),
    )
    out_specs = P("dom", None)
    return jax.shard_map(body, mesh=mesh, in_specs=in_specs, out_specs=out_specs, check_vma=False)
```

```python
import functools
import math

import jax
import jax.numpy as jnp
from jax import lax
from jax.experimental import pallas as pl
from jax.experimental.pallas import tpu as pltpu
from jax.sharding import PartitionSpec as P

HEAD_DIM = 16
GROUPS_PER_LANE = 64
FOLD = 4


def passed_along(value, axis, steps):
    count = lax.axis_size(axis)
    first, last = (max(0, -steps), min(count, count - steps))
    return lax.ppermute(value, axis, [(source, source + steps) for source in range(first, last)])


def _radix_kernel(radix, steps, x_ref, o_ref, inbox, send_sem, recv_sem):
    me = lax.axis_index("dom")
    spans = [radix**s for s in range(steps)]
    digits = [(me // span) % radix for span in spans]
    partners = [
        [me + ((digit + j) % radix - digit) * span for j in range(1, radix)]
        for digit, span in zip(digits, spans)
    ]
    barrier = pltpu.get_barrier_semaphore()
    for group in partners:
        for partner in group:
            pl.semaphore_signal(
                barrier, 1, device_id={"dom": partner}, device_id_type=pl.DeviceIdType.MESH
            )
    pl.semaphore_wait(barrier, steps * (radix - 1))
    for s in range(steps):
        source = x_ref if s == 0 else o_ref
        copies = []
        for j, partner in enumerate(partners[s]):
            copy = pltpu.make_async_remote_copy(
                src_ref=source,
                dst_ref=inbox.at[s, digits[s]],
                send_sem=send_sem.at[s, j],
                recv_sem=recv_sem.at[s, digits[s]],
                device_id={"dom": partner},
                device_id_type=pl.DeviceIdType.MESH,
            )
            copy.start()
            copies.append(copy)
        inbox[s, digits[s]] = source[...]
        for copy in copies:
            copy.wait_send()
        for j, partner in enumerate(partners[s]):
            slot = (digits[s] + j + 1) % radix
            pltpu.make_async_remote_copy(
                src_ref=source,
                dst_ref=inbox.at[s, slot],
                send_sem=send_sem.at[s, j],
                recv_sem=recv_sem.at[s, slot],
                device_id={"dom": partner},
                device_id_type=pl.DeviceIdType.MESH,
            ).wait_recv()
        total = inbox[s, 0]
        for d in range(1, radix):
            total = total + inbox[s, d]
        o_ref[...] = total


def dom_sum(flat):
    count = lax.axis_size("dom")
    radix = 4
    steps = 0
    while radix ** (steps + 1) <= count:
        steps += 1
    assert radix**steps == count
    return pl.pallas_call(
        functools.partial(_radix_kernel, radix, steps),
        out_shape=jax.ShapeDtypeStruct(flat.shape, flat.dtype),
        in_specs=[pl.BlockSpec(memory_space=pltpu.VMEM)],
        out_specs=pl.BlockSpec(memory_space=pltpu.VMEM),
        scratch_shapes=[
            pltpu.VMEM((steps, radix) + flat.shape, flat.dtype),
            pltpu.SemaphoreType.DMA((steps, radix - 1)),
            pltpu.SemaphoreType.DMA((steps, radix)),
        ],
        compiler_params=pltpu.CompilerParams(collective_id=0, has_side_effects=True),
    )(flat)


def _halo_kernel(offsets, own_ref, out_ref, ext_ref, send_sem, recv_sem, pass_sem, land_sem):
    me = lax.axis_index("dom")
    count = lax.axis_size("dom")
    core = lax.axis_index("head")
    sibling = 1 - core
    rows = own_ref.shape[0]
    halo = out_ref.shape[1]
    half = halo // 2
    mesh_ids = pl.DeviceIdType.MESH
    barrier = pltpu.get_barrier_semaphore()
    for offset in offsets:
        pl.semaphore_signal(
            barrier, 1, device_id={"dom": (me + offset + count) % count}, device_id_type=mesh_ids
        )
    pl.semaphore_signal(barrier, 1, device_id={"head": sibling}, device_id_type=mesh_ids)
    pl.semaphore_wait(barrier, len(offsets) + 1)
    sends = []
    for k, offset in enumerate(offsets):
        copy = pltpu.make_async_remote_copy(
            src_ref=out_ref.at[k, pl.ds(core * half, half)],
            dst_ref=ext_ref.at[pl.ds(rows + k * halo + core * half, half)],
            send_sem=send_sem.at[k],
            recv_sem=recv_sem.at[k],
            device_id={"dom": (me + offset + count) % count},
            device_id_type=mesh_ids,
        )
        copy.start()
        sends.append(copy)
    ext_ref[pl.ds(0, rows)] = own_ref[...]
    passes = []
    for k in range(len(offsets)):
        sends[k].wait_recv()
        forward = pltpu.make_async_remote_copy(
            src_ref=ext_ref.at[pl.ds(rows + k * halo + core * half, half)],
            dst_ref=ext_ref.at[pl.ds(rows + k * halo + core * half, half)],
            send_sem=pass_sem.at[k],
            recv_sem=land_sem.at[k],
            device_id={"head": sibling},
            device_id_type=mesh_ids,
        )
        forward.start()
        passes.append(forward)
    for copy in sends:
        copy.wait_send()
    for forward in passes:
        forward.wait()
    for k, offset in enumerate(offsets):
        if offset > 0:
            inside = (me + count - offset) // count
        else:
            inside = (2 * count - 1 + offset - me) // count
        slot = pl.ds(rows + k * halo, halo)
        ext_ref[slot] = ext_ref[slot] * inside.astype(ext_ref.dtype)


def exchange_halos(own_rows, outgoing, offsets):
    rows = own_rows.shape[0]
    total = rows + outgoing.shape[0] * outgoing.shape[1]
    return pl.pallas_call(
        functools.partial(_halo_kernel, offsets),
        out_shape=jax.ShapeDtypeStruct((total, own_rows.shape[1]), own_rows.dtype),
        in_specs=[pl.BlockSpec(memory_space=pltpu.VMEM)] * 2,
        out_specs=pl.BlockSpec(memory_space=pltpu.VMEM),
        scratch_shapes=[pltpu.SemaphoreType.DMA((len(offsets),))] * 4,
        compiler_params=pltpu.CompilerParams(collective_id=1, has_side_effects=True),
    )(own_rows, outgoing)


def _sibling_kernel(x_ref, o_ref, inbox, send_sem, recv_sem):
    sibling = 1 - lax.axis_index("head")
    mesh_ids = pl.DeviceIdType.MESH
    barrier = pltpu.get_barrier_semaphore()
    pl.semaphore_signal(barrier, 1, device_id={"head": sibling}, device_id_type=mesh_ids)
    pl.semaphore_wait(barrier, 1)
    copy = pltpu.make_async_remote_copy(
        src_ref=x_ref,
        dst_ref=inbox,
        send_sem=send_sem,
        recv_sem=recv_sem,
        device_id={"head": sibling},
        device_id_type=mesh_ids,
    )
    copy.start()
    copy.wait()
    o_ref[...] = x_ref[...] + inbox[...]


def sibling_sum(x, collective_id):
    return pl.pallas_call(
        _sibling_kernel,
        out_shape=jax.ShapeDtypeStruct(x.shape, x.dtype),
        in_specs=[pl.BlockSpec(memory_space=pltpu.VMEM)],
        out_specs=pl.BlockSpec(memory_space=pltpu.VMEM),
        scratch_shapes=[
            pltpu.VMEM(x.shape, x.dtype),
            pltpu.SemaphoreType.DMA(()),
            pltpu.SemaphoreType.DMA(()),
        ],
        compiler_params=pltpu.CompilerParams(
            collective_id=collective_id, has_side_effects=True
        ),
    )(x)


def _silu(values):
    return values * (1.0 / (1.0 + jnp.exp(-values)))


def _fold_pick(table_ref, ids, fold):
    chunk = ids.shape[0]
    groups = table_ref.shape[0]
    width = table_ref.shape[1] // fold
    shift = fold.bit_length() - 1
    hot = (
        lax.shift_right_logical(ids, shift) == lax.broadcasted_iota(jnp.int32, (chunk, groups), 1)
    ).astype(jnp.bfloat16)
    picked = jnp.dot(hot, table_ref[...], preferred_element_type=jnp.float32)
    lane = jnp.bitwise_and(ids, fold - 1)
    rows = picked[:, :width]
    for j in range(1, fold):
        rows = jnp.where(lane == j, picked[:, j * width : (j + 1) * width], rows)
    return rows.astype(jnp.bfloat16)


def _edge_kernel(fold, scalars, edge_ref, src_ref, dst_ref, dst_row_ref, ext_ref, own_ref,
                 alpha_ref, beta_ref, gamma_ref, gain_ref, out_ref):
    step = pl.program_id(0)
    chunk, width = edge_ref.shape

    @pl.when(step == 0)
    def _():
        out_ref[...] = jnp.zeros_like(out_ref)

    edge = edge_ref[...]
    dst = dst_ref[...]
    sender = _fold_pick(ext_ref, src_ref[...], fold)
    receiver = _fold_pick(own_ref, dst, fold)
    pre = jnp.dot(edge, alpha_ref[0:width], preferred_element_type=jnp.float32)
    pre = pre + jnp.dot(sender, alpha_ref[width : 2 * width], preferred_element_type=jnp.float32)
    pre = pre + jnp.dot(receiver, alpha_ref[2 * width :], preferred_element_type=jnp.float32)
    first = _silu(pre).astype(jnp.bfloat16)
    second = _silu(jnp.dot(first, beta_ref[...], preferred_element_type=jnp.float32)).astype(
        jnp.bfloat16
    )
    third = jnp.dot(second, gamma_ref[...], preferred_element_type=jnp.float32)
    row_mean = jnp.mean(third, axis=-1, keepdims=True)
    centred = third - row_mean
    row_var = jnp.mean(centred * centred, axis=-1, keepdims=True)
    normed = centred * lax.rsqrt(row_var + 1e-05) * gain_ref[...]
    edge_new = (edge.astype(jnp.float32) + normed).astype(jnp.bfloat16)
    position = scalars[1] + step * chunk + lax.broadcasted_iota(jnp.int32, (chunk, 1), 0)
    live = position < scalars[2]
    messages = jnp.where(live, edge_new, jnp.zeros_like(edge_new))
    lane = jnp.bitwise_and(dst, fold - 1)
    spread = jnp.concatenate(
        [jnp.where(lane == j, messages, jnp.zeros_like(messages)) for j in range(fold)], axis=1
    )
    groups = out_ref.shape[0]
    shift = fold.bit_length() - 1
    hot_t = (
        lax.broadcasted_iota(jnp.int32, (groups, chunk), 0)
        == lax.shift_right_logical(dst_row_ref[0], shift)
    ).astype(jnp.bfloat16)
    out_ref[...] += jnp.dot(hot_t, spread, preferred_element_type=jnp.float32)


def edge_messages(edges, send_ids, recv_ids, extended, own_rows, alpha, beta, gamma, gain,
                  first_row, share, tally, chunk=1024, fold=FOLD):
    slots, width = edges.shape
    nodes = own_rows.shape[0]
    turns = share // chunk
    scalars = jnp.stack([first_row // chunk, first_row, tally]).astype(jnp.int32)
    send_ids = lax.dynamic_slice_in_dim(send_ids, first_row, share, 0)
    recv_ids = lax.dynamic_slice_in_dim(recv_ids, first_row, share, 0)
    ext_wide = extended.reshape(extended.shape[0] // fold, fold * width)
    own_wide = own_rows.reshape(nodes // fold, fold * width)
    full = lambda shape: pl.BlockSpec(shape, lambda i, s: (0,) * len(shape))
    grid_spec = pltpu.PrefetchScalarGridSpec(
        num_scalar_prefetch=1,
        grid=(turns,),
        in_specs=[
            pl.BlockSpec((chunk, width), lambda i, s: (s[0] + i, 0)),
            pl.BlockSpec((chunk, 1), lambda i, s: (i, 0)),
            pl.BlockSpec((chunk, 1), lambda i, s: (i, 0)),
            pl.BlockSpec((1, 1, chunk), lambda i, s: (i, 0, 0)),
            full(ext_wide.shape),
            full(own_wide.shape),
            full(alpha.shape),
            full(beta.shape),
            full(gamma.shape),
            full((1, width)),
        ],
        out_specs=full((nodes // fold, fold * width)),
    )
    total = pl.pallas_call(
        functools.partial(_edge_kernel, fold),
        out_shape=jax.ShapeDtypeStruct((nodes // fold, fold * width), jnp.float32),
        grid_spec=grid_spec,
    )(
        scalars,
        edges,
        send_ids.reshape(share, 1),
        recv_ids.reshape(share, 1),
        recv_ids.reshape(turns, 1, chunk),
        ext_wide,
        own_wide,
        alpha,
        beta,
        gamma,
        gain.reshape(1, width).astype(jnp.float32),
    )
    return total.reshape(nodes, width)


def psum_slices(numer, denom):
    joined = jnp.concatenate([numer.reshape(-1), denom.reshape(-1)])
    rows = -(-joined.shape[0] // 1024) * 8
    padded = jnp.zeros((rows * 128,), joined.dtype).at[: joined.shape[0]].set(joined)
    total = dom_sum(padded.reshape(rows, 128)).reshape(-1)
    numer_size = numer.size
    return (
        total[:numer_size].reshape(numer.shape),
        total[numer_size : numer_size + denom.size].reshape(denom.shape),
    )


def layer_norm(values, gain_row):
    row_mean = jnp.mean(values, axis=-1, keepdims=True)
    centred = values - row_mean
    row_var = jnp.mean(centred * centred, axis=-1, keepdims=True)
    return centred * lax.rsqrt(row_var + 1e-05) * gain_row


def node_section(
    own_rows,
    summed_b,
    vertex_layer_alpha,
    vertex_layer_beta,
    vertex_layer_gamma,
    vertex_scale_factor,
):
    feature_width = own_rows.shape[1]
    node_pre = jnp.dot(
        own_rows, vertex_layer_alpha[:feature_width], preferred_element_type=jnp.float32
    )
    node_pre = node_pre + jnp.dot(
        summed_b, vertex_layer_alpha[feature_width:], preferred_element_type=jnp.float32
    )
    node_one = jax.nn.silu(node_pre).astype(jnp.bfloat16)
    node_two = jax.nn.silu(
        jnp.dot(node_one, vertex_layer_beta, preferred_element_type=jnp.float32)
    ).astype(jnp.bfloat16)
    node_three = jnp.dot(node_two, vertex_layer_gamma, preferred_element_type=jnp.float32)
    return (own_rows.astype(jnp.float32) + layer_norm(node_three, vertex_scale_factor)).astype(
        jnp.bfloat16
    )


def slice_partial_terms(
    refreshed_vertices,
    focus_scale_factor,
    vertex_content_factor,
    cluster_affinity_factor,
    softness_level,
):
    count_of_rows = refreshed_vertices.shape[0]
    domain_channel_split = softness_level.shape[0]
    standardised_entries = layer_norm(
        refreshed_vertices.astype(jnp.float32), focus_scale_factor
    ).astype(jnp.bfloat16)
    values = jnp.dot(
        standardised_entries, vertex_content_factor, preferred_element_type=jnp.float32
    ).astype(jnp.bfloat16)
    cluster_affinities = jnp.dot(
        standardised_entries, cluster_affinity_factor, preferred_element_type=jnp.float32
    )
    cluster_affinities = (
        cluster_affinities.reshape(count_of_rows, domain_channel_split, GROUPS_PER_LANE)
        / softness_level[None, :, None]
    )
    weights = jax.nn.softmax(cluster_affinities, axis=-1)
    weights_b = weights.astype(jnp.bfloat16)
    numer = jnp.einsum(
        "nhs,nhc->hsc",
        weights_b,
        values.reshape(count_of_rows, domain_channel_split, HEAD_DIM),
        preferred_element_type=jnp.float32,
    )
    denom = jnp.sum(weights, axis=0)
    return (weights_b, numer, denom)


def slice_mixing(numer, denom, cluster_probe_lookup, cluster_content_linear):
    tokens = numer / denom[:, :, None]
    highest = lax.Precision.HIGHEST
    query = jnp.einsum("hsc,hcd->hsd", tokens, cluster_probe_lookup[0], precision=highest)
    keys = jnp.einsum("hsc,hcd->hsd", tokens, cluster_probe_lookup[1], precision=highest)
    carried = jnp.einsum("hsc,hcd->hsd", tokens, cluster_content_linear, precision=highest)
    scores = jnp.einsum("hsd,htd->hst", query, keys, precision=highest) / math.sqrt(HEAD_DIM)
    mixing = jax.nn.softmax(scores, axis=-1)
    return jnp.einsum("hst,htd->hsd", mixing, carried, precision=highest).astype(jnp.bfloat16)


def attend_rows(weights_b, slice_out):
    count_of_rows = weights_b.shape[0]
    domain_channel_split = weights_b.shape[1]
    attended = jnp.einsum("nhs,hsd->nhd", weights_b, slice_out, preferred_element_type=jnp.float32)
    return attended.reshape(count_of_rows, domain_channel_split * HEAD_DIM).astype(jnp.bfloat16)


def pick_rows(table, row_ids):
    table_ids = jnp.arange(table.shape[0], dtype=jnp.int32)
    selector = (row_ids[:, None] == table_ids[None, :]).astype(jnp.bfloat16)
    return jnp.dot(selector, table, preferred_element_type=jnp.float32).astype(jnp.bfloat16)


def gather_rows(table, row_ids, fold):
    count, width = table.shape
    wide = table.reshape(count // fold, fold * width)
    hot = (row_ids[:, None] // fold == jnp.arange(count // fold, dtype=jnp.int32)[None, :]).astype(
        jnp.bfloat16
    )
    picked = jnp.dot(hot, wide, preferred_element_type=jnp.float32)
    lane = row_ids % fold
    rows = picked[:, :width]
    for j in range(1, fold):
        rows = jnp.where((lane == j)[:, None], picked[:, j * width : (j + 1) * width], rows)
    return rows.astype(jnp.bfloat16)


def scatter_rows(messages, row_ids, count, fold):
    width = messages.shape[1]
    lane = row_ids % fold
    spread = jnp.concatenate(
        [jnp.where((lane == j)[:, None], messages, jnp.zeros_like(messages)) for j in range(fold)],
        axis=1,
    )
    hot = (row_ids[:, None] // fold == jnp.arange(count // fold, dtype=jnp.int32)[None, :]).astype(
        jnp.bfloat16
    )
    total = lax.dot_general(
        hot, spread, (((0,), (0,)), ((), ())), preferred_element_type=jnp.float32
    )
    return total.reshape(count, width)


def body(
    vertex_state,
    link_state_slotted,
    source_vertex_ids,
    target_vertex_ids,
    active_link_tally,
    halo_outgoing_ids,
    link_layer_alpha,
    link_layer_beta,
    link_layer_gamma,
    link_scale_factor,
    vertex_layer_alpha,
    vertex_layer_beta,
    vertex_layer_gamma,
    vertex_scale_factor,
    focus_scale_factor,
    vertex_content_factor,
    cluster_affinity_factor,
    softness_level,
    cluster_probe_lookup,
    cluster_content_linear,
    closing_linear_factor,
):
    node_count = vertex_state.shape[0]
    feature_width = vertex_state.shape[1]
    capacity = link_state_slotted.shape[0]
    offsets = (1, -1, 2, -2)
    outgoing = pick_rows(vertex_state, halo_outgoing_ids[0].reshape(-1))
    extended = exchange_halos(
        vertex_state, outgoing.reshape(halo_outgoing_ids.shape[1:] + (feature_width,)), offsets
    )
    share = capacity // lax.axis_size("head")
    first_row = lax.axis_index("head") * share
    total = edge_messages(
        link_state_slotted,
        source_vertex_ids,
        target_vertex_ids,
        extended,
        vertex_state,
        link_layer_alpha,
        link_layer_beta,
        link_layer_gamma,
        link_scale_factor,
        first_row,
        share,
        active_link_tally[0],
    )
    summed = sibling_sum(total, 2)
    refreshed_vertices = node_section(
        vertex_state,
        summed.astype(jnp.bfloat16),
        vertex_layer_alpha,
        vertex_layer_beta,
        vertex_layer_gamma,
        vertex_scale_factor,
    )
    weights_b, numer, denom = slice_partial_terms(
        refreshed_vertices,
        focus_scale_factor,
        vertex_content_factor,
        cluster_affinity_factor,
        softness_level,
    )
    numer, denom = psum_slices(numer, denom)
    slice_out = slice_mixing(numer, denom, cluster_probe_lookup, cluster_content_linear)
    attended = attend_rows(weights_b, slice_out)
    projected = sibling_sum(
        jnp.dot(attended, closing_linear_factor, preferred_element_type=jnp.float32), 3
    )
    return (refreshed_vertices.astype(jnp.float32) + projected).astype(jnp.bfloat16)


def solution(mesh):
    in_specs = (
        P("dom", None),
        P("dom", None),
        P("dom"),
        P("dom"),
        P("dom"),
        P("dom", None, None),
        P(),
        P(),
        P(),
        P(),
        P(),
        P(),
        P(),
        P(),
        P(),
        P(None, "head"),
        P(None, "head"),
        P("head"),
        P(None, "head", None, None),
        P("head", None, None),
        P("head", None),
    )
    out_specs = P("dom", None)
    return jax.shard_map(body, mesh=mesh, in_specs=in_specs, out_specs=out_specs, check_vma=False)
```

```python
import functools
import math

import jax
import jax.numpy as jnp
from jax import lax
from jax.experimental import pallas as pl
from jax.experimental.pallas import tpu as pltpu
from jax.sharding import PartitionSpec as P

HEAD_DIM = 16
GROUPS_PER_LANE = 64
FOLD = 4


def passed_along(value, axis, steps):
    count = lax.axis_size(axis)
    first, last = (max(0, -steps), min(count, count - steps))
    return lax.ppermute(value, axis, [(source, source + steps) for source in range(first, last)])


def _radix_kernel(radix, steps, x_ref, o_ref, inbox, send_sem, recv_sem):
    me = lax.axis_index("dom")
    spans = [radix**s for s in range(steps)]
    digits = [(me // span) % radix for span in spans]
    partners = [
        [me + ((digit + j) % radix - digit) * span for j in range(1, radix)]
        for digit, span in zip(digits, spans)
    ]
    barrier = pltpu.get_barrier_semaphore()
    for group in partners:
        for partner in group:
            pl.semaphore_signal(
                barrier, 1, device_id={"dom": partner}, device_id_type=pl.DeviceIdType.MESH
            )
    pl.semaphore_wait(barrier, steps * (radix - 1))
    for s in range(steps):
        source = x_ref if s == 0 else o_ref
        copies = []
        for j, partner in enumerate(partners[s]):
            copy = pltpu.make_async_remote_copy(
                src_ref=source,
                dst_ref=inbox.at[s, digits[s]],
                send_sem=send_sem.at[s, j],
                recv_sem=recv_sem.at[s, digits[s]],
                device_id={"dom": partner},
                device_id_type=pl.DeviceIdType.MESH,
            )
            copy.start()
            copies.append(copy)
        inbox[s, digits[s]] = source[...]
        for copy in copies:
            copy.wait_send()
        for j, partner in enumerate(partners[s]):
            slot = (digits[s] + j + 1) % radix
            pltpu.make_async_remote_copy(
                src_ref=source,
                dst_ref=inbox.at[s, slot],
                send_sem=send_sem.at[s, j],
                recv_sem=recv_sem.at[s, slot],
                device_id={"dom": partner},
                device_id_type=pl.DeviceIdType.MESH,
            ).wait_recv()
        total = inbox[s, 0]
        for d in range(1, radix):
            total = total + inbox[s, d]
        o_ref[...] = total


def dom_sum(flat):
    count = lax.axis_size("dom")
    radix = 4
    steps = 0
    while radix ** (steps + 1) <= count:
        steps += 1
    assert radix**steps == count
    return pl.pallas_call(
        functools.partial(_radix_kernel, radix, steps),
        out_shape=jax.ShapeDtypeStruct(flat.shape, flat.dtype),
        in_specs=[pl.BlockSpec(memory_space=pltpu.VMEM)],
        out_specs=pl.BlockSpec(memory_space=pltpu.VMEM),
        scratch_shapes=[
            pltpu.VMEM((steps, radix) + flat.shape, flat.dtype),
            pltpu.SemaphoreType.DMA((steps, radix - 1)),
            pltpu.SemaphoreType.DMA((steps, radix)),
        ],
        compiler_params=pltpu.CompilerParams(collective_id=0, has_side_effects=True),
    )(flat)


def _halo_kernel(offsets, own_ref, out_ref, ext_ref, send_sem, recv_sem, pass_sem, land_sem):
    me = lax.axis_index("dom")
    count = lax.axis_size("dom")
    core = lax.axis_index("head")
    sibling = 1 - core
    rows = own_ref.shape[0]
    halo = out_ref.shape[1]
    half = halo // 2
    mesh_ids = pl.DeviceIdType.MESH
    barrier = pltpu.get_barrier_semaphore()
    for offset in offsets:
        pl.semaphore_signal(
            barrier, 1, device_id={"dom": (me + offset + count) % count}, device_id_type=mesh_ids
        )
    pl.semaphore_signal(barrier, 1, device_id={"head": sibling}, device_id_type=mesh_ids)
    pl.semaphore_wait(barrier, len(offsets) + 1)
    sends = []
    for k, offset in enumerate(offsets):
        copy = pltpu.make_async_remote_copy(
            src_ref=out_ref.at[k, pl.ds(core * half, half)],
            dst_ref=ext_ref.at[pl.ds(rows + k * halo + core * half, half)],
            send_sem=send_sem.at[k],
            recv_sem=recv_sem.at[k],
            device_id={"dom": (me + offset + count) % count},
            device_id_type=mesh_ids,
        )
        copy.start()
        sends.append(copy)
    ext_ref[pl.ds(0, rows)] = own_ref[...]
    passes = []
    for k in range(len(offsets)):
        sends[k].wait_recv()
        forward = pltpu.make_async_remote_copy(
            src_ref=ext_ref.at[pl.ds(rows + k * halo + core * half, half)],
            dst_ref=ext_ref.at[pl.ds(rows + k * halo + core * half, half)],
            send_sem=pass_sem.at[k],
            recv_sem=land_sem.at[k],
            device_id={"head": sibling},
            device_id_type=mesh_ids,
        )
        forward.start()
        passes.append(forward)
    for copy in sends:
        copy.wait_send()
    for forward in passes:
        forward.wait()
    for k, offset in enumerate(offsets):
        if offset > 0:
            inside = (me + count - offset) // count
        else:
            inside = (2 * count - 1 + offset - me) // count
        slot = pl.ds(rows + k * halo, halo)
        ext_ref[slot] = ext_ref[slot] * inside.astype(ext_ref.dtype)


def exchange_halos(own_rows, outgoing, offsets):
    rows = own_rows.shape[0]
    total = rows + outgoing.shape[0] * outgoing.shape[1]
    return pl.pallas_call(
        functools.partial(_halo_kernel, offsets),
        out_shape=jax.ShapeDtypeStruct((total, own_rows.shape[1]), own_rows.dtype),
        in_specs=[pl.BlockSpec(memory_space=pltpu.VMEM)] * 2,
        out_specs=pl.BlockSpec(memory_space=pltpu.VMEM),
        scratch_shapes=[pltpu.SemaphoreType.DMA((len(offsets),))] * 4,
        compiler_params=pltpu.CompilerParams(collective_id=1, has_side_effects=True),
    )(own_rows, outgoing)


def _sibling_kernel(x_ref, o_ref, inbox, send_sem, recv_sem):
    sibling = 1 - lax.axis_index("head")
    mesh_ids = pl.DeviceIdType.MESH
    barrier = pltpu.get_barrier_semaphore()
    pl.semaphore_signal(barrier, 1, device_id={"head": sibling}, device_id_type=mesh_ids)
    pl.semaphore_wait(barrier, 1)
    copy = pltpu.make_async_remote_copy(
        src_ref=x_ref,
        dst_ref=inbox,
        send_sem=send_sem,
        recv_sem=recv_sem,
        device_id={"head": sibling},
        device_id_type=mesh_ids,
    )
    copy.start()
    copy.wait()
    o_ref[...] = x_ref[...].astype(o_ref.dtype) + inbox[...].astype(o_ref.dtype)


def sibling_sum(x, collective_id):
    return pl.pallas_call(
        _sibling_kernel,
        out_shape=jax.ShapeDtypeStruct(x.shape, jnp.float32),
        in_specs=[pl.BlockSpec(memory_space=pltpu.VMEM)],
        out_specs=pl.BlockSpec(memory_space=pltpu.VMEM),
        scratch_shapes=[
            pltpu.VMEM(x.shape, x.dtype),
            pltpu.SemaphoreType.DMA(()),
            pltpu.SemaphoreType.DMA(()),
        ],
        compiler_params=pltpu.CompilerParams(
            collective_id=collective_id, has_side_effects=True
        ),
    )(x)


def _silu(values):
    return values * (1.0 / (1.0 + jnp.exp(-values)))


def _fold_pick(table_ref, ids, fold):
    chunk = ids.shape[0]
    groups = table_ref.shape[0]
    width = table_ref.shape[1] // fold
    shift = fold.bit_length() - 1
    hot = (
        lax.shift_right_logical(ids, shift) == lax.broadcasted_iota(jnp.int32, (chunk, groups), 1)
    ).astype(jnp.bfloat16)
    picked = jnp.dot(hot, table_ref[...], preferred_element_type=jnp.float32)
    lane = jnp.bitwise_and(ids, fold - 1)
    rows = picked[:, :width]
    for j in range(1, fold):
        rows = jnp.where(lane == j, picked[:, j * width : (j + 1) * width], rows)
    return rows.astype(jnp.bfloat16)


def _edge_kernel(fold, scalars, edge_ref, src_ref, dst_ref, dst_row_ref, ext_ref, own_ref,
                 alpha_ref, beta_ref, gamma_ref, gain_ref, out_ref):
    step = pl.program_id(0)
    chunk, width = edge_ref.shape

    @pl.when(step == 0)
    def _():
        out_ref[...] = jnp.zeros_like(out_ref)

    edge = edge_ref[...]
    dst = dst_ref[...]
    sender = _fold_pick(ext_ref, src_ref[...], fold)
    receiver = _fold_pick(own_ref, dst, fold)
    pre = jnp.dot(edge, alpha_ref[0:width], preferred_element_type=jnp.float32)
    pre = pre + jnp.dot(sender, alpha_ref[width : 2 * width], preferred_element_type=jnp.float32)
    pre = pre + jnp.dot(receiver, alpha_ref[2 * width :], preferred_element_type=jnp.float32)
    first = _silu(pre).astype(jnp.bfloat16)
    second = _silu(jnp.dot(first, beta_ref[...], preferred_element_type=jnp.float32)).astype(
        jnp.bfloat16
    )
    third = jnp.dot(second, gamma_ref[...], preferred_element_type=jnp.float32)
    row_mean = jnp.mean(third, axis=-1, keepdims=True)
    centred = third - row_mean
    row_var = jnp.mean(centred * centred, axis=-1, keepdims=True)
    normed = centred * lax.rsqrt(row_var + 1e-05) * gain_ref[...]
    edge_new = (edge.astype(jnp.float32) + normed).astype(jnp.bfloat16)
    position = scalars[1] + step * chunk + lax.broadcasted_iota(jnp.int32, (chunk, 1), 0)
    live = position < scalars[2]
    messages = jnp.where(live, edge_new, jnp.zeros_like(edge_new))
    lane = jnp.bitwise_and(dst, fold - 1)
    spread = jnp.concatenate(
        [jnp.where(lane == j, messages, jnp.zeros_like(messages)) for j in range(fold)], axis=1
    )
    groups = out_ref.shape[0]
    shift = fold.bit_length() - 1
    hot_t = (
        lax.broadcasted_iota(jnp.int32, (groups, chunk), 0)
        == lax.shift_right_logical(dst_row_ref[0], shift)
    ).astype(jnp.bfloat16)
    out_ref[...] += jnp.dot(hot_t, spread, preferred_element_type=jnp.float32)


def edge_messages(edges, send_ids, recv_ids, extended, own_rows, alpha, beta, gamma, gain,
                  first_row, share, tally, chunk=1024, fold=FOLD):
    slots, width = edges.shape
    nodes = own_rows.shape[0]
    turns = share // chunk
    scalars = jnp.stack([first_row // chunk, first_row, tally]).astype(jnp.int32)
    send_ids = lax.dynamic_slice_in_dim(send_ids, first_row, share, 0)
    recv_ids = lax.dynamic_slice_in_dim(recv_ids, first_row, share, 0)
    ext_wide = extended.reshape(extended.shape[0] // fold, fold * width)
    own_wide = own_rows.reshape(nodes // fold, fold * width)
    full = lambda shape: pl.BlockSpec(shape, lambda i, s: (0,) * len(shape))
    grid_spec = pltpu.PrefetchScalarGridSpec(
        num_scalar_prefetch=1,
        grid=(turns,),
        in_specs=[
            pl.BlockSpec((chunk, width), lambda i, s: (s[0] + i, 0)),
            pl.BlockSpec((chunk, 1), lambda i, s: (i, 0)),
            pl.BlockSpec((chunk, 1), lambda i, s: (i, 0)),
            pl.BlockSpec((1, 1, chunk), lambda i, s: (i, 0, 0)),
            full(ext_wide.shape),
            full(own_wide.shape),
            full(alpha.shape),
            full(beta.shape),
            full(gamma.shape),
            full((1, width)),
        ],
        out_specs=full((nodes // fold, fold * width)),
    )
    total = pl.pallas_call(
        functools.partial(_edge_kernel, fold),
        out_shape=jax.ShapeDtypeStruct((nodes // fold, fold * width), jnp.float32),
        grid_spec=grid_spec,
    )(
        scalars,
        edges,
        send_ids.reshape(share, 1),
        recv_ids.reshape(share, 1),
        recv_ids.reshape(turns, 1, chunk),
        ext_wide,
        own_wide,
        alpha,
        beta,
        gamma,
        gain.reshape(1, width).astype(jnp.float32),
    )
    return total.reshape(nodes, width)


def psum_slices(numer, denom):
    joined = jnp.concatenate([numer.reshape(-1), denom.reshape(-1)])
    rows = -(-joined.shape[0] // 1024) * 8
    padded = jnp.zeros((rows * 128,), joined.dtype).at[: joined.shape[0]].set(joined)
    total = dom_sum(padded.reshape(rows, 128)).reshape(-1)
    numer_size = numer.size
    return (
        total[:numer_size].reshape(numer.shape),
        total[numer_size : numer_size + denom.size].reshape(denom.shape),
    )


def layer_norm(values, gain_row):
    row_mean = jnp.mean(values, axis=-1, keepdims=True)
    centred = values - row_mean
    row_var = jnp.mean(centred * centred, axis=-1, keepdims=True)
    return centred * lax.rsqrt(row_var + 1e-05) * gain_row


def node_section(
    own_rows,
    summed_b,
    vertex_layer_alpha,
    vertex_layer_beta,
    vertex_layer_gamma,
    vertex_scale_factor,
):
    feature_width = own_rows.shape[1]
    node_pre = jnp.dot(
        own_rows, vertex_layer_alpha[:feature_width], preferred_element_type=jnp.float32
    )
    node_pre = node_pre + jnp.dot(
        summed_b, vertex_layer_alpha[feature_width:], preferred_element_type=jnp.float32
    )
    node_one = jax.nn.silu(node_pre).astype(jnp.bfloat16)
    node_two = jax.nn.silu(
        jnp.dot(node_one, vertex_layer_beta, preferred_element_type=jnp.float32)
    ).astype(jnp.bfloat16)
    node_three = jnp.dot(node_two, vertex_layer_gamma, preferred_element_type=jnp.float32)
    return (own_rows.astype(jnp.float32) + layer_norm(node_three, vertex_scale_factor)).astype(
        jnp.bfloat16
    )


def slice_partial_terms(
    refreshed_vertices,
    focus_scale_factor,
    vertex_content_factor,
    cluster_affinity_factor,
    softness_level,
):
    count_of_rows = refreshed_vertices.shape[0]
    domain_channel_split = softness_level.shape[0]
    standardised_entries = layer_norm(
        refreshed_vertices.astype(jnp.float32), focus_scale_factor
    ).astype(jnp.bfloat16)
    values = jnp.dot(
        standardised_entries, vertex_content_factor, preferred_element_type=jnp.float32
    ).astype(jnp.bfloat16)
    cluster_affinities = jnp.dot(
        standardised_entries, cluster_affinity_factor, preferred_element_type=jnp.float32
    )
    cluster_affinities = (
        cluster_affinities.reshape(count_of_rows, domain_channel_split, GROUPS_PER_LANE)
        / softness_level[None, :, None]
    )
    weights = jax.nn.softmax(cluster_affinities, axis=-1)
    weights_b = weights.astype(jnp.bfloat16)
    numer = jnp.einsum(
        "nhs,nhc->hsc",
        weights_b,
        values.reshape(count_of_rows, domain_channel_split, HEAD_DIM),
        preferred_element_type=jnp.float32,
    )
    denom = jnp.sum(weights, axis=0)
    return (weights_b, numer, denom)


def slice_mixing(numer, denom, cluster_probe_lookup, cluster_content_linear):
    tokens = numer / denom[:, :, None]
    highest = lax.Precision.HIGHEST
    query = jnp.einsum("hsc,hcd->hsd", tokens, cluster_probe_lookup[0], precision=highest)
    keys = jnp.einsum("hsc,hcd->hsd", tokens, cluster_probe_lookup[1], precision=highest)
    carried = jnp.einsum("hsc,hcd->hsd", tokens, cluster_content_linear, precision=highest)
    scores = jnp.einsum("hsd,htd->hst", query, keys, precision=highest) / math.sqrt(HEAD_DIM)
    mixing = jax.nn.softmax(scores, axis=-1)
    return jnp.einsum("hst,htd->hsd", mixing, carried, precision=highest).astype(jnp.bfloat16)


def attend_rows(weights_b, slice_out):
    count_of_rows = weights_b.shape[0]
    domain_channel_split = weights_b.shape[1]
    attended = jnp.einsum("nhs,hsd->nhd", weights_b, slice_out, preferred_element_type=jnp.float32)
    return attended.reshape(count_of_rows, domain_channel_split * HEAD_DIM).astype(jnp.bfloat16)


def pick_rows(table, row_ids):
    table_ids = jnp.arange(table.shape[0], dtype=jnp.int32)
    selector = (row_ids[:, None] == table_ids[None, :]).astype(jnp.bfloat16)
    return jnp.dot(selector, table, preferred_element_type=jnp.float32).astype(jnp.bfloat16)


def gather_rows(table, row_ids, fold):
    count, width = table.shape
    wide = table.reshape(count // fold, fold * width)
    hot = (row_ids[:, None] // fold == jnp.arange(count // fold, dtype=jnp.int32)[None, :]).astype(
        jnp.bfloat16
    )
    picked = jnp.dot(hot, wide, preferred_element_type=jnp.float32)
    lane = row_ids % fold
    rows = picked[:, :width]
    for j in range(1, fold):
        rows = jnp.where((lane == j)[:, None], picked[:, j * width : (j + 1) * width], rows)
    return rows.astype(jnp.bfloat16)


def scatter_rows(messages, row_ids, count, fold):
    width = messages.shape[1]
    lane = row_ids % fold
    spread = jnp.concatenate(
        [jnp.where((lane == j)[:, None], messages, jnp.zeros_like(messages)) for j in range(fold)],
        axis=1,
    )
    hot = (row_ids[:, None] // fold == jnp.arange(count // fold, dtype=jnp.int32)[None, :]).astype(
        jnp.bfloat16
    )
    total = lax.dot_general(
        hot, spread, (((0,), (0,)), ((), ())), preferred_element_type=jnp.float32
    )
    return total.reshape(count, width)


def body(
    vertex_state,
    link_state_slotted,
    source_vertex_ids,
    target_vertex_ids,
    active_link_tally,
    halo_outgoing_ids,
    link_layer_alpha,
    link_layer_beta,
    link_layer_gamma,
    link_scale_factor,
    vertex_layer_alpha,
    vertex_layer_beta,
    vertex_layer_gamma,
    vertex_scale_factor,
    focus_scale_factor,
    vertex_content_factor,
    cluster_affinity_factor,
    softness_level,
    cluster_probe_lookup,
    cluster_content_linear,
    closing_linear_factor,
):
    node_count = vertex_state.shape[0]
    feature_width = vertex_state.shape[1]
    capacity = link_state_slotted.shape[0]
    offsets = (1, -1, 2, -2)
    outgoing = pick_rows(vertex_state, halo_outgoing_ids[0].reshape(-1))
    extended = exchange_halos(
        vertex_state, outgoing.reshape(halo_outgoing_ids.shape[1:] + (feature_width,)), offsets
    )
    share = capacity // lax.axis_size("head")
    first_row = lax.axis_index("head") * share
    total = edge_messages(
        link_state_slotted,
        source_vertex_ids,
        target_vertex_ids,
        extended,
        vertex_state,
        link_layer_alpha,
        link_layer_beta,
        link_layer_gamma,
        link_scale_factor,
        first_row,
        share,
        active_link_tally[0],
    )
    summed = sibling_sum(total, 2)
    refreshed_vertices = node_section(
        vertex_state,
        summed.astype(jnp.bfloat16),
        vertex_layer_alpha,
        vertex_layer_beta,
        vertex_layer_gamma,
        vertex_scale_factor,
    )
    weights_b, numer, denom = slice_partial_terms(
        refreshed_vertices,
        focus_scale_factor,
        vertex_content_factor,
        cluster_affinity_factor,
        softness_level,
    )
    numer, denom = psum_slices(numer, denom)
    slice_out = slice_mixing(numer, denom, cluster_probe_lookup, cluster_content_linear)
    attended = attend_rows(weights_b, slice_out)
    projected = sibling_sum(
        jnp.dot(attended, closing_linear_factor, preferred_element_type=jnp.float32).astype(
            jnp.bfloat16
        ),
        3,
    )
    return (refreshed_vertices.astype(jnp.float32) + projected.astype(jnp.float32)).astype(
        jnp.bfloat16
    )


def solution(mesh):
    in_specs = (
        P("dom", None),
        P("dom", None),
        P("dom"),
        P("dom"),
        P("dom"),
        P("dom", None, None),
        P(),
        P(),
        P(),
        P(),
        P(),
        P(),
        P(),
        P(),
        P(),
        P(None, "head"),
        P(None, "head"),
        P("head"),
        P(None, "head", None, None),
        P("head", None, None),
        P("head", None),
    )
    out_specs = P("dom", None)
    return jax.shard_map(body, mesh=mesh, in_specs=in_specs, out_specs=out_specs, check_vma=False)
```

```python
import functools
import math

import jax
import jax.numpy as jnp
from jax import lax
from jax.experimental import pallas as pl
from jax.experimental.pallas import tpu as pltpu
from jax.sharding import PartitionSpec as P

HEAD_DIM = 16
GROUPS_PER_LANE = 64
FOLD = 4


def passed_along(value, axis, steps):
    count = lax.axis_size(axis)
    first, last = (max(0, -steps), min(count, count - steps))
    return lax.ppermute(value, axis, [(source, source + steps) for source in range(first, last)])


def _radix_kernel(radix, steps, x_ref, o_ref, inbox, send_sem, recv_sem):
    me = lax.axis_index("dom")
    spans = [radix**s for s in range(steps)]
    digits = [(me // span) % radix for span in spans]
    partners = [
        [me + ((digit + j) % radix - digit) * span for j in range(1, radix)]
        for digit, span in zip(digits, spans)
    ]
    barrier = pltpu.get_barrier_semaphore()
    for group in partners:
        for partner in group:
            pl.semaphore_signal(
                barrier, 1, device_id={"dom": partner}, device_id_type=pl.DeviceIdType.MESH
            )
    pl.semaphore_wait(barrier, steps * (radix - 1))
    for s in range(steps):
        source = x_ref if s == 0 else o_ref
        copies = []
        for j, partner in enumerate(partners[s]):
            copy = pltpu.make_async_remote_copy(
                src_ref=source,
                dst_ref=inbox.at[s, digits[s]],
                send_sem=send_sem.at[s, j],
                recv_sem=recv_sem.at[s, digits[s]],
                device_id={"dom": partner},
                device_id_type=pl.DeviceIdType.MESH,
            )
            copy.start()
            copies.append(copy)
        inbox[s, digits[s]] = source[...]
        for copy in copies:
            copy.wait_send()
        for j, partner in enumerate(partners[s]):
            slot = (digits[s] + j + 1) % radix
            pltpu.make_async_remote_copy(
                src_ref=source,
                dst_ref=inbox.at[s, slot],
                send_sem=send_sem.at[s, j],
                recv_sem=recv_sem.at[s, slot],
                device_id={"dom": partner},
                device_id_type=pl.DeviceIdType.MESH,
            ).wait_recv()
        total = inbox[s, 0]
        for d in range(1, radix):
            total = total + inbox[s, d]
        o_ref[...] = total


def dom_sum(flat):
    count = lax.axis_size("dom")
    radix = 4
    steps = 0
    while radix ** (steps + 1) <= count:
        steps += 1
    assert radix**steps == count
    return pl.pallas_call(
        functools.partial(_radix_kernel, radix, steps),
        out_shape=jax.ShapeDtypeStruct(flat.shape, flat.dtype),
        in_specs=[pl.BlockSpec(memory_space=pltpu.VMEM)],
        out_specs=pl.BlockSpec(memory_space=pltpu.VMEM),
        scratch_shapes=[
            pltpu.VMEM((steps, radix) + flat.shape, flat.dtype),
            pltpu.SemaphoreType.DMA((steps, radix - 1)),
            pltpu.SemaphoreType.DMA((steps, radix)),
        ],
        compiler_params=pltpu.CompilerParams(collective_id=0, has_side_effects=True),
    )(flat)


def _halo_kernel(offsets, own_ref, out_ref, ext_ref, send_sem, recv_sem, pass_sem, land_sem):
    me = lax.axis_index("dom")
    count = lax.axis_size("dom")
    core = lax.axis_index("head")
    sibling = 1 - core
    rows = own_ref.shape[0]
    halo = out_ref.shape[1]
    half = halo // 2
    mesh_ids = pl.DeviceIdType.MESH
    barrier = pltpu.get_barrier_semaphore()
    for offset in offsets:
        pl.semaphore_signal(
            barrier, 1, device_id={"dom": (me + offset + count) % count}, device_id_type=mesh_ids
        )
    pl.semaphore_signal(barrier, 1, device_id={"head": sibling}, device_id_type=mesh_ids)
    pl.semaphore_wait(barrier, len(offsets) + 1)
    sends = []
    for k, offset in enumerate(offsets):
        copy = pltpu.make_async_remote_copy(
            src_ref=out_ref.at[k, pl.ds(core * half, half)],
            dst_ref=ext_ref.at[pl.ds(rows + k * halo + core * half, half)],
            send_sem=send_sem.at[k],
            recv_sem=recv_sem.at[k],
            device_id={"dom": (me + offset + count) % count},
            device_id_type=mesh_ids,
        )
        copy.start()
        sends.append(copy)
    ext_ref[pl.ds(0, rows)] = own_ref[...]
    passes = []
    for k in range(len(offsets)):
        sends[k].wait_recv()
        forward = pltpu.make_async_remote_copy(
            src_ref=ext_ref.at[pl.ds(rows + k * halo + core * half, half)],
            dst_ref=ext_ref.at[pl.ds(rows + k * halo + core * half, half)],
            send_sem=pass_sem.at[k],
            recv_sem=land_sem.at[k],
            device_id={"head": sibling},
            device_id_type=mesh_ids,
        )
        forward.start()
        passes.append(forward)
    for copy in sends:
        copy.wait_send()
    for forward in passes:
        forward.wait()
    for k, offset in enumerate(offsets):
        if offset > 0:
            inside = (me + count - offset) // count
        else:
            inside = (2 * count - 1 + offset - me) // count
        slot = pl.ds(rows + k * halo, halo)
        ext_ref[slot] = ext_ref[slot] * inside.astype(ext_ref.dtype)


def exchange_halos(own_rows, outgoing, offsets):
    rows = own_rows.shape[0]
    total = rows + outgoing.shape[0] * outgoing.shape[1]
    return pl.pallas_call(
        functools.partial(_halo_kernel, offsets),
        out_shape=jax.ShapeDtypeStruct((total, own_rows.shape[1]), own_rows.dtype),
        in_specs=[pl.BlockSpec(memory_space=pltpu.VMEM)] * 2,
        out_specs=pl.BlockSpec(memory_space=pltpu.VMEM),
        scratch_shapes=[pltpu.SemaphoreType.DMA((len(offsets),))] * 4,
        compiler_params=pltpu.CompilerParams(collective_id=1, has_side_effects=True),
    )(own_rows, outgoing)


def _sibling_kernel(x_ref, o_ref, inbox, send_sem, recv_sem):
    sibling = 1 - lax.axis_index("head")
    mesh_ids = pl.DeviceIdType.MESH
    barrier = pltpu.get_barrier_semaphore()
    pl.semaphore_signal(barrier, 1, device_id={"head": sibling}, device_id_type=mesh_ids)
    pl.semaphore_wait(barrier, 1)
    copy = pltpu.make_async_remote_copy(
        src_ref=x_ref,
        dst_ref=inbox,
        send_sem=send_sem,
        recv_sem=recv_sem,
        device_id={"head": sibling},
        device_id_type=mesh_ids,
    )
    copy.start()
    copy.wait()
    o_ref[...] = x_ref[...].astype(o_ref.dtype) + inbox[...].astype(o_ref.dtype)


def sibling_sum(x, collective_id):
    return pl.pallas_call(
        _sibling_kernel,
        out_shape=jax.ShapeDtypeStruct(x.shape, jnp.float32),
        in_specs=[pl.BlockSpec(memory_space=pltpu.VMEM)],
        out_specs=pl.BlockSpec(memory_space=pltpu.VMEM),
        scratch_shapes=[
            pltpu.VMEM(x.shape, x.dtype),
            pltpu.SemaphoreType.DMA(()),
            pltpu.SemaphoreType.DMA(()),
        ],
        compiler_params=pltpu.CompilerParams(
            collective_id=collective_id, has_side_effects=True
        ),
    )(x)


def _silu(values):
    return values * (1.0 / (1.0 + jnp.exp(-values)))


def _fold_pick(table_ref, ids, fold):
    chunk = ids.shape[0]
    groups = table_ref.shape[0]
    width = table_ref.shape[1] // fold
    shift = fold.bit_length() - 1
    hot = (
        lax.shift_right_logical(ids, shift) == lax.broadcasted_iota(jnp.int32, (chunk, groups), 1)
    ).astype(jnp.bfloat16)
    picked = jnp.dot(hot, table_ref[...], preferred_element_type=jnp.float32)
    lane = jnp.bitwise_and(ids, fold - 1)
    rows = picked[:, :width]
    for j in range(1, fold):
        rows = jnp.where(lane == j, picked[:, j * width : (j + 1) * width], rows)
    return rows.astype(jnp.bfloat16)


def _edge_kernel(fold, scalars, edge_ref, src_ref, dst_ref, dst_row_ref, ext_ref, own_ref,
                 alpha_ref, beta_ref, gamma_ref, gain_ref, out_ref):
    step = pl.program_id(0)
    chunk, width = edge_ref.shape

    @pl.when(step == 0)
    def _():
        out_ref[...] = jnp.zeros_like(out_ref)

    edge = edge_ref[...]
    dst = dst_ref[...]
    sender = _fold_pick(ext_ref, src_ref[...], fold)
    receiver = _fold_pick(own_ref, dst, fold)
    pre = jnp.dot(edge, alpha_ref[0:width], preferred_element_type=jnp.float32)
    pre = pre + jnp.dot(sender, alpha_ref[width : 2 * width], preferred_element_type=jnp.float32)
    pre = pre + jnp.dot(receiver, alpha_ref[2 * width :], preferred_element_type=jnp.float32)
    first = _silu(pre).astype(jnp.bfloat16)
    second = _silu(jnp.dot(first, beta_ref[...], preferred_element_type=jnp.float32)).astype(
        jnp.bfloat16
    )
    third = jnp.dot(second, gamma_ref[...], preferred_element_type=jnp.float32)
    row_mean = jnp.mean(third, axis=-1, keepdims=True)
    centred = third - row_mean
    row_var = jnp.mean(centred * centred, axis=-1, keepdims=True)
    normed = centred * lax.rsqrt(row_var + 1e-05) * gain_ref[...]
    edge_new = (edge.astype(jnp.float32) + normed).astype(jnp.bfloat16)
    position = scalars[1] + step * chunk + lax.broadcasted_iota(jnp.int32, (chunk, 1), 0)
    live = position < scalars[2]
    messages = jnp.where(live, edge_new, jnp.zeros_like(edge_new))
    lane = jnp.bitwise_and(dst, fold - 1)
    spread = jnp.concatenate(
        [jnp.where(lane == j, messages, jnp.zeros_like(messages)) for j in range(fold)], axis=1
    )
    groups = out_ref.shape[0]
    shift = fold.bit_length() - 1
    hot_t = (
        lax.broadcasted_iota(jnp.int32, (groups, chunk), 0)
        == lax.shift_right_logical(dst_row_ref[0], shift)
    ).astype(jnp.bfloat16)
    out_ref[...] += jnp.dot(hot_t, spread, preferred_element_type=jnp.float32)


def edge_messages(edges, send_ids, recv_ids, extended, own_rows, alpha, beta, gamma, gain,
                  first_row, share, tally, chunk=1024, fold=FOLD):
    slots, width = edges.shape
    nodes = own_rows.shape[0]
    turns = share // chunk
    scalars = jnp.stack([first_row // chunk, first_row, tally]).astype(jnp.int32)
    both_ids = lax.dynamic_slice_in_dim(jnp.stack([send_ids, recv_ids]), first_row, share, 1)
    columns = both_ids.reshape(2, share, 1)
    recv_ids = both_ids[1]
    ext_wide = extended.reshape(extended.shape[0] // fold, fold * width)
    own_wide = own_rows.reshape(nodes // fold, fold * width)
    full = lambda shape: pl.BlockSpec(shape, lambda i, s: (0,) * len(shape))
    grid_spec = pltpu.PrefetchScalarGridSpec(
        num_scalar_prefetch=1,
        grid=(turns,),
        in_specs=[
            pl.BlockSpec((chunk, width), lambda i, s: (s[0] + i, 0)),
            pl.BlockSpec((chunk, 1), lambda i, s: (i, 0)),
            pl.BlockSpec((chunk, 1), lambda i, s: (i, 0)),
            pl.BlockSpec((1, 1, chunk), lambda i, s: (i, 0, 0)),
            full(ext_wide.shape),
            full(own_wide.shape),
            full(alpha.shape),
            full(beta.shape),
            full(gamma.shape),
            full((1, width)),
        ],
        out_specs=full((nodes // fold, fold * width)),
    )
    total = pl.pallas_call(
        functools.partial(_edge_kernel, fold),
        out_shape=jax.ShapeDtypeStruct((nodes // fold, fold * width), jnp.float32),
        grid_spec=grid_spec,
    )(
        scalars,
        edges,
        columns[0],
        columns[1],
        recv_ids.reshape(turns, 1, chunk),
        ext_wide,
        own_wide,
        alpha,
        beta,
        gamma,
        gain.reshape(1, width).astype(jnp.float32),
    )
    return total


def psum_slices(numer, denom):
    joined = jnp.concatenate([numer.reshape(-1), denom.reshape(-1)])
    rows = -(-joined.shape[0] // 1024) * 8
    padded = jnp.zeros((rows * 128,), joined.dtype).at[: joined.shape[0]].set(joined)
    total = dom_sum(padded.reshape(rows, 128)).reshape(-1)
    numer_size = numer.size
    return (
        total[:numer_size].reshape(numer.shape),
        total[numer_size : numer_size + denom.size].reshape(denom.shape),
    )


def layer_norm(values, gain_row):
    row_mean = jnp.mean(values, axis=-1, keepdims=True)
    centred = values - row_mean
    row_var = jnp.mean(centred * centred, axis=-1, keepdims=True)
    return centred * lax.rsqrt(row_var + 1e-05) * gain_row


def node_section(
    own_rows,
    summed_b,
    vertex_layer_alpha,
    vertex_layer_beta,
    vertex_layer_gamma,
    vertex_scale_factor,
):
    feature_width = own_rows.shape[1]
    node_pre = jnp.dot(
        own_rows, vertex_layer_alpha[:feature_width], preferred_element_type=jnp.float32
    )
    node_pre = node_pre + jnp.dot(
        summed_b, vertex_layer_alpha[feature_width:], preferred_element_type=jnp.float32
    )
    node_one = jax.nn.silu(node_pre).astype(jnp.bfloat16)
    node_two = jax.nn.silu(
        jnp.dot(node_one, vertex_layer_beta, preferred_element_type=jnp.float32)
    ).astype(jnp.bfloat16)
    node_three = jnp.dot(node_two, vertex_layer_gamma, preferred_element_type=jnp.float32)
    return (own_rows.astype(jnp.float32) + layer_norm(node_three, vertex_scale_factor)).astype(
        jnp.bfloat16
    )


def slice_partial_terms(
    refreshed_vertices,
    focus_scale_factor,
    vertex_content_factor,
    cluster_affinity_factor,
    softness_level,
):
    count_of_rows = refreshed_vertices.shape[0]
    domain_channel_split = softness_level.shape[0]
    standardised_entries = layer_norm(
        refreshed_vertices.astype(jnp.float32), focus_scale_factor
    ).astype(jnp.bfloat16)
    values = jnp.dot(
        standardised_entries, vertex_content_factor, preferred_element_type=jnp.float32
    ).astype(jnp.bfloat16)
    cluster_affinities = jnp.dot(
        standardised_entries, cluster_affinity_factor, preferred_element_type=jnp.float32
    )
    cluster_affinities = (
        cluster_affinities.reshape(count_of_rows, domain_channel_split, GROUPS_PER_LANE)
        / softness_level[None, :, None]
    )
    weights = jax.nn.softmax(cluster_affinities, axis=-1)
    weights_b = weights.astype(jnp.bfloat16)
    numer = jnp.einsum(
        "nhs,nhc->hsc",
        weights_b,
        values.reshape(count_of_rows, domain_channel_split, HEAD_DIM),
        preferred_element_type=jnp.float32,
    )
    denom = jnp.sum(weights, axis=0)
    return (weights_b, numer, denom)


def slice_mixing(numer, denom, cluster_probe_lookup, cluster_content_linear):
    tokens = numer / denom[:, :, None]
    highest = lax.Precision.HIGHEST
    query = jnp.einsum("hsc,hcd->hsd", tokens, cluster_probe_lookup[0], precision=highest)
    keys = jnp.einsum("hsc,hcd->hsd", tokens, cluster_probe_lookup[1], precision=highest)
    carried = jnp.einsum("hsc,hcd->hsd", tokens, cluster_content_linear, precision=highest)
    scores = jnp.einsum("hsd,htd->hst", query, keys, precision=highest) / math.sqrt(HEAD_DIM)
    mixing = jax.nn.softmax(scores, axis=-1)
    return jnp.einsum("hst,htd->hsd", mixing, carried, precision=highest).astype(jnp.bfloat16)


def attend_rows(weights_b, slice_out):
    count_of_rows = weights_b.shape[0]
    domain_channel_split = weights_b.shape[1]
    attended = jnp.einsum("nhs,hsd->nhd", weights_b, slice_out, preferred_element_type=jnp.float32)
    return attended.reshape(count_of_rows, domain_channel_split * HEAD_DIM).astype(jnp.bfloat16)


def pick_rows(table, row_ids):
    table_ids = jnp.arange(table.shape[0], dtype=jnp.int32)
    selector = (row_ids[:, None] == table_ids[None, :]).astype(jnp.bfloat16)
    return jnp.dot(selector, table, preferred_element_type=jnp.float32).astype(jnp.bfloat16)


def gather_rows(table, row_ids, fold):
    count, width = table.shape
    wide = table.reshape(count // fold, fold * width)
    hot = (row_ids[:, None] // fold == jnp.arange(count // fold, dtype=jnp.int32)[None, :]).astype(
        jnp.bfloat16
    )
    picked = jnp.dot(hot, wide, preferred_element_type=jnp.float32)
    lane = row_ids % fold
    rows = picked[:, :width]
    for j in range(1, fold):
        rows = jnp.where((lane == j)[:, None], picked[:, j * width : (j + 1) * width], rows)
    return rows.astype(jnp.bfloat16)


def scatter_rows(messages, row_ids, count, fold):
    width = messages.shape[1]
    lane = row_ids % fold
    spread = jnp.concatenate(
        [jnp.where((lane == j)[:, None], messages, jnp.zeros_like(messages)) for j in range(fold)],
        axis=1,
    )
    hot = (row_ids[:, None] // fold == jnp.arange(count // fold, dtype=jnp.int32)[None, :]).astype(
        jnp.bfloat16
    )
    total = lax.dot_general(
        hot, spread, (((0,), (0,)), ((), ())), preferred_element_type=jnp.float32
    )
    return total.reshape(count, width)


def body(
    vertex_state,
    link_state_slotted,
    source_vertex_ids,
    target_vertex_ids,
    active_link_tally,
    halo_outgoing_ids,
    link_layer_alpha,
    link_layer_beta,
    link_layer_gamma,
    link_scale_factor,
    vertex_layer_alpha,
    vertex_layer_beta,
    vertex_layer_gamma,
    vertex_scale_factor,
    focus_scale_factor,
    vertex_content_factor,
    cluster_affinity_factor,
    softness_level,
    cluster_probe_lookup,
    cluster_content_linear,
    closing_linear_factor,
):
    node_count = vertex_state.shape[0]
    feature_width = vertex_state.shape[1]
    capacity = link_state_slotted.shape[0]
    offsets = (1, -1, 2, -2)
    outgoing = pick_rows(vertex_state, halo_outgoing_ids[0].reshape(-1))
    extended = exchange_halos(
        vertex_state, outgoing.reshape(halo_outgoing_ids.shape[1:] + (feature_width,)), offsets
    )
    share = capacity // lax.axis_size("head")
    first_row = lax.axis_index("head") * share
    total = edge_messages(
        link_state_slotted,
        source_vertex_ids,
        target_vertex_ids,
        extended,
        vertex_state,
        link_layer_alpha,
        link_layer_beta,
        link_layer_gamma,
        link_scale_factor,
        first_row,
        share,
        active_link_tally[0],
    )
    summed = sibling_sum(total, 2).astype(jnp.bfloat16).reshape(vertex_state.shape)
    refreshed_vertices = node_section(
        vertex_state,
        summed.astype(jnp.bfloat16),
        vertex_layer_alpha,
        vertex_layer_beta,
        vertex_layer_gamma,
        vertex_scale_factor,
    )
    weights_b, numer, denom = slice_partial_terms(
        refreshed_vertices,
        focus_scale_factor,
        vertex_content_factor,
        cluster_affinity_factor,
        softness_level,
    )
    numer, denom = psum_slices(numer, denom)
    slice_out = slice_mixing(numer, denom, cluster_probe_lookup, cluster_content_linear)
    attended = attend_rows(weights_b, slice_out)
    projected = sibling_sum(
        jnp.dot(attended, closing_linear_factor, preferred_element_type=jnp.float32).astype(
            jnp.bfloat16
        ),
        3,
    )
    return (refreshed_vertices.astype(jnp.float32) + projected.astype(jnp.float32)).astype(
        jnp.bfloat16
    )


def solution(mesh):
    in_specs = (
        P("dom", None),
        P("dom", None),
        P("dom"),
        P("dom"),
        P("dom"),
        P("dom", None, None),
        P(),
        P(),
        P(),
        P(),
        P(),
        P(),
        P(),
        P(),
        P(),
        P(None, "head"),
        P(None, "head"),
        P("head"),
        P(None, "head", None, None),
        P("head", None, None),
        P("head", None),
    )
    out_specs = P("dom", None)
    return jax.shard_map(body, mesh=mesh, in_specs=in_specs, out_specs=out_specs, check_vma=False)
```

```python
import functools
import math

import jax
import jax.numpy as jnp
from jax import lax
from jax.experimental import pallas as pl
from jax.experimental.pallas import tpu as pltpu
from jax.sharding import PartitionSpec as P

HEAD_DIM = 16
GROUPS_PER_LANE = 64
FOLD = 4


def passed_along(value, axis, steps):
    count = lax.axis_size(axis)
    first, last = (max(0, -steps), min(count, count - steps))
    return lax.ppermute(value, axis, [(source, source + steps) for source in range(first, last)])


def _radix_kernel(radix, steps, x_ref, o_ref, inbox, send_sem, recv_sem):
    me = lax.axis_index("dom")
    spans = [radix**s for s in range(steps)]
    digits = [(me // span) % radix for span in spans]
    partners = [
        [me + ((digit + j) % radix - digit) * span for j in range(1, radix)]
        for digit, span in zip(digits, spans)
    ]
    barrier = pltpu.get_barrier_semaphore()
    for group in partners:
        for partner in group:
            pl.semaphore_signal(
                barrier, 1, device_id={"dom": partner}, device_id_type=pl.DeviceIdType.MESH
            )
    pl.semaphore_wait(barrier, steps * (radix - 1))
    for s in range(steps):
        source = x_ref if s == 0 else o_ref
        copies = []
        for j, partner in enumerate(partners[s]):
            copy = pltpu.make_async_remote_copy(
                src_ref=source,
                dst_ref=inbox.at[s, digits[s]],
                send_sem=send_sem.at[s, j],
                recv_sem=recv_sem.at[s, digits[s]],
                device_id={"dom": partner},
                device_id_type=pl.DeviceIdType.MESH,
            )
            copy.start()
            copies.append(copy)
        inbox[s, digits[s]] = source[...]
        for copy in copies:
            copy.wait_send()
        for j, partner in enumerate(partners[s]):
            slot = (digits[s] + j + 1) % radix
            pltpu.make_async_remote_copy(
                src_ref=source,
                dst_ref=inbox.at[s, slot],
                send_sem=send_sem.at[s, j],
                recv_sem=recv_sem.at[s, slot],
                device_id={"dom": partner},
                device_id_type=pl.DeviceIdType.MESH,
            ).wait_recv()
        total = inbox[s, 0]
        for d in range(1, radix):
            total = total + inbox[s, d]
        o_ref[...] = total


def dom_sum(flat):
    count = lax.axis_size("dom")
    radix = 4
    steps = 0
    while radix ** (steps + 1) <= count:
        steps += 1
    assert radix**steps == count
    return pl.pallas_call(
        functools.partial(_radix_kernel, radix, steps),
        out_shape=jax.ShapeDtypeStruct(flat.shape, flat.dtype),
        in_specs=[pl.BlockSpec(memory_space=pltpu.VMEM)],
        out_specs=pl.BlockSpec(memory_space=pltpu.VMEM),
        scratch_shapes=[
            pltpu.VMEM((steps, radix) + flat.shape, flat.dtype),
            pltpu.SemaphoreType.DMA((steps, radix - 1)),
            pltpu.SemaphoreType.DMA((steps, radix)),
        ],
        compiler_params=pltpu.CompilerParams(collective_id=0, has_side_effects=True),
    )(flat)


def _halo_kernel(offsets, own_ref, out_ref, ext_ref, send_sem, recv_sem, pass_sem, land_sem):
    me = lax.axis_index("dom")
    count = lax.axis_size("dom")
    core = lax.axis_index("head")
    sibling = 1 - core
    rows = own_ref.shape[0]
    halo = out_ref.shape[0] // len(offsets)
    half = halo // 2
    mesh_ids = pl.DeviceIdType.MESH
    barrier = pltpu.get_barrier_semaphore()
    for offset in offsets:
        pl.semaphore_signal(
            barrier, 1, device_id={"dom": (me + offset + count) % count}, device_id_type=mesh_ids
        )
    pl.semaphore_signal(barrier, 1, device_id={"head": sibling}, device_id_type=mesh_ids)
    pl.semaphore_wait(barrier, len(offsets) + 1)
    sends = []
    for k, offset in enumerate(offsets):
        copy = pltpu.make_async_remote_copy(
            src_ref=out_ref.at[pl.ds(k * halo + core * half, half)],
            dst_ref=ext_ref.at[pl.ds(rows + k * halo + core * half, half)],
            send_sem=send_sem.at[k],
            recv_sem=recv_sem.at[k],
            device_id={"dom": (me + offset + count) % count},
            device_id_type=mesh_ids,
        )
        copy.start()
        sends.append(copy)
    ext_ref[pl.ds(0, rows)] = own_ref[...]
    passes = []
    for k in range(len(offsets)):
        sends[k].wait_recv()
        forward = pltpu.make_async_remote_copy(
            src_ref=ext_ref.at[pl.ds(rows + k * halo + core * half, half)],
            dst_ref=ext_ref.at[pl.ds(rows + k * halo + core * half, half)],
            send_sem=pass_sem.at[k],
            recv_sem=land_sem.at[k],
            device_id={"head": sibling},
            device_id_type=mesh_ids,
        )
        forward.start()
        passes.append(forward)
    for copy in sends:
        copy.wait_send()
    for forward in passes:
        forward.wait()
    for k, offset in enumerate(offsets):
        if offset > 0:
            inside = (me + count - offset) // count
        else:
            inside = (2 * count - 1 + offset - me) // count
        slot = pl.ds(rows + k * halo, halo)
        ext_ref[slot] = ext_ref[slot] * inside.astype(ext_ref.dtype)


def exchange_halos(own_rows, outgoing, offsets):
    total = own_rows.shape[0] + outgoing.shape[0]
    return pl.pallas_call(
        functools.partial(_halo_kernel, offsets),
        out_shape=jax.ShapeDtypeStruct((total, own_rows.shape[1]), own_rows.dtype),
        in_specs=[pl.BlockSpec(memory_space=pltpu.VMEM)] * 2,
        out_specs=pl.BlockSpec(memory_space=pltpu.VMEM),
        scratch_shapes=[pltpu.SemaphoreType.DMA((len(offsets),))] * 4,
        compiler_params=pltpu.CompilerParams(collective_id=1, has_side_effects=True),
    )(own_rows, outgoing)


def _sibling_kernel(x_ref, o_ref, inbox, send_sem, recv_sem):
    sibling = 1 - lax.axis_index("head")
    mesh_ids = pl.DeviceIdType.MESH
    barrier = pltpu.get_barrier_semaphore()
    pl.semaphore_signal(barrier, 1, device_id={"head": sibling}, device_id_type=mesh_ids)
    pl.semaphore_wait(barrier, 1)
    copy = pltpu.make_async_remote_copy(
        src_ref=x_ref,
        dst_ref=inbox,
        send_sem=send_sem,
        recv_sem=recv_sem,
        device_id={"head": sibling},
        device_id_type=mesh_ids,
    )
    copy.start()
    copy.wait()
    o_ref[...] = x_ref[...].astype(o_ref.dtype) + inbox[...].astype(o_ref.dtype)


def sibling_sum(x, collective_id):
    return pl.pallas_call(
        _sibling_kernel,
        out_shape=jax.ShapeDtypeStruct(x.shape, jnp.float32),
        in_specs=[pl.BlockSpec(memory_space=pltpu.VMEM)],
        out_specs=pl.BlockSpec(memory_space=pltpu.VMEM),
        scratch_shapes=[
            pltpu.VMEM(x.shape, x.dtype),
            pltpu.SemaphoreType.DMA(()),
            pltpu.SemaphoreType.DMA(()),
        ],
        compiler_params=pltpu.CompilerParams(
            collective_id=collective_id, has_side_effects=True
        ),
    )(x)


def _silu(values):
    return values * (1.0 / (1.0 + jnp.exp(-values)))


def _fold_pick(table_ref, ids, fold):
    chunk = ids.shape[0]
    groups = table_ref.shape[0]
    width = table_ref.shape[1] // fold
    shift = fold.bit_length() - 1
    hot = (
        lax.shift_right_logical(ids, shift) == lax.broadcasted_iota(jnp.int32, (chunk, groups), 1)
    ).astype(jnp.bfloat16)
    picked = jnp.dot(hot, table_ref[...], preferred_element_type=jnp.float32)
    lane = jnp.bitwise_and(ids, fold - 1)
    rows = picked[:, :width]
    for j in range(1, fold):
        rows = jnp.where(lane == j, picked[:, j * width : (j + 1) * width], rows)
    return rows.astype(jnp.bfloat16)


def _edge_kernel(fold, scalars, edge_ref, src_ref, dst_ref, dst_row_ref, ext_ref, own_ref,
                 alpha_ref, beta_ref, gamma_ref, gain_ref, out_ref):
    step = pl.program_id(0)
    chunk, width = edge_ref.shape

    @pl.when(step == 0)
    def _():
        out_ref[...] = jnp.zeros_like(out_ref)

    edge = edge_ref[...]
    dst = dst_ref[...]
    sender = _fold_pick(ext_ref, src_ref[...], fold)
    receiver = _fold_pick(own_ref, dst, fold)
    pre = jnp.dot(edge, alpha_ref[0:width], preferred_element_type=jnp.float32)
    pre = pre + jnp.dot(sender, alpha_ref[width : 2 * width], preferred_element_type=jnp.float32)
    pre = pre + jnp.dot(receiver, alpha_ref[2 * width :], preferred_element_type=jnp.float32)
    first = _silu(pre).astype(jnp.bfloat16)
    second = _silu(jnp.dot(first, beta_ref[...], preferred_element_type=jnp.float32)).astype(
        jnp.bfloat16
    )
    third = jnp.dot(second, gamma_ref[...], preferred_element_type=jnp.float32)
    row_mean = jnp.mean(third, axis=-1, keepdims=True)
    centred = third - row_mean
    row_var = jnp.mean(centred * centred, axis=-1, keepdims=True)
    normed = centred * lax.rsqrt(row_var + 1e-05) * gain_ref[...]
    edge_new = (edge.astype(jnp.float32) + normed).astype(jnp.bfloat16)
    position = scalars[1] + step * chunk + lax.broadcasted_iota(jnp.int32, (chunk, 1), 0)
    live = position < scalars[2]
    messages = jnp.where(live, edge_new, jnp.zeros_like(edge_new))
    lane = jnp.bitwise_and(dst, fold - 1)
    spread = jnp.concatenate(
        [jnp.where(lane == j, messages, jnp.zeros_like(messages)) for j in range(fold)], axis=1
    )
    groups = out_ref.shape[0]
    shift = fold.bit_length() - 1
    hot_t = (
        lax.broadcasted_iota(jnp.int32, (groups, chunk), 0)
        == lax.shift_right_logical(dst_row_ref[0], shift)
    ).astype(jnp.bfloat16)
    out_ref[...] += jnp.dot(hot_t, spread, preferred_element_type=jnp.float32)


def edge_messages(edges, send_ids, recv_ids, extended, own_rows, alpha, beta, gamma, gain,
                  first_row, share, tally, chunk=1024, fold=FOLD):
    slots, width = edges.shape
    nodes = own_rows.shape[0] * fold
    turns = share // chunk
    scalars = jnp.stack([first_row // chunk, first_row, tally]).astype(jnp.int32)
    both_ids = lax.dynamic_slice_in_dim(jnp.stack([send_ids, recv_ids]), first_row, share, 1)
    columns = both_ids.reshape(2, share, 1)
    recv_ids = both_ids[1]
    ext_wide = extended
    own_wide = own_rows
    full = lambda shape: pl.BlockSpec(shape, lambda i, s: (0,) * len(shape))
    grid_spec = pltpu.PrefetchScalarGridSpec(
        num_scalar_prefetch=1,
        grid=(turns,),
        in_specs=[
            pl.BlockSpec((chunk, width), lambda i, s: (s[0] + i, 0)),
            pl.BlockSpec((chunk, 1), lambda i, s: (i, 0)),
            pl.BlockSpec((chunk, 1), lambda i, s: (i, 0)),
            pl.BlockSpec((1, 1, chunk), lambda i, s: (i, 0, 0)),
            full(ext_wide.shape),
            full(own_wide.shape),
            full(alpha.shape),
            full(beta.shape),
            full(gamma.shape),
            full((1, width)),
        ],
        out_specs=full((nodes // fold, fold * width)),
    )
    total = pl.pallas_call(
        functools.partial(_edge_kernel, fold),
        out_shape=jax.ShapeDtypeStruct((nodes // fold, fold * width), jnp.float32),
        grid_spec=grid_spec,
    )(
        scalars,
        edges,
        columns[0],
        columns[1],
        recv_ids.reshape(turns, 1, chunk),
        ext_wide,
        own_wide,
        alpha,
        beta,
        gamma,
        gain.reshape(1, width).astype(jnp.float32),
    )
    return total


def psum_slices(numer, denom):
    joined = jnp.concatenate([numer.reshape(-1), denom.reshape(-1)])
    rows = -(-joined.shape[0] // 1024) * 8
    padded = jnp.zeros((rows * 128,), joined.dtype).at[: joined.shape[0]].set(joined)
    total = dom_sum(padded.reshape(rows, 128)).reshape(-1)
    numer_size = numer.size
    return (
        total[:numer_size].reshape(numer.shape),
        total[numer_size : numer_size + denom.size].reshape(denom.shape),
    )


def layer_norm(values, gain_row):
    row_mean = jnp.mean(values, axis=-1, keepdims=True)
    centred = values - row_mean
    row_var = jnp.mean(centred * centred, axis=-1, keepdims=True)
    return centred * lax.rsqrt(row_var + 1e-05) * gain_row


def node_section(
    own_rows,
    summed_b,
    vertex_layer_alpha,
    vertex_layer_beta,
    vertex_layer_gamma,
    vertex_scale_factor,
):
    feature_width = own_rows.shape[1]
    node_pre = jnp.dot(
        own_rows, vertex_layer_alpha[:feature_width], preferred_element_type=jnp.float32
    )
    node_pre = node_pre + jnp.dot(
        summed_b, vertex_layer_alpha[feature_width:], preferred_element_type=jnp.float32
    )
    node_one = jax.nn.silu(node_pre).astype(jnp.bfloat16)
    node_two = jax.nn.silu(
        jnp.dot(node_one, vertex_layer_beta, preferred_element_type=jnp.float32)
    ).astype(jnp.bfloat16)
    node_three = jnp.dot(node_two, vertex_layer_gamma, preferred_element_type=jnp.float32)
    return (own_rows.astype(jnp.float32) + layer_norm(node_three, vertex_scale_factor)).astype(
        jnp.bfloat16
    )


def slice_partial_terms(
    refreshed_vertices,
    focus_scale_factor,
    vertex_content_factor,
    cluster_affinity_factor,
    softness_level,
):
    count_of_rows = refreshed_vertices.shape[0]
    domain_channel_split = softness_level.shape[0]
    standardised_entries = layer_norm(
        refreshed_vertices.astype(jnp.float32), focus_scale_factor
    ).astype(jnp.bfloat16)
    values = jnp.dot(
        standardised_entries, vertex_content_factor, preferred_element_type=jnp.float32
    ).astype(jnp.bfloat16)
    cluster_affinities = jnp.dot(
        standardised_entries, cluster_affinity_factor, preferred_element_type=jnp.float32
    )
    cluster_affinities = (
        cluster_affinities.reshape(count_of_rows, domain_channel_split, GROUPS_PER_LANE)
        / softness_level[None, :, None]
    )
    weights = jax.nn.softmax(cluster_affinities, axis=-1)
    weights_b = weights.astype(jnp.bfloat16)
    numer = jnp.einsum(
        "nhs,nhc->hsc",
        weights_b,
        values.reshape(count_of_rows, domain_channel_split, HEAD_DIM),
        preferred_element_type=jnp.float32,
    )
    denom = jnp.sum(weights, axis=0)
    return (weights_b, numer, denom)


def slice_mixing(numer, denom, cluster_probe_lookup, cluster_content_linear):
    tokens = numer / denom[:, :, None]
    highest = lax.Precision.HIGHEST
    query = jnp.einsum("hsc,hcd->hsd", tokens, cluster_probe_lookup[0], precision=highest)
    keys = jnp.einsum("hsc,hcd->hsd", tokens, cluster_probe_lookup[1], precision=highest)
    carried = jnp.einsum("hsc,hcd->hsd", tokens, cluster_content_linear, precision=highest)
    scores = jnp.einsum("hsd,htd->hst", query, keys, precision=highest) / math.sqrt(HEAD_DIM)
    mixing = jax.nn.softmax(scores, axis=-1)
    return jnp.einsum("hst,htd->hsd", mixing, carried, precision=highest).astype(jnp.bfloat16)


def attend_rows(weights_b, slice_out):
    count_of_rows = weights_b.shape[0]
    domain_channel_split = weights_b.shape[1]
    attended = jnp.einsum("nhs,hsd->nhd", weights_b, slice_out, preferred_element_type=jnp.float32)
    return attended.reshape(count_of_rows, domain_channel_split * HEAD_DIM).astype(jnp.bfloat16)


def pick_rows(table, row_ids):
    table_ids = jnp.arange(table.shape[0], dtype=jnp.int32)
    selector = (row_ids[:, None] == table_ids[None, :]).astype(jnp.bfloat16)
    return jnp.dot(selector, table, preferred_element_type=jnp.float32).astype(jnp.bfloat16)


def gather_rows(table, row_ids, fold):
    count, width = table.shape
    wide = table.reshape(count // fold, fold * width)
    hot = (row_ids[:, None] // fold == jnp.arange(count // fold, dtype=jnp.int32)[None, :]).astype(
        jnp.bfloat16
    )
    picked = jnp.dot(hot, wide, preferred_element_type=jnp.float32)
    lane = row_ids % fold
    rows = picked[:, :width]
    for j in range(1, fold):
        rows = jnp.where((lane == j)[:, None], picked[:, j * width : (j + 1) * width], rows)
    return rows.astype(jnp.bfloat16)


def scatter_rows(messages, row_ids, count, fold):
    width = messages.shape[1]
    lane = row_ids % fold
    spread = jnp.concatenate(
        [jnp.where((lane == j)[:, None], messages, jnp.zeros_like(messages)) for j in range(fold)],
        axis=1,
    )
    hot = (row_ids[:, None] // fold == jnp.arange(count // fold, dtype=jnp.int32)[None, :]).astype(
        jnp.bfloat16
    )
    total = lax.dot_general(
        hot, spread, (((0,), (0,)), ((), ())), preferred_element_type=jnp.float32
    )
    return total.reshape(count, width)


def body(
    vertex_state,
    link_state_slotted,
    source_vertex_ids,
    target_vertex_ids,
    active_link_tally,
    halo_outgoing_ids,
    link_layer_alpha,
    link_layer_beta,
    link_layer_gamma,
    link_scale_factor,
    vertex_layer_alpha,
    vertex_layer_beta,
    vertex_layer_gamma,
    vertex_scale_factor,
    focus_scale_factor,
    vertex_content_factor,
    cluster_affinity_factor,
    softness_level,
    cluster_probe_lookup,
    cluster_content_linear,
    closing_linear_factor,
):
    node_count = vertex_state.shape[0]
    feature_width = vertex_state.shape[1]
    capacity = link_state_slotted.shape[0]
    offsets = (1, -1, 2, -2)
    own_wide = vertex_state.reshape(node_count // FOLD, FOLD * feature_width)
    picked_ids = halo_outgoing_ids[0].reshape(-1, FOLD)
    outgoing = jnp.concatenate(
        [pick_rows(vertex_state, picked_ids[:, j]) for j in range(FOLD)], axis=1
    )
    extended = exchange_halos(own_wide, outgoing, offsets)
    share = capacity // lax.axis_size("head")
    first_row = lax.axis_index("head") * share
    total = edge_messages(
        link_state_slotted,
        source_vertex_ids,
        target_vertex_ids,
        extended,
        own_wide,
        link_layer_alpha,
        link_layer_beta,
        link_layer_gamma,
        link_scale_factor,
        first_row,
        share,
        active_link_tally[0],
    )
    summed = sibling_sum(total, 2).astype(jnp.bfloat16).reshape(vertex_state.shape)
    refreshed_vertices = node_section(
        vertex_state,
        summed.astype(jnp.bfloat16),
        vertex_layer_alpha,
        vertex_layer_beta,
        vertex_layer_gamma,
        vertex_scale_factor,
    )
    weights_b, numer, denom = slice_partial_terms(
        refreshed_vertices,
        focus_scale_factor,
        vertex_content_factor,
        cluster_affinity_factor,
        softness_level,
    )
    numer, denom = psum_slices(numer, denom)
    slice_out = slice_mixing(numer, denom, cluster_probe_lookup, cluster_content_linear)
    attended = attend_rows(weights_b, slice_out)
    projected = sibling_sum(
        jnp.dot(attended, closing_linear_factor, preferred_element_type=jnp.float32).astype(
            jnp.bfloat16
        ),
        3,
    )
    return (refreshed_vertices.astype(jnp.float32) + projected.astype(jnp.float32)).astype(
        jnp.bfloat16
    )


def solution(mesh):
    in_specs = (
        P("dom", None),
        P("dom", None),
        P("dom"),
        P("dom"),
        P("dom"),
        P("dom", None, None),
        P(),
        P(),
        P(),
        P(),
        P(),
        P(),
        P(),
        P(),
        P(),
        P(None, "head"),
        P(None, "head"),
        P("head"),
        P(None, "head", None, None),
        P("head", None, None),
        P("head", None),
    )
    out_specs = P("dom", None)
    return jax.shard_map(body, mesh=mesh, in_specs=in_specs, out_specs=out_specs, check_vma=False)
```

```python
import functools
import math

import jax
import jax.numpy as jnp
from jax import lax
from jax.experimental import pallas as pl
from jax.experimental.pallas import tpu as pltpu
from jax.sharding import PartitionSpec as P

HEAD_DIM = 16
GROUPS_PER_LANE = 64
FOLD = 4


def passed_along(value, axis, steps):
    count = lax.axis_size(axis)
    first, last = (max(0, -steps), min(count, count - steps))
    return lax.ppermute(value, axis, [(source, source + steps) for source in range(first, last)])


def _radix_kernel(radix, steps, x_ref, o_ref, inbox, send_sem, recv_sem):
    me = lax.axis_index("dom")
    spans = [radix**s for s in range(steps)]
    digits = [(me // span) % radix for span in spans]
    partners = [
        [me + ((digit + j) % radix - digit) * span for j in range(1, radix)]
        for digit, span in zip(digits, spans)
    ]
    barrier = pltpu.get_barrier_semaphore()
    for group in partners:
        for partner in group:
            pl.semaphore_signal(
                barrier, 1, device_id={"dom": partner}, device_id_type=pl.DeviceIdType.MESH
            )
    pl.semaphore_wait(barrier, steps * (radix - 1))
    for s in range(steps):
        source = x_ref if s == 0 else o_ref
        copies = []
        for j, partner in enumerate(partners[s]):
            copy = pltpu.make_async_remote_copy(
                src_ref=source,
                dst_ref=inbox.at[s, digits[s]],
                send_sem=send_sem.at[s, j],
                recv_sem=recv_sem.at[s, digits[s]],
                device_id={"dom": partner},
                device_id_type=pl.DeviceIdType.MESH,
            )
            copy.start()
            copies.append(copy)
        inbox[s, digits[s]] = source[...]
        for copy in copies:
            copy.wait_send()
        for j, partner in enumerate(partners[s]):
            slot = (digits[s] + j + 1) % radix
            pltpu.make_async_remote_copy(
                src_ref=source,
                dst_ref=inbox.at[s, slot],
                send_sem=send_sem.at[s, j],
                recv_sem=recv_sem.at[s, slot],
                device_id={"dom": partner},
                device_id_type=pl.DeviceIdType.MESH,
            ).wait_recv()
        total = inbox[s, 0]
        for d in range(1, radix):
            total = total + inbox[s, d]
        o_ref[...] = total


def dom_sum(flat):
    count = lax.axis_size("dom")
    radix = 8
    steps = 0
    while radix ** (steps + 1) <= count:
        steps += 1
    assert radix**steps == count
    return pl.pallas_call(
        functools.partial(_radix_kernel, radix, steps),
        out_shape=jax.ShapeDtypeStruct(flat.shape, flat.dtype),
        in_specs=[pl.BlockSpec(memory_space=pltpu.VMEM)],
        out_specs=pl.BlockSpec(memory_space=pltpu.VMEM),
        scratch_shapes=[
            pltpu.VMEM((steps, radix) + flat.shape, flat.dtype),
            pltpu.SemaphoreType.DMA((steps, radix - 1)),
            pltpu.SemaphoreType.DMA((steps, radix)),
        ],
        compiler_params=pltpu.CompilerParams(collective_id=0, has_side_effects=True),
    )(flat)


def _halo_kernel(offsets, own_ref, out_ref, ext_ref, send_sem, recv_sem, pass_sem, land_sem):
    me = lax.axis_index("dom")
    count = lax.axis_size("dom")
    core = lax.axis_index("head")
    sibling = 1 - core
    rows = own_ref.shape[0]
    halo = out_ref.shape[0] // len(offsets)
    half = halo // 2
    mesh_ids = pl.DeviceIdType.MESH
    barrier = pltpu.get_barrier_semaphore()
    for offset in offsets:
        pl.semaphore_signal(
            barrier, 1, device_id={"dom": (me + offset + count) % count}, device_id_type=mesh_ids
        )
    pl.semaphore_signal(barrier, 1, device_id={"head": sibling}, device_id_type=mesh_ids)
    pl.semaphore_wait(barrier, len(offsets) + 1)
    sends = []
    for k, offset in enumerate(offsets):
        copy = pltpu.make_async_remote_copy(
            src_ref=out_ref.at[pl.ds(k * halo + core * half, half)],
            dst_ref=ext_ref.at[pl.ds(rows + k * halo + core * half, half)],
            send_sem=send_sem.at[k],
            recv_sem=recv_sem.at[k],
            device_id={"dom": (me + offset + count) % count},
            device_id_type=mesh_ids,
        )
        copy.start()
        sends.append(copy)
    ext_ref[pl.ds(0, rows)] = own_ref[...]
    passes = []
    for k in range(len(offsets)):
        sends[k].wait_recv()
        forward = pltpu.make_async_remote_copy(
            src_ref=ext_ref.at[pl.ds(rows + k * halo + core * half, half)],
            dst_ref=ext_ref.at[pl.ds(rows + k * halo + core * half, half)],
            send_sem=pass_sem.at[k],
            recv_sem=land_sem.at[k],
            device_id={"head": sibling},
            device_id_type=mesh_ids,
        )
        forward.start()
        passes.append(forward)
    for copy in sends:
        copy.wait_send()
    for forward in passes:
        forward.wait()
    for k, offset in enumerate(offsets):
        if offset > 0:
            inside = (me + count - offset) // count
        else:
            inside = (2 * count - 1 + offset - me) // count
        slot = pl.ds(rows + k * halo, halo)
        ext_ref[slot] = ext_ref[slot] * inside.astype(ext_ref.dtype)


def exchange_halos(own_rows, outgoing, offsets):
    total = own_rows.shape[0] + outgoing.shape[0]
    return pl.pallas_call(
        functools.partial(_halo_kernel, offsets),
        out_shape=jax.ShapeDtypeStruct((total, own_rows.shape[1]), own_rows.dtype),
        in_specs=[pl.BlockSpec(memory_space=pltpu.VMEM)] * 2,
        out_specs=pl.BlockSpec(memory_space=pltpu.VMEM),
        scratch_shapes=[pltpu.SemaphoreType.DMA((len(offsets),))] * 4,
        compiler_params=pltpu.CompilerParams(collective_id=1, has_side_effects=True),
    )(own_rows, outgoing)


def _sibling_kernel(x_ref, o_ref, inbox, send_sem, recv_sem):
    sibling = 1 - lax.axis_index("head")
    mesh_ids = pl.DeviceIdType.MESH
    barrier = pltpu.get_barrier_semaphore()
    pl.semaphore_signal(barrier, 1, device_id={"head": sibling}, device_id_type=mesh_ids)
    pl.semaphore_wait(barrier, 1)
    copy = pltpu.make_async_remote_copy(
        src_ref=x_ref,
        dst_ref=inbox,
        send_sem=send_sem,
        recv_sem=recv_sem,
        device_id={"head": sibling},
        device_id_type=mesh_ids,
    )
    copy.start()
    copy.wait()
    o_ref[...] = x_ref[...].astype(o_ref.dtype) + inbox[...].astype(o_ref.dtype)


def sibling_sum(x, collective_id):
    return pl.pallas_call(
        _sibling_kernel,
        out_shape=jax.ShapeDtypeStruct(x.shape, jnp.float32),
        in_specs=[pl.BlockSpec(memory_space=pltpu.VMEM)],
        out_specs=pl.BlockSpec(memory_space=pltpu.VMEM),
        scratch_shapes=[
            pltpu.VMEM(x.shape, x.dtype),
            pltpu.SemaphoreType.DMA(()),
            pltpu.SemaphoreType.DMA(()),
        ],
        compiler_params=pltpu.CompilerParams(
            collective_id=collective_id, has_side_effects=True
        ),
    )(x)


def _silu(values):
    return values * (1.0 / (1.0 + jnp.exp(-values)))


def _fold_pick(table_ref, ids, fold):
    chunk = ids.shape[0]
    groups = table_ref.shape[0]
    width = table_ref.shape[1] // fold
    shift = fold.bit_length() - 1
    hot = (
        lax.shift_right_logical(ids, shift) == lax.broadcasted_iota(jnp.int32, (chunk, groups), 1)
    ).astype(jnp.bfloat16)
    picked = jnp.dot(hot, table_ref[...], preferred_element_type=jnp.float32)
    lane = jnp.bitwise_and(ids, fold - 1)
    rows = picked[:, :width]
    for j in range(1, fold):
        rows = jnp.where(lane == j, picked[:, j * width : (j + 1) * width], rows)
    return rows.astype(jnp.bfloat16)


def _edge_kernel(fold, scalars, edge_ref, src_ref, dst_ref, dst_row_ref, ext_ref, own_ref,
                 alpha_ref, beta_ref, gamma_ref, gain_ref, out_ref):
    step = pl.program_id(0)
    chunk, width = edge_ref.shape

    @pl.when(step == 0)
    def _():
        out_ref[...] = jnp.zeros_like(out_ref)

    edge = edge_ref[...]
    dst = dst_ref[...]
    sender = _fold_pick(ext_ref, src_ref[...], fold)
    receiver = _fold_pick(own_ref, dst, fold)
    pre = jnp.dot(edge, alpha_ref[0:width], preferred_element_type=jnp.float32)
    pre = pre + jnp.dot(sender, alpha_ref[width : 2 * width], preferred_element_type=jnp.float32)
    pre = pre + jnp.dot(receiver, alpha_ref[2 * width :], preferred_element_type=jnp.float32)
    first = _silu(pre).astype(jnp.bfloat16)
    second = _silu(jnp.dot(first, beta_ref[...], preferred_element_type=jnp.float32)).astype(
        jnp.bfloat16
    )
    third = jnp.dot(second, gamma_ref[...], preferred_element_type=jnp.float32)
    row_mean = jnp.mean(third, axis=-1, keepdims=True)
    centred = third - row_mean
    row_var = jnp.mean(centred * centred, axis=-1, keepdims=True)
    normed = centred * lax.rsqrt(row_var + 1e-05) * gain_ref[...]
    edge_new = (edge.astype(jnp.float32) + normed).astype(jnp.bfloat16)
    position = scalars[1] + step * chunk + lax.broadcasted_iota(jnp.int32, (chunk, 1), 0)
    live = position < scalars[2]
    messages = jnp.where(live, edge_new, jnp.zeros_like(edge_new))
    lane = jnp.bitwise_and(dst, fold - 1)
    spread = jnp.concatenate(
        [jnp.where(lane == j, messages, jnp.zeros_like(messages)) for j in range(fold)], axis=1
    )
    groups = out_ref.shape[0]
    shift = fold.bit_length() - 1
    hot_t = (
        lax.broadcasted_iota(jnp.int32, (groups, chunk), 0)
        == lax.shift_right_logical(dst_row_ref[0], shift)
    ).astype(jnp.bfloat16)
    out_ref[...] += jnp.dot(hot_t, spread, preferred_element_type=jnp.float32)


def edge_messages(edges, send_ids, recv_ids, extended, own_rows, alpha, beta, gamma, gain,
                  first_row, share, tally, chunk=1024, fold=FOLD):
    slots, width = edges.shape
    nodes = own_rows.shape[0] * fold
    turns = share // chunk
    scalars = jnp.stack([first_row // chunk, first_row, tally]).astype(jnp.int32)
    both_ids = lax.dynamic_slice_in_dim(jnp.stack([send_ids, recv_ids]), first_row, share, 1)
    columns = both_ids.reshape(2, share, 1)
    recv_ids = both_ids[1]
    ext_wide = extended
    own_wide = own_rows
    full = lambda shape: pl.BlockSpec(shape, lambda i, s: (0,) * len(shape))
    grid_spec = pltpu.PrefetchScalarGridSpec(
        num_scalar_prefetch=1,
        grid=(turns,),
        in_specs=[
            pl.BlockSpec((chunk, width), lambda i, s: (s[0] + i, 0)),
            pl.BlockSpec((chunk, 1), lambda i, s: (i, 0)),
            pl.BlockSpec((chunk, 1), lambda i, s: (i, 0)),
            pl.BlockSpec((1, 1, chunk), lambda i, s: (i, 0, 0)),
            full(ext_wide.shape),
            full(own_wide.shape),
            full(alpha.shape),
            full(beta.shape),
            full(gamma.shape),
            full((1, width)),
        ],
        out_specs=full((nodes // fold, fold * width)),
    )
    total = pl.pallas_call(
        functools.partial(_edge_kernel, fold),
        out_shape=jax.ShapeDtypeStruct((nodes // fold, fold * width), jnp.float32),
        grid_spec=grid_spec,
    )(
        scalars,
        edges,
        columns[0],
        columns[1],
        recv_ids.reshape(turns, 1, chunk),
        ext_wide,
        own_wide,
        alpha,
        beta,
        gamma,
        gain.reshape(1, width).astype(jnp.float32),
    )
    return total


def psum_slices(numer, denom):
    joined = jnp.concatenate([numer.reshape(-1), denom.reshape(-1)])
    rows = -(-joined.shape[0] // 1024) * 8
    padded = jnp.zeros((rows * 128,), joined.dtype).at[: joined.shape[0]].set(joined)
    total = dom_sum(padded.reshape(rows, 128)).reshape(-1)
    numer_size = numer.size
    return (
        total[:numer_size].reshape(numer.shape),
        total[numer_size : numer_size + denom.size].reshape(denom.shape),
    )


def layer_norm(values, gain_row):
    row_mean = jnp.mean(values, axis=-1, keepdims=True)
    centred = values - row_mean
    row_var = jnp.mean(centred * centred, axis=-1, keepdims=True)
    return centred * lax.rsqrt(row_var + 1e-05) * gain_row


def node_section(
    own_rows,
    summed_b,
    vertex_layer_alpha,
    vertex_layer_beta,
    vertex_layer_gamma,
    vertex_scale_factor,
):
    feature_width = own_rows.shape[1]
    node_pre = jnp.dot(
        own_rows, vertex_layer_alpha[:feature_width], preferred_element_type=jnp.float32
    )
    node_pre = node_pre + jnp.dot(
        summed_b, vertex_layer_alpha[feature_width:], preferred_element_type=jnp.float32
    )
    node_one = jax.nn.silu(node_pre).astype(jnp.bfloat16)
    node_two = jax.nn.silu(
        jnp.dot(node_one, vertex_layer_beta, preferred_element_type=jnp.float32)
    ).astype(jnp.bfloat16)
    node_three = jnp.dot(node_two, vertex_layer_gamma, preferred_element_type=jnp.float32)
    return (own_rows.astype(jnp.float32) + layer_norm(node_three, vertex_scale_factor)).astype(
        jnp.bfloat16
    )


def slice_partial_terms(
    refreshed_vertices,
    focus_scale_factor,
    vertex_content_factor,
    cluster_affinity_factor,
    softness_level,
):
    count_of_rows = refreshed_vertices.shape[0]
    domain_channel_split = softness_level.shape[0]
    standardised_entries = layer_norm(
        refreshed_vertices.astype(jnp.float32), focus_scale_factor
    ).astype(jnp.bfloat16)
    values = jnp.dot(
        standardised_entries, vertex_content_factor, preferred_element_type=jnp.float32
    ).astype(jnp.bfloat16)
    cluster_affinities = jnp.dot(
        standardised_entries, cluster_affinity_factor, preferred_element_type=jnp.float32
    )
    cluster_affinities = (
        cluster_affinities.reshape(count_of_rows, domain_channel_split, GROUPS_PER_LANE)
        / softness_level[None, :, None]
    )
    weights = jax.nn.softmax(cluster_affinities, axis=-1)
    weights_b = weights.astype(jnp.bfloat16)
    numer = jnp.einsum(
        "nhs,nhc->hsc",
        weights_b,
        values.reshape(count_of_rows, domain_channel_split, HEAD_DIM),
        preferred_element_type=jnp.float32,
    )
    denom = jnp.sum(weights, axis=0)
    return (weights_b, numer, denom)


def slice_mixing(numer, denom, cluster_probe_lookup, cluster_content_linear):
    tokens = numer / denom[:, :, None]
    highest = lax.Precision.HIGHEST
    query = jnp.einsum("hsc,hcd->hsd", tokens, cluster_probe_lookup[0], precision=highest)
    keys = jnp.einsum("hsc,hcd->hsd", tokens, cluster_probe_lookup[1], precision=highest)
    carried = jnp.einsum("hsc,hcd->hsd", tokens, cluster_content_linear, precision=highest)
    scores = jnp.einsum("hsd,htd->hst", query, keys, precision=highest) / math.sqrt(HEAD_DIM)
    mixing = jax.nn.softmax(scores, axis=-1)
    return jnp.einsum("hst,htd->hsd", mixing, carried, precision=highest).astype(jnp.bfloat16)


def attend_rows(weights_b, slice_out):
    count_of_rows = weights_b.shape[0]
    domain_channel_split = weights_b.shape[1]
    attended = jnp.einsum("nhs,hsd->nhd", weights_b, slice_out, preferred_element_type=jnp.float32)
    return attended.reshape(count_of_rows, domain_channel_split * HEAD_DIM).astype(jnp.bfloat16)


def pick_rows(table, row_ids):
    table_ids = jnp.arange(table.shape[0], dtype=jnp.int32)
    selector = (row_ids[:, None] == table_ids[None, :]).astype(jnp.bfloat16)
    return jnp.dot(selector, table, preferred_element_type=jnp.float32).astype(jnp.bfloat16)


def gather_rows(table, row_ids, fold):
    count, width = table.shape
    wide = table.reshape(count // fold, fold * width)
    hot = (row_ids[:, None] // fold == jnp.arange(count // fold, dtype=jnp.int32)[None, :]).astype(
        jnp.bfloat16
    )
    picked = jnp.dot(hot, wide, preferred_element_type=jnp.float32)
    lane = row_ids % fold
    rows = picked[:, :width]
    for j in range(1, fold):
        rows = jnp.where((lane == j)[:, None], picked[:, j * width : (j + 1) * width], rows)
    return rows.astype(jnp.bfloat16)


def scatter_rows(messages, row_ids, count, fold):
    width = messages.shape[1]
    lane = row_ids % fold
    spread = jnp.concatenate(
        [jnp.where((lane == j)[:, None], messages, jnp.zeros_like(messages)) for j in range(fold)],
        axis=1,
    )
    hot = (row_ids[:, None] // fold == jnp.arange(count // fold, dtype=jnp.int32)[None, :]).astype(
        jnp.bfloat16
    )
    total = lax.dot_general(
        hot, spread, (((0,), (0,)), ((), ())), preferred_element_type=jnp.float32
    )
    return total.reshape(count, width)


def body(
    vertex_state,
    link_state_slotted,
    source_vertex_ids,
    target_vertex_ids,
    active_link_tally,
    halo_outgoing_ids,
    link_layer_alpha,
    link_layer_beta,
    link_layer_gamma,
    link_scale_factor,
    vertex_layer_alpha,
    vertex_layer_beta,
    vertex_layer_gamma,
    vertex_scale_factor,
    focus_scale_factor,
    vertex_content_factor,
    cluster_affinity_factor,
    softness_level,
    cluster_probe_lookup,
    cluster_content_linear,
    closing_linear_factor,
):
    node_count = vertex_state.shape[0]
    feature_width = vertex_state.shape[1]
    capacity = link_state_slotted.shape[0]
    offsets = (1, -1, 2, -2)
    own_wide = vertex_state.reshape(node_count // FOLD, FOLD * feature_width)
    picked_ids = halo_outgoing_ids[0].reshape(-1, FOLD)
    outgoing = jnp.concatenate(
        [pick_rows(vertex_state, picked_ids[:, j]) for j in range(FOLD)], axis=1
    )
    extended = exchange_halos(own_wide, outgoing, offsets)
    share = capacity // lax.axis_size("head")
    first_row = lax.axis_index("head") * share
    total = edge_messages(
        link_state_slotted,
        source_vertex_ids,
        target_vertex_ids,
        extended,
        own_wide,
        link_layer_alpha,
        link_layer_beta,
        link_layer_gamma,
        link_scale_factor,
        first_row,
        share,
        active_link_tally[0],
    )
    summed = sibling_sum(total, 2).astype(jnp.bfloat16).reshape(vertex_state.shape)
    refreshed_vertices = node_section(
        vertex_state,
        summed.astype(jnp.bfloat16),
        vertex_layer_alpha,
        vertex_layer_beta,
        vertex_layer_gamma,
        vertex_scale_factor,
    )
    weights_b, numer, denom = slice_partial_terms(
        refreshed_vertices,
        focus_scale_factor,
        vertex_content_factor,
        cluster_affinity_factor,
        softness_level,
    )
    numer, denom = psum_slices(numer, denom)
    slice_out = slice_mixing(numer, denom, cluster_probe_lookup, cluster_content_linear)
    attended = attend_rows(weights_b, slice_out)
    projected = sibling_sum(
        jnp.dot(attended, closing_linear_factor, preferred_element_type=jnp.float32).astype(
            jnp.bfloat16
        ),
        3,
    )
    return (refreshed_vertices.astype(jnp.float32) + projected.astype(jnp.float32)).astype(
        jnp.bfloat16
    )


def solution(mesh):
    in_specs = (
        P("dom", None),
        P("dom", None),
        P("dom"),
        P("dom"),
        P("dom"),
        P("dom", None, None),
        P(),
        P(),
        P(),
        P(),
        P(),
        P(),
        P(),
        P(),
        P(),
        P(None, "head"),
        P(None, "head"),
        P("head"),
        P(None, "head", None, None),
        P("head", None, None),
        P("head", None),
    )
    out_specs = P("dom", None)
    return jax.shard_map(body, mesh=mesh, in_specs=in_specs, out_specs=out_specs, check_vma=False)
```

```python
import functools
import math

import jax
import jax.numpy as jnp
from jax import lax
from jax.experimental import pallas as pl
from jax.experimental.pallas import tpu as pltpu
from jax.sharding import PartitionSpec as P

HEAD_DIM = 16
GROUPS_PER_LANE = 64
FOLD = 4


def passed_along(value, axis, steps):
    count = lax.axis_size(axis)
    first, last = (max(0, -steps), min(count, count - steps))
    return lax.ppermute(value, axis, [(source, source + steps) for source in range(first, last)])


def _radix_kernel(radix, steps, x_ref, o_ref, inbox, send_sem, recv_sem):
    me = lax.axis_index("dom")
    spans = [radix**s for s in range(steps)]
    digits = [(me // span) % radix for span in spans]
    partners = [
        [me + ((digit + j) % radix - digit) * span for j in range(1, radix)]
        for digit, span in zip(digits, spans)
    ]
    barrier = pltpu.get_barrier_semaphore()
    for group in partners:
        for partner in group:
            pl.semaphore_signal(
                barrier, 1, device_id={"dom": partner}, device_id_type=pl.DeviceIdType.MESH
            )
    pl.semaphore_wait(barrier, steps * (radix - 1))
    for s in range(steps):
        source = x_ref if s == 0 else o_ref
        copies = []
        for j, partner in enumerate(partners[s]):
            copy = pltpu.make_async_remote_copy(
                src_ref=source,
                dst_ref=inbox.at[s, digits[s]],
                send_sem=send_sem.at[s, j],
                recv_sem=recv_sem.at[s, digits[s]],
                device_id={"dom": partner},
                device_id_type=pl.DeviceIdType.MESH,
            )
            copy.start()
            copies.append(copy)
        inbox[s, digits[s]] = source[...]
        for copy in copies:
            copy.wait_send()
        for j, partner in enumerate(partners[s]):
            slot = (digits[s] + j + 1) % radix
            pltpu.make_async_remote_copy(
                src_ref=source,
                dst_ref=inbox.at[s, slot],
                send_sem=send_sem.at[s, j],
                recv_sem=recv_sem.at[s, slot],
                device_id={"dom": partner},
                device_id_type=pl.DeviceIdType.MESH,
            ).wait_recv()
        total = inbox[s, 0]
        for d in range(1, radix):
            total = total + inbox[s, d]
        o_ref[...] = total


def dom_sum(flat):
    count = lax.axis_size("dom")
    radix = 8
    steps = 0
    while radix ** (steps + 1) <= count:
        steps += 1
    assert radix**steps == count
    return pl.pallas_call(
        functools.partial(_radix_kernel, radix, steps),
        out_shape=jax.ShapeDtypeStruct(flat.shape, flat.dtype),
        in_specs=[pl.BlockSpec(memory_space=pltpu.VMEM)],
        out_specs=pl.BlockSpec(memory_space=pltpu.VMEM),
        scratch_shapes=[
            pltpu.VMEM((steps, radix) + flat.shape, flat.dtype),
            pltpu.SemaphoreType.DMA((steps, radix - 1)),
            pltpu.SemaphoreType.DMA((steps, radix)),
        ],
        compiler_params=pltpu.CompilerParams(collective_id=0, has_side_effects=True),
    )(flat)


def _halo_kernel(offsets, own_ref, out_ref, ext_ref, send_sem, recv_sem, pass_sem, land_sem):
    me = lax.axis_index("dom")
    count = lax.axis_size("dom")
    core = lax.axis_index("head")
    sibling = 1 - core
    rows = own_ref.shape[0]
    halo = out_ref.shape[0] // len(offsets)
    half = halo // 2
    mesh_ids = pl.DeviceIdType.MESH
    barrier = pltpu.get_barrier_semaphore()
    for offset in offsets:
        pl.semaphore_signal(
            barrier, 1, device_id={"dom": (me + offset + count) % count}, device_id_type=mesh_ids
        )
    pl.semaphore_signal(barrier, 1, device_id={"head": sibling}, device_id_type=mesh_ids)
    pl.semaphore_wait(barrier, len(offsets) + 1)
    sends = []
    for k, offset in enumerate(offsets):
        copy = pltpu.make_async_remote_copy(
            src_ref=out_ref.at[pl.ds(k * halo + core * half, half)],
            dst_ref=ext_ref.at[pl.ds(rows + k * halo + core * half, half)],
            send_sem=send_sem.at[k],
            recv_sem=recv_sem.at[k],
            device_id={"dom": (me + offset + count) % count},
            device_id_type=mesh_ids,
        )
        copy.start()
        sends.append(copy)
    ext_ref[pl.ds(0, rows)] = own_ref[...]
    passes = []
    for k in range(len(offsets)):
        sends[k].wait_recv()
        forward = pltpu.make_async_remote_copy(
            src_ref=ext_ref.at[pl.ds(rows + k * halo + core * half, half)],
            dst_ref=ext_ref.at[pl.ds(rows + k * halo + core * half, half)],
            send_sem=pass_sem.at[k],
            recv_sem=land_sem.at[k],
            device_id={"head": sibling},
            device_id_type=mesh_ids,
        )
        forward.start()
        passes.append(forward)
    for copy in sends:
        copy.wait_send()
    for forward in passes:
        forward.wait()
    for k, offset in enumerate(offsets):
        if offset > 0:
            inside = (me + count - offset) // count
        else:
            inside = (2 * count - 1 + offset - me) // count
        slot = pl.ds(rows + k * halo, halo)
        ext_ref[slot] = ext_ref[slot] * inside.astype(ext_ref.dtype)


def exchange_halos(own_rows, outgoing, offsets):
    total = own_rows.shape[0] + outgoing.shape[0]
    return pl.pallas_call(
        functools.partial(_halo_kernel, offsets),
        out_shape=jax.ShapeDtypeStruct((total, own_rows.shape[1]), own_rows.dtype),
        in_specs=[pl.BlockSpec(memory_space=pltpu.VMEM)] * 2,
        out_specs=pl.BlockSpec(memory_space=pltpu.VMEM),
        scratch_shapes=[pltpu.SemaphoreType.DMA((len(offsets),))] * 4,
        compiler_params=pltpu.CompilerParams(collective_id=1, has_side_effects=True),
    )(own_rows, outgoing)


def _sibling_kernel(x_ref, o_ref, inbox, send_sem, recv_sem):
    sibling = 1 - lax.axis_index("head")
    mesh_ids = pl.DeviceIdType.MESH
    barrier = pltpu.get_barrier_semaphore()
    pl.semaphore_signal(barrier, 1, device_id={"head": sibling}, device_id_type=mesh_ids)
    pl.semaphore_wait(barrier, 1)
    copy = pltpu.make_async_remote_copy(
        src_ref=x_ref,
        dst_ref=inbox,
        send_sem=send_sem,
        recv_sem=recv_sem,
        device_id={"head": sibling},
        device_id_type=mesh_ids,
    )
    copy.start()
    copy.wait()
    o_ref[...] = x_ref[...].astype(o_ref.dtype) + inbox[...].astype(o_ref.dtype)


def sibling_sum(x, collective_id):
    return pl.pallas_call(
        _sibling_kernel,
        out_shape=jax.ShapeDtypeStruct(x.shape, jnp.float32),
        in_specs=[pl.BlockSpec(memory_space=pltpu.VMEM)],
        out_specs=pl.BlockSpec(memory_space=pltpu.VMEM),
        scratch_shapes=[
            pltpu.VMEM(x.shape, x.dtype),
            pltpu.SemaphoreType.DMA(()),
            pltpu.SemaphoreType.DMA(()),
        ],
        compiler_params=pltpu.CompilerParams(
            collective_id=collective_id, has_side_effects=True
        ),
    )(x)


def _silu(values):
    return values * (1.0 / (1.0 + jnp.exp(-values)))


def _fold_pick(table_ref, ids, fold):
    chunk = ids.shape[0]
    groups = table_ref.shape[0]
    width = table_ref.shape[1] // fold
    shift = fold.bit_length() - 1
    hot = (
        lax.shift_right_logical(ids, shift) == lax.broadcasted_iota(jnp.int32, (chunk, groups), 1)
    ).astype(jnp.bfloat16)
    picked = jnp.dot(hot, table_ref[...], preferred_element_type=jnp.float32)
    lane = jnp.bitwise_and(ids, fold - 1)
    rows = picked[:, :width]
    for j in range(1, fold):
        rows = jnp.where(lane == j, picked[:, j * width : (j + 1) * width], rows)
    return rows.astype(jnp.bfloat16)


def _edge_kernel(fold, scalars, edge_ref, src_ref, dst_ref, dst_row_ref, ext_ref, own_ref,
                 alpha_ref, beta_ref, gamma_ref, gain_ref, out_ref):
    step = pl.program_id(0)
    chunk, width = edge_ref.shape

    @pl.when(step == 0)
    def _():
        out_ref[...] = jnp.zeros_like(out_ref)

    edge = edge_ref[...]
    dst = dst_ref[...]
    sender = _fold_pick(ext_ref, src_ref[...], fold)
    receiver = _fold_pick(own_ref, dst, fold)
    pre = jnp.dot(edge, alpha_ref[0:width], preferred_element_type=jnp.float32)
    pre = pre + jnp.dot(sender, alpha_ref[width : 2 * width], preferred_element_type=jnp.float32)
    pre = pre + jnp.dot(receiver, alpha_ref[2 * width :], preferred_element_type=jnp.float32)
    first = _silu(pre).astype(jnp.bfloat16)
    second = _silu(jnp.dot(first, beta_ref[...], preferred_element_type=jnp.float32)).astype(
        jnp.bfloat16
    )
    third = jnp.dot(second, gamma_ref[...], preferred_element_type=jnp.float32)
    row_mean = jnp.mean(third, axis=-1, keepdims=True)
    centred = third - row_mean
    row_var = jnp.mean(centred * centred, axis=-1, keepdims=True)
    normed = centred * lax.rsqrt(row_var + 1e-05) * gain_ref[...]
    edge_new = (edge.astype(jnp.float32) + normed).astype(jnp.bfloat16)
    position = scalars[1] + step * chunk + lax.broadcasted_iota(jnp.int32, (chunk, 1), 0)
    live = position < scalars[2]
    messages = jnp.where(live, edge_new, jnp.zeros_like(edge_new))
    lane = jnp.bitwise_and(dst, fold - 1)
    spread = jnp.concatenate(
        [jnp.where(lane == j, messages, jnp.zeros_like(messages)) for j in range(fold)], axis=1
    )
    groups = out_ref.shape[0]
    shift = fold.bit_length() - 1
    hot_t = (
        lax.broadcasted_iota(jnp.int32, (groups, chunk), 0)
        == lax.shift_right_logical(dst_row_ref[0], shift)
    ).astype(jnp.bfloat16)
    out_ref[...] += jnp.dot(hot_t, spread, preferred_element_type=jnp.float32)


def edge_messages(edges, send_ids, recv_ids, extended, own_rows, alpha, beta, gamma, gain,
                  first_row, share, tally, chunk=1024, fold=FOLD):
    slots, width = edges.shape
    nodes = own_rows.shape[0] * fold
    turns = share // chunk
    scalars = jnp.stack([first_row // chunk, first_row, tally]).astype(jnp.int32)
    both_ids = lax.dynamic_slice_in_dim(jnp.stack([send_ids, recv_ids]), first_row, share, 1)
    columns = both_ids.reshape(2, share, 1)
    recv_ids = both_ids[1]
    ext_wide = extended
    own_wide = own_rows
    full = lambda shape: pl.BlockSpec(shape, lambda i, s: (0,) * len(shape))
    grid_spec = pltpu.PrefetchScalarGridSpec(
        num_scalar_prefetch=1,
        grid=(turns,),
        in_specs=[
            pl.BlockSpec((chunk, width), lambda i, s: (s[0] + i, 0)),
            pl.BlockSpec((chunk, 1), lambda i, s: (i, 0)),
            pl.BlockSpec((chunk, 1), lambda i, s: (i, 0)),
            pl.BlockSpec((1, 1, chunk), lambda i, s: (i, 0, 0)),
            full(ext_wide.shape),
            full(own_wide.shape),
            full(alpha.shape),
            full(beta.shape),
            full(gamma.shape),
            full((1, width)),
        ],
        out_specs=full((nodes // fold, fold * width)),
    )
    total = pl.pallas_call(
        functools.partial(_edge_kernel, fold),
        out_shape=jax.ShapeDtypeStruct((nodes // fold, fold * width), jnp.float32),
        grid_spec=grid_spec,
    )(
        scalars,
        edges,
        columns[0],
        columns[1],
        recv_ids.reshape(turns, 1, chunk),
        ext_wide,
        own_wide,
        alpha,
        beta,
        gamma,
        gain.reshape(1, width).astype(jnp.float32),
    )
    return total


def psum_slices(numer, denom):
    joined = jnp.concatenate([numer.reshape(-1), denom.reshape(-1)])
    rows = -(-joined.shape[0] // 1024) * 8
    padded = jnp.zeros((rows * 128,), joined.dtype).at[: joined.shape[0]].set(joined)
    total = dom_sum(padded.reshape(rows, 128)).reshape(-1)
    numer_size = numer.size
    return (
        total[:numer_size].reshape(numer.shape),
        total[numer_size : numer_size + denom.size].reshape(denom.shape),
    )


def layer_norm(values, gain_row):
    row_mean = jnp.mean(values, axis=-1, keepdims=True)
    centred = values - row_mean
    row_var = jnp.mean(centred * centred, axis=-1, keepdims=True)
    return centred * lax.rsqrt(row_var + 1e-05) * gain_row


def node_section(
    own_rows,
    summed_b,
    vertex_layer_alpha,
    vertex_layer_beta,
    vertex_layer_gamma,
    vertex_scale_factor,
):
    feature_width = own_rows.shape[1]
    node_pre = jnp.dot(
        own_rows, vertex_layer_alpha[:feature_width], preferred_element_type=jnp.float32
    )
    node_pre = node_pre + jnp.dot(
        summed_b, vertex_layer_alpha[feature_width:], preferred_element_type=jnp.float32
    )
    node_one = jax.nn.silu(node_pre).astype(jnp.bfloat16)
    node_two = jax.nn.silu(
        jnp.dot(node_one, vertex_layer_beta, preferred_element_type=jnp.float32)
    ).astype(jnp.bfloat16)
    node_three = jnp.dot(node_two, vertex_layer_gamma, preferred_element_type=jnp.float32)
    return (own_rows.astype(jnp.float32) + layer_norm(node_three, vertex_scale_factor)).astype(
        jnp.bfloat16
    )


def slice_partial_terms(
    refreshed_vertices,
    focus_scale_factor,
    vertex_content_factor,
    cluster_affinity_factor,
    softness_level,
):
    count_of_rows = refreshed_vertices.shape[0]
    domain_channel_split = softness_level.shape[0]
    standardised_entries = layer_norm(
        refreshed_vertices.astype(jnp.float32), focus_scale_factor
    ).astype(jnp.bfloat16)
    values = jnp.dot(
        standardised_entries, vertex_content_factor, preferred_element_type=jnp.float32
    ).astype(jnp.bfloat16)
    cluster_affinities = jnp.dot(
        standardised_entries, cluster_affinity_factor, preferred_element_type=jnp.float32
    )
    cluster_affinities = (
        cluster_affinities.reshape(count_of_rows, domain_channel_split, GROUPS_PER_LANE)
        / softness_level[None, :, None]
    )
    weights = jax.nn.softmax(cluster_affinities, axis=-1)
    weights_b = weights.astype(jnp.bfloat16)
    numer = jnp.einsum(
        "nhs,nhc->hsc",
        weights_b,
        values.reshape(count_of_rows, domain_channel_split, HEAD_DIM),
        preferred_element_type=jnp.float32,
    )
    denom = jnp.sum(weights, axis=0)
    return (weights_b, numer, denom)


def slice_mixing(numer, denom, cluster_probe_lookup, cluster_content_linear):
    tokens = numer / denom[:, :, None]
    highest = lax.Precision.HIGHEST
    query = jnp.einsum("hsc,hcd->hsd", tokens, cluster_probe_lookup[0], precision=highest)
    keys = jnp.einsum("hsc,hcd->hsd", tokens, cluster_probe_lookup[1], precision=highest)
    carried = jnp.einsum("hsc,hcd->hsd", tokens, cluster_content_linear, precision=highest)
    scores = jnp.einsum("hsd,htd->hst", query, keys, precision=highest) / math.sqrt(HEAD_DIM)
    mixing = jax.nn.softmax(scores, axis=-1)
    return jnp.einsum("hst,htd->hsd", mixing, carried, precision=highest).astype(jnp.bfloat16)


def attend_rows(weights_b, slice_out):
    count_of_rows = weights_b.shape[0]
    domain_channel_split = weights_b.shape[1]
    attended = jnp.einsum("nhs,hsd->nhd", weights_b, slice_out, preferred_element_type=jnp.float32)
    return attended.reshape(count_of_rows, domain_channel_split * HEAD_DIM).astype(jnp.bfloat16)


def pick_rows(table, row_ids):
    table_ids = jnp.arange(table.shape[0], dtype=jnp.int32)
    selector = (row_ids[:, None] == table_ids[None, :]).astype(jnp.bfloat16)
    return jnp.dot(selector, table, preferred_element_type=jnp.float32).astype(jnp.bfloat16)


def gather_rows(table, row_ids, fold):
    count, width = table.shape
    wide = table.reshape(count // fold, fold * width)
    hot = (row_ids[:, None] // fold == jnp.arange(count // fold, dtype=jnp.int32)[None, :]).astype(
        jnp.bfloat16
    )
    picked = jnp.dot(hot, wide, preferred_element_type=jnp.float32)
    lane = row_ids % fold
    rows = picked[:, :width]
    for j in range(1, fold):
        rows = jnp.where((lane == j)[:, None], picked[:, j * width : (j + 1) * width], rows)
    return rows.astype(jnp.bfloat16)


def scatter_rows(messages, row_ids, count, fold):
    width = messages.shape[1]
    lane = row_ids % fold
    spread = jnp.concatenate(
        [jnp.where((lane == j)[:, None], messages, jnp.zeros_like(messages)) for j in range(fold)],
        axis=1,
    )
    hot = (row_ids[:, None] // fold == jnp.arange(count // fold, dtype=jnp.int32)[None, :]).astype(
        jnp.bfloat16
    )
    total = lax.dot_general(
        hot, spread, (((0,), (0,)), ((), ())), preferred_element_type=jnp.float32
    )
    return total.reshape(count, width)


def body(
    vertex_state,
    link_state_slotted,
    source_vertex_ids,
    target_vertex_ids,
    active_link_tally,
    halo_outgoing_ids,
    link_layer_alpha,
    link_layer_beta,
    link_layer_gamma,
    link_scale_factor,
    vertex_layer_alpha,
    vertex_layer_beta,
    vertex_layer_gamma,
    vertex_scale_factor,
    focus_scale_factor,
    vertex_content_factor,
    cluster_affinity_factor,
    softness_level,
    cluster_probe_lookup,
    cluster_content_linear,
    closing_linear_factor,
):
    node_count = vertex_state.shape[0]
    feature_width = vertex_state.shape[1]
    capacity = link_state_slotted.shape[0]
    offsets = (1, -1, 2, -2)
    own_wide = vertex_state.reshape(node_count // FOLD, FOLD * feature_width)
    picked_ids = halo_outgoing_ids[0].reshape(-1, FOLD)
    outgoing = jnp.concatenate(
        [pick_rows(vertex_state, picked_ids[:, j]) for j in range(FOLD)], axis=1
    )
    extended = exchange_halos(own_wide, outgoing, offsets)
    share = capacity // lax.axis_size("head")
    first_row = lax.axis_index("head") * share
    total = edge_messages(
        link_state_slotted,
        source_vertex_ids,
        target_vertex_ids,
        extended,
        own_wide,
        link_layer_alpha,
        link_layer_beta,
        link_layer_gamma,
        link_scale_factor,
        first_row,
        share,
        active_link_tally[0],
    )
    summed = sibling_sum(total.astype(jnp.bfloat16), 2).astype(jnp.bfloat16)
    summed = summed.reshape(vertex_state.shape)
    refreshed_vertices = node_section(
        vertex_state,
        summed.astype(jnp.bfloat16),
        vertex_layer_alpha,
        vertex_layer_beta,
        vertex_layer_gamma,
        vertex_scale_factor,
    )
    weights_b, numer, denom = slice_partial_terms(
        refreshed_vertices,
        focus_scale_factor,
        vertex_content_factor,
        cluster_affinity_factor,
        softness_level,
    )
    numer, denom = psum_slices(numer, denom)
    slice_out = slice_mixing(numer, denom, cluster_probe_lookup, cluster_content_linear)
    attended = attend_rows(weights_b, slice_out)
    projected = sibling_sum(
        jnp.dot(attended, closing_linear_factor, preferred_element_type=jnp.float32).astype(
            jnp.bfloat16
        ),
        3,
    )
    return (refreshed_vertices.astype(jnp.float32) + projected.astype(jnp.float32)).astype(
        jnp.bfloat16
    )


def solution(mesh):
    in_specs = (
        P("dom", None),
        P("dom", None),
        P("dom"),
        P("dom"),
        P("dom"),
        P("dom", None, None),
        P(),
        P(),
        P(),
        P(),
        P(),
        P(),
        P(),
        P(),
        P(),
        P(None, "head"),
        P(None, "head"),
        P("head"),
        P(None, "head", None, None),
        P("head", None, None),
        P("head", None),
    )
    out_specs = P("dom", None)
    return jax.shard_map(body, mesh=mesh, in_specs=in_specs, out_specs=out_specs, check_vma=False)
```

```python
import functools
import math

import jax
import jax.numpy as jnp
from jax import lax
from jax.experimental import pallas as pl
from jax.experimental.pallas import tpu as pltpu
from jax.sharding import PartitionSpec as P

HEAD_DIM = 16
GROUPS_PER_LANE = 64
FOLD = 4


def passed_along(value, axis, steps):
    count = lax.axis_size(axis)
    first, last = (max(0, -steps), min(count, count - steps))
    return lax.ppermute(value, axis, [(source, source + steps) for source in range(first, last)])


def _radix_kernel(radix, steps, x_ref, o_ref, inbox, send_sem, recv_sem):
    me = lax.axis_index("dom")
    spans = [radix**s for s in range(steps)]
    digits = [(me // span) % radix for span in spans]
    partners = [
        [me + ((digit + j) % radix - digit) * span for j in range(1, radix)]
        for digit, span in zip(digits, spans)
    ]
    barrier = pltpu.get_barrier_semaphore()
    for group in partners:
        for partner in group:
            pl.semaphore_signal(
                barrier, 1, device_id={"dom": partner}, device_id_type=pl.DeviceIdType.MESH
            )
    pl.semaphore_wait(barrier, steps * (radix - 1))
    for s in range(steps):
        source = x_ref if s == 0 else o_ref
        copies = []
        for j, partner in enumerate(partners[s]):
            copy = pltpu.make_async_remote_copy(
                src_ref=source,
                dst_ref=inbox.at[s, digits[s]],
                send_sem=send_sem.at[s, j],
                recv_sem=recv_sem.at[s, digits[s]],
                device_id={"dom": partner},
                device_id_type=pl.DeviceIdType.MESH,
            )
            copy.start()
            copies.append(copy)
        inbox[s, digits[s]] = source[...]
        for copy in copies:
            copy.wait_send()
        for j, partner in enumerate(partners[s]):
            slot = (digits[s] + j + 1) % radix
            pltpu.make_async_remote_copy(
                src_ref=source,
                dst_ref=inbox.at[s, slot],
                send_sem=send_sem.at[s, j],
                recv_sem=recv_sem.at[s, slot],
                device_id={"dom": partner},
                device_id_type=pl.DeviceIdType.MESH,
            ).wait_recv()
        total = inbox[s, 0]
        for d in range(1, radix):
            total = total + inbox[s, d]
        o_ref[...] = total


def dom_sum(flat):
    count = lax.axis_size("dom")
    radix = 8
    steps = 0
    while radix ** (steps + 1) <= count:
        steps += 1
    assert radix**steps == count
    return pl.pallas_call(
        functools.partial(_radix_kernel, radix, steps),
        out_shape=jax.ShapeDtypeStruct(flat.shape, flat.dtype),
        in_specs=[pl.BlockSpec(memory_space=pltpu.VMEM)],
        out_specs=pl.BlockSpec(memory_space=pltpu.VMEM),
        scratch_shapes=[
            pltpu.VMEM((steps, radix) + flat.shape, flat.dtype),
            pltpu.SemaphoreType.DMA((steps, radix - 1)),
            pltpu.SemaphoreType.DMA((steps, radix)),
        ],
        compiler_params=pltpu.CompilerParams(collective_id=0, has_side_effects=True),
    )(flat)


def _halo_kernel(offsets, own_ref, out_ref, ext_ref, send_sem, recv_sem, pass_sem, land_sem):
    me = lax.axis_index("dom")
    count = lax.axis_size("dom")
    core = lax.axis_index("head")
    sibling = 1 - core
    rows = own_ref.shape[0]
    halo = out_ref.shape[0] // len(offsets)
    half = halo // 2
    mesh_ids = pl.DeviceIdType.MESH
    barrier = pltpu.get_barrier_semaphore()
    for offset in offsets:
        pl.semaphore_signal(
            barrier, 1, device_id={"dom": (me + offset + count) % count}, device_id_type=mesh_ids
        )
    pl.semaphore_signal(barrier, 1, device_id={"head": sibling}, device_id_type=mesh_ids)
    pl.semaphore_wait(barrier, len(offsets) + 1)
    sends = []
    for k, offset in enumerate(offsets):
        copy = pltpu.make_async_remote_copy(
            src_ref=out_ref.at[pl.ds(k * halo + core * half, half)],
            dst_ref=ext_ref.at[pl.ds(rows + k * halo + core * half, half)],
            send_sem=send_sem.at[k],
            recv_sem=recv_sem.at[k],
            device_id={"dom": (me + offset + count) % count},
            device_id_type=mesh_ids,
        )
        copy.start()
        sends.append(copy)
    ext_ref[pl.ds(0, rows)] = own_ref[...]
    passes = []
    for k in range(len(offsets)):
        sends[k].wait_recv()
        forward = pltpu.make_async_remote_copy(
            src_ref=ext_ref.at[pl.ds(rows + k * halo + core * half, half)],
            dst_ref=ext_ref.at[pl.ds(rows + k * halo + core * half, half)],
            send_sem=pass_sem.at[k],
            recv_sem=land_sem.at[k],
            device_id={"head": sibling},
            device_id_type=mesh_ids,
        )
        forward.start()
        passes.append(forward)
    for copy in sends:
        copy.wait_send()
    for forward in passes:
        forward.wait()
    for k, offset in enumerate(offsets):
        if offset > 0:
            inside = (me + count - offset) // count
        else:
            inside = (2 * count - 1 + offset - me) // count
        slot = pl.ds(rows + k * halo, halo)
        ext_ref[slot] = ext_ref[slot] * inside.astype(ext_ref.dtype)


def exchange_halos(own_rows, outgoing, offsets):
    total = own_rows.shape[0] + outgoing.shape[0]
    return pl.pallas_call(
        functools.partial(_halo_kernel, offsets),
        out_shape=jax.ShapeDtypeStruct((total, own_rows.shape[1]), own_rows.dtype),
        in_specs=[pl.BlockSpec(memory_space=pltpu.VMEM)] * 2,
        out_specs=pl.BlockSpec(memory_space=pltpu.VMEM),
        scratch_shapes=[pltpu.SemaphoreType.DMA((len(offsets),))] * 4,
        compiler_params=pltpu.CompilerParams(collective_id=1, has_side_effects=True),
    )(own_rows, outgoing)


def _sibling_kernel(x_ref, o_ref, inbox, send_sem, recv_sem):
    sibling = 1 - lax.axis_index("head")
    mesh_ids = pl.DeviceIdType.MESH
    barrier = pltpu.get_barrier_semaphore()
    pl.semaphore_signal(barrier, 1, device_id={"head": sibling}, device_id_type=mesh_ids)
    pl.semaphore_wait(barrier, 1)
    copy = pltpu.make_async_remote_copy(
        src_ref=x_ref,
        dst_ref=inbox,
        send_sem=send_sem,
        recv_sem=recv_sem,
        device_id={"head": sibling},
        device_id_type=mesh_ids,
    )
    copy.start()
    copy.wait()
    o_ref[...] = x_ref[...].astype(o_ref.dtype) + inbox[...].astype(o_ref.dtype)


def sibling_sum(x, collective_id):
    return pl.pallas_call(
        _sibling_kernel,
        out_shape=jax.ShapeDtypeStruct(x.shape, jnp.float32),
        in_specs=[pl.BlockSpec(memory_space=pltpu.VMEM)],
        out_specs=pl.BlockSpec(memory_space=pltpu.VMEM),
        scratch_shapes=[
            pltpu.VMEM(x.shape, x.dtype),
            pltpu.SemaphoreType.DMA(()),
            pltpu.SemaphoreType.DMA(()),
        ],
        compiler_params=pltpu.CompilerParams(
            collective_id=collective_id, has_side_effects=True
        ),
    )(x)


def _silu(values):
    return values * (1.0 / (1.0 + jnp.exp(-values)))


def _fold_pick(table_ref, ids, fold):
    chunk = ids.shape[0]
    groups = table_ref.shape[0]
    width = table_ref.shape[1] // fold
    shift = fold.bit_length() - 1
    hot = (
        lax.shift_right_logical(ids, shift) == lax.broadcasted_iota(jnp.int32, (chunk, groups), 1)
    ).astype(jnp.bfloat16)
    picked = jnp.dot(hot, table_ref[...], preferred_element_type=jnp.float32)
    lane = jnp.bitwise_and(ids, fold - 1)
    rows = picked[:, :width]
    for j in range(1, fold):
        rows = jnp.where(lane == j, picked[:, j * width : (j + 1) * width], rows)
    return rows.astype(jnp.bfloat16)


def _edge_kernel(fold, scalars, edge_ref, ids_ref, dst_row_ref, ext_ref, own_ref,
                 alpha_ref, beta_ref, gamma_ref, gain_ref, out_ref):
    step = pl.program_id(0)
    chunk, width = edge_ref.shape

    @pl.when(step == 0)
    def _():
        out_ref[...] = jnp.zeros_like(out_ref)

    edge = edge_ref[...]
    dst = ids_ref[1]
    sender = _fold_pick(ext_ref, ids_ref[0], fold)
    receiver = _fold_pick(own_ref, dst, fold)
    pre = jnp.dot(edge, alpha_ref[0:width], preferred_element_type=jnp.float32)
    pre = pre + jnp.dot(sender, alpha_ref[width : 2 * width], preferred_element_type=jnp.float32)
    pre = pre + jnp.dot(receiver, alpha_ref[2 * width :], preferred_element_type=jnp.float32)
    first = _silu(pre).astype(jnp.bfloat16)
    second = _silu(jnp.dot(first, beta_ref[...], preferred_element_type=jnp.float32)).astype(
        jnp.bfloat16
    )
    third = jnp.dot(second, gamma_ref[...], preferred_element_type=jnp.float32)
    row_mean = jnp.mean(third, axis=-1, keepdims=True)
    centred = third - row_mean
    row_var = jnp.mean(centred * centred, axis=-1, keepdims=True)
    normed = centred * lax.rsqrt(row_var + 1e-05) * gain_ref[...]
    edge_new = (edge.astype(jnp.float32) + normed).astype(jnp.bfloat16)
    position = scalars[1] + step * chunk + lax.broadcasted_iota(jnp.int32, (chunk, 1), 0)
    live = position < scalars[2]
    messages = jnp.where(live, edge_new, jnp.zeros_like(edge_new))
    lane = jnp.bitwise_and(dst, fold - 1)
    spread = jnp.concatenate(
        [jnp.where(lane == j, messages, jnp.zeros_like(messages)) for j in range(fold)], axis=1
    )
    groups = out_ref.shape[0]
    shift = fold.bit_length() - 1
    hot_t = (
        lax.broadcasted_iota(jnp.int32, (groups, chunk), 0)
        == lax.shift_right_logical(dst_row_ref[0], shift)
    ).astype(jnp.bfloat16)
    out_ref[...] += jnp.dot(hot_t, spread, preferred_element_type=jnp.float32)


def edge_messages(edges, send_ids, recv_ids, extended, own_rows, alpha, beta, gamma, gain,
                  first_row, share, tally, chunk=1024, fold=FOLD):
    slots, width = edges.shape
    nodes = own_rows.shape[0] * fold
    turns = share // chunk
    scalars = jnp.stack([first_row // chunk, first_row, tally]).astype(jnp.int32)
    both_ids = lax.dynamic_slice_in_dim(jnp.stack([send_ids, recv_ids]), first_row, share, 1)
    columns = both_ids.reshape(2, share, 1)
    recv_ids = both_ids[1]
    ext_wide = extended
    own_wide = own_rows
    full = lambda shape: pl.BlockSpec(shape, lambda i, s: (0,) * len(shape))
    grid_spec = pltpu.PrefetchScalarGridSpec(
        num_scalar_prefetch=1,
        grid=(turns,),
        in_specs=[
            pl.BlockSpec((chunk, width), lambda i, s: (s[0] + i, 0)),
            pl.BlockSpec((2, chunk, 1), lambda i, s: (0, i, 0)),
            pl.BlockSpec((1, 1, chunk), lambda i, s: (i, 0, 0)),
            full(ext_wide.shape),
            full(own_wide.shape),
            full(alpha.shape),
            full(beta.shape),
            full(gamma.shape),
            full((1, width)),
        ],
        out_specs=full((nodes // fold, fold * width)),
    )
    total = pl.pallas_call(
        functools.partial(_edge_kernel, fold),
        out_shape=jax.ShapeDtypeStruct((nodes // fold, fold * width), jnp.float32),
        grid_spec=grid_spec,
    )(
        scalars,
        edges,
        columns,
        recv_ids.reshape(turns, 1, chunk),
        ext_wide,
        own_wide,
        alpha,
        beta,
        gamma,
        gain.reshape(1, width).astype(jnp.float32),
    )
    return total


def psum_slices(numer, denom):
    joined = jnp.concatenate([numer.reshape(-1), denom.reshape(-1)])
    rows = -(-joined.shape[0] // 1024) * 8
    padded = jnp.zeros((rows * 128,), joined.dtype).at[: joined.shape[0]].set(joined)
    total = dom_sum(padded.reshape(rows, 128)).reshape(-1)
    numer_size = numer.size
    return (
        total[:numer_size].reshape(numer.shape),
        total[numer_size : numer_size + denom.size].reshape(denom.shape),
    )


def layer_norm(values, gain_row):
    row_mean = jnp.mean(values, axis=-1, keepdims=True)
    centred = values - row_mean
    row_var = jnp.mean(centred * centred, axis=-1, keepdims=True)
    return centred * lax.rsqrt(row_var + 1e-05) * gain_row


def node_section(
    own_rows,
    summed_b,
    vertex_layer_alpha,
    vertex_layer_beta,
    vertex_layer_gamma,
    vertex_scale_factor,
):
    feature_width = own_rows.shape[1]
    node_pre = jnp.dot(
        own_rows, vertex_layer_alpha[:feature_width], preferred_element_type=jnp.float32
    )
    node_pre = node_pre + jnp.dot(
        summed_b, vertex_layer_alpha[feature_width:], preferred_element_type=jnp.float32
    )
    node_one = jax.nn.silu(node_pre).astype(jnp.bfloat16)
    node_two = jax.nn.silu(
        jnp.dot(node_one, vertex_layer_beta, preferred_element_type=jnp.float32)
    ).astype(jnp.bfloat16)
    node_three = jnp.dot(node_two, vertex_layer_gamma, preferred_element_type=jnp.float32)
    return (own_rows.astype(jnp.float32) + layer_norm(node_three, vertex_scale_factor)).astype(
        jnp.bfloat16
    )


def slice_partial_terms(
    refreshed_vertices,
    focus_scale_factor,
    vertex_content_factor,
    cluster_affinity_factor,
    softness_level,
):
    count_of_rows = refreshed_vertices.shape[0]
    domain_channel_split = softness_level.shape[0]
    standardised_entries = layer_norm(
        refreshed_vertices.astype(jnp.float32), focus_scale_factor
    ).astype(jnp.bfloat16)
    values = jnp.dot(
        standardised_entries, vertex_content_factor, preferred_element_type=jnp.float32
    ).astype(jnp.bfloat16)
    cluster_affinities = jnp.dot(
        standardised_entries, cluster_affinity_factor, preferred_element_type=jnp.float32
    )
    cluster_affinities = (
        cluster_affinities.reshape(count_of_rows, domain_channel_split, GROUPS_PER_LANE)
        / softness_level[None, :, None]
    )
    weights = jax.nn.softmax(cluster_affinities, axis=-1)
    weights_b = weights.astype(jnp.bfloat16)
    numer = jnp.einsum(
        "nhs,nhc->hsc",
        weights_b,
        values.reshape(count_of_rows, domain_channel_split, HEAD_DIM),
        preferred_element_type=jnp.float32,
    )
    denom = jnp.sum(weights, axis=0)
    return (weights_b, numer, denom)


def slice_mixing(numer, denom, cluster_probe_lookup, cluster_content_linear):
    tokens = numer / denom[:, :, None]
    highest = lax.Precision.HIGHEST
    query = jnp.einsum("hsc,hcd->hsd", tokens, cluster_probe_lookup[0], precision=highest)
    keys = jnp.einsum("hsc,hcd->hsd", tokens, cluster_probe_lookup[1], precision=highest)
    carried = jnp.einsum("hsc,hcd->hsd", tokens, cluster_content_linear, precision=highest)
    scores = jnp.einsum("hsd,htd->hst", query, keys, precision=highest) / math.sqrt(HEAD_DIM)
    mixing = jax.nn.softmax(scores, axis=-1)
    return jnp.einsum("hst,htd->hsd", mixing, carried, precision=highest).astype(jnp.bfloat16)


def attend_rows(weights_b, slice_out):
    count_of_rows = weights_b.shape[0]
    domain_channel_split = weights_b.shape[1]
    attended = jnp.einsum("nhs,hsd->nhd", weights_b, slice_out, preferred_element_type=jnp.float32)
    return attended.reshape(count_of_rows, domain_channel_split * HEAD_DIM).astype(jnp.bfloat16)


def pick_rows(table, row_ids):
    table_ids = jnp.arange(table.shape[0], dtype=jnp.int32)
    selector = (row_ids[:, None] == table_ids[None, :]).astype(jnp.bfloat16)
    return jnp.dot(selector, table, preferred_element_type=jnp.float32).astype(jnp.bfloat16)


def gather_rows(table, row_ids, fold):
    count, width = table.shape
    wide = table.reshape(count // fold, fold * width)
    hot = (row_ids[:, None] // fold == jnp.arange(count // fold, dtype=jnp.int32)[None, :]).astype(
        jnp.bfloat16
    )
    picked = jnp.dot(hot, wide, preferred_element_type=jnp.float32)
    lane = row_ids % fold
    rows = picked[:, :width]
    for j in range(1, fold):
        rows = jnp.where((lane == j)[:, None], picked[:, j * width : (j + 1) * width], rows)
    return rows.astype(jnp.bfloat16)


def scatter_rows(messages, row_ids, count, fold):
    width = messages.shape[1]
    lane = row_ids % fold
    spread = jnp.concatenate(
        [jnp.where((lane == j)[:, None], messages, jnp.zeros_like(messages)) for j in range(fold)],
        axis=1,
    )
    hot = (row_ids[:, None] // fold == jnp.arange(count // fold, dtype=jnp.int32)[None, :]).astype(
        jnp.bfloat16
    )
    total = lax.dot_general(
        hot, spread, (((0,), (0,)), ((), ())), preferred_element_type=jnp.float32
    )
    return total.reshape(count, width)


def body(
    vertex_state,
    link_state_slotted,
    source_vertex_ids,
    target_vertex_ids,
    active_link_tally,
    halo_outgoing_ids,
    link_layer_alpha,
    link_layer_beta,
    link_layer_gamma,
    link_scale_factor,
    vertex_layer_alpha,
    vertex_layer_beta,
    vertex_layer_gamma,
    vertex_scale_factor,
    focus_scale_factor,
    vertex_content_factor,
    cluster_affinity_factor,
    softness_level,
    cluster_probe_lookup,
    cluster_content_linear,
    closing_linear_factor,
):
    node_count = vertex_state.shape[0]
    feature_width = vertex_state.shape[1]
    capacity = link_state_slotted.shape[0]
    offsets = (1, -1, 2, -2)
    own_wide = vertex_state.reshape(node_count // FOLD, FOLD * feature_width)
    picked_ids = halo_outgoing_ids[0].reshape(-1, FOLD)
    outgoing = jnp.concatenate(
        [pick_rows(vertex_state, picked_ids[:, j]) for j in range(FOLD)], axis=1
    )
    extended = exchange_halos(own_wide, outgoing, offsets)
    share = capacity // lax.axis_size("head")
    first_row = lax.axis_index("head") * share
    total = edge_messages(
        link_state_slotted,
        source_vertex_ids,
        target_vertex_ids,
        extended,
        own_wide,
        link_layer_alpha,
        link_layer_beta,
        link_layer_gamma,
        link_scale_factor,
        first_row,
        share,
        active_link_tally[0],
    )
    summed = sibling_sum(total, 2).astype(jnp.bfloat16).reshape(vertex_state.shape)
    refreshed_vertices = node_section(
        vertex_state,
        summed.astype(jnp.bfloat16),
        vertex_layer_alpha,
        vertex_layer_beta,
        vertex_layer_gamma,
        vertex_scale_factor,
    )
    weights_b, numer, denom = slice_partial_terms(
        refreshed_vertices,
        focus_scale_factor,
        vertex_content_factor,
        cluster_affinity_factor,
        softness_level,
    )
    numer, denom = psum_slices(numer, denom)
    slice_out = slice_mixing(numer, denom, cluster_probe_lookup, cluster_content_linear)
    attended = attend_rows(weights_b, slice_out)
    projected = sibling_sum(
        jnp.dot(attended, closing_linear_factor, preferred_element_type=jnp.float32).astype(
            jnp.bfloat16
        ),
        3,
    )
    return (refreshed_vertices.astype(jnp.float32) + projected.astype(jnp.float32)).astype(
        jnp.bfloat16
    )


def solution(mesh):
    in_specs = (
        P("dom", None),
        P("dom", None),
        P("dom"),
        P("dom"),
        P("dom"),
        P("dom", None, None),
        P(),
        P(),
        P(),
        P(),
        P(),
        P(),
        P(),
        P(),
        P(),
        P(None, "head"),
        P(None, "head"),
        P("head"),
        P(None, "head", None, None),
        P("head", None, None),
        P("head", None),
    )
    out_specs = P("dom", None)
    return jax.shard_map(body, mesh=mesh, in_specs=in_specs, out_specs=out_specs, check_vma=False)
```

```python
import functools
import math

import jax
import jax.numpy as jnp
from jax import lax
from jax.experimental import pallas as pl
from jax.experimental.pallas import tpu as pltpu
from jax.sharding import PartitionSpec as P

HEAD_DIM = 16
GROUPS_PER_LANE = 64
FOLD = 4


def passed_along(value, axis, steps):
    count = lax.axis_size(axis)
    first, last = (max(0, -steps), min(count, count - steps))
    return lax.ppermute(value, axis, [(source, source + steps) for source in range(first, last)])


def _radix_kernel(radix, steps, x_ref, o_ref, inbox, send_sem, recv_sem):
    me = lax.axis_index("dom")
    spans = [radix**s for s in range(steps)]
    digits = [(me // span) % radix for span in spans]
    partners = [
        [me + ((digit + j) % radix - digit) * span for j in range(1, radix)]
        for digit, span in zip(digits, spans)
    ]
    barrier = pltpu.get_barrier_semaphore()
    for group in partners:
        for partner in group:
            pl.semaphore_signal(
                barrier, 1, device_id={"dom": partner}, device_id_type=pl.DeviceIdType.MESH
            )
    pl.semaphore_wait(barrier, steps * (radix - 1))
    for s in range(steps):
        source = x_ref if s == 0 else o_ref
        copies = []
        for j, partner in enumerate(partners[s]):
            copy = pltpu.make_async_remote_copy(
                src_ref=source,
                dst_ref=inbox.at[s, digits[s]],
                send_sem=send_sem.at[s, j],
                recv_sem=recv_sem.at[s, digits[s]],
                device_id={"dom": partner},
                device_id_type=pl.DeviceIdType.MESH,
            )
            copy.start()
            copies.append(copy)
        inbox[s, digits[s]] = source[...]
        for copy in copies:
            copy.wait_send()
        for j, partner in enumerate(partners[s]):
            slot = (digits[s] + j + 1) % radix
            pltpu.make_async_remote_copy(
                src_ref=source,
                dst_ref=inbox.at[s, slot],
                send_sem=send_sem.at[s, j],
                recv_sem=recv_sem.at[s, slot],
                device_id={"dom": partner},
                device_id_type=pl.DeviceIdType.MESH,
            ).wait_recv()
        total = inbox[s, 0]
        for d in range(1, radix):
            total = total + inbox[s, d]
        o_ref[...] = total


def dom_sum(flat):
    count = lax.axis_size("dom")
    radix = 8
    steps = 0
    while radix ** (steps + 1) <= count:
        steps += 1
    assert radix**steps == count
    return pl.pallas_call(
        functools.partial(_radix_kernel, radix, steps),
        out_shape=jax.ShapeDtypeStruct(flat.shape, flat.dtype),
        in_specs=[pl.BlockSpec(memory_space=pltpu.VMEM)],
        out_specs=pl.BlockSpec(memory_space=pltpu.VMEM),
        scratch_shapes=[
            pltpu.VMEM((steps, radix) + flat.shape, flat.dtype),
            pltpu.SemaphoreType.DMA((steps, radix - 1)),
            pltpu.SemaphoreType.DMA((steps, radix)),
        ],
        compiler_params=pltpu.CompilerParams(collective_id=0, has_side_effects=True),
    )(flat)


def _halo_kernel(offsets, own_ref, out_ref, ext_ref, send_sem, recv_sem, pass_sem, land_sem):
    me = lax.axis_index("dom")
    count = lax.axis_size("dom")
    core = lax.axis_index("head")
    sibling = 1 - core
    rows = own_ref.shape[0]
    halo = out_ref.shape[0] // len(offsets)
    half = halo // 2
    mesh_ids = pl.DeviceIdType.MESH
    barrier = pltpu.get_barrier_semaphore()
    for offset in offsets:
        pl.semaphore_signal(
            barrier, 1, device_id={"dom": (me + offset + count) % count}, device_id_type=mesh_ids
        )
    pl.semaphore_signal(barrier, 1, device_id={"head": sibling}, device_id_type=mesh_ids)
    pl.semaphore_wait(barrier, len(offsets) + 1)
    sends = []
    for k, offset in enumerate(offsets):
        copy = pltpu.make_async_remote_copy(
            src_ref=out_ref.at[pl.ds(k * halo + core * half, half)],
            dst_ref=ext_ref.at[pl.ds(rows + k * halo + core * half, half)],
            send_sem=send_sem.at[k],
            recv_sem=recv_sem.at[k],
            device_id={"dom": (me + offset + count) % count},
            device_id_type=mesh_ids,
        )
        copy.start()
        sends.append(copy)
    ext_ref[pl.ds(0, rows)] = own_ref[...]
    passes = []
    for k in range(len(offsets)):
        sends[k].wait_recv()
        forward = pltpu.make_async_remote_copy(
            src_ref=ext_ref.at[pl.ds(rows + k * halo + core * half, half)],
            dst_ref=ext_ref.at[pl.ds(rows + k * halo + core * half, half)],
            send_sem=pass_sem.at[k],
            recv_sem=land_sem.at[k],
            device_id={"head": sibling},
            device_id_type=mesh_ids,
        )
        forward.start()
        passes.append(forward)
    for copy in sends:
        copy.wait_send()
    for forward in passes:
        forward.wait()
    for k, offset in enumerate(offsets):
        if offset > 0:
            inside = (me + count - offset) // count
        else:
            inside = (2 * count - 1 + offset - me) // count
        slot = pl.ds(rows + k * halo, halo)
        ext_ref[slot] = ext_ref[slot] * inside.astype(ext_ref.dtype)


def exchange_halos(own_rows, outgoing, offsets):
    total = own_rows.shape[0] + outgoing.shape[0]
    return pl.pallas_call(
        functools.partial(_halo_kernel, offsets),
        out_shape=jax.ShapeDtypeStruct((total, own_rows.shape[1]), own_rows.dtype),
        in_specs=[pl.BlockSpec(memory_space=pltpu.VMEM)] * 2,
        out_specs=pl.BlockSpec(memory_space=pltpu.VMEM),
        scratch_shapes=[pltpu.SemaphoreType.DMA((len(offsets),))] * 4,
        compiler_params=pltpu.CompilerParams(collective_id=1, has_side_effects=True),
    )(own_rows, outgoing)


def _sibling_kernel(x_ref, o_ref, inbox, send_sem, recv_sem):
    sibling = 1 - lax.axis_index("head")
    mesh_ids = pl.DeviceIdType.MESH
    barrier = pltpu.get_barrier_semaphore()
    pl.semaphore_signal(barrier, 1, device_id={"head": sibling}, device_id_type=mesh_ids)
    pl.semaphore_wait(barrier, 1)
    copy = pltpu.make_async_remote_copy(
        src_ref=x_ref,
        dst_ref=inbox,
        send_sem=send_sem,
        recv_sem=recv_sem,
        device_id={"head": sibling},
        device_id_type=mesh_ids,
    )
    copy.start()
    copy.wait()
    o_ref[...] = x_ref[...].astype(o_ref.dtype) + inbox[...].astype(o_ref.dtype)


def sibling_sum(x, collective_id):
    return pl.pallas_call(
        _sibling_kernel,
        out_shape=jax.ShapeDtypeStruct(x.shape, jnp.float32),
        in_specs=[pl.BlockSpec(memory_space=pltpu.VMEM)],
        out_specs=pl.BlockSpec(memory_space=pltpu.VMEM),
        scratch_shapes=[
            pltpu.VMEM(x.shape, x.dtype),
            pltpu.SemaphoreType.DMA(()),
            pltpu.SemaphoreType.DMA(()),
        ],
        compiler_params=pltpu.CompilerParams(
            collective_id=collective_id, has_side_effects=True
        ),
    )(x)


def _silu(values):
    return values * (1.0 / (1.0 + jnp.exp(-values)))


def _fold_pick(table_ref, ids, fold):
    chunk = ids.shape[0]
    groups = table_ref.shape[0]
    width = table_ref.shape[1] // fold
    shift = fold.bit_length() - 1
    hot = (
        lax.shift_right_logical(ids, shift) == lax.broadcasted_iota(jnp.int32, (chunk, groups), 1)
    ).astype(jnp.bfloat16)
    picked = jnp.dot(hot, table_ref[...], preferred_element_type=jnp.float32)
    lane = jnp.bitwise_and(ids, fold - 1)
    rows = picked[:, :width]
    for j in range(1, fold):
        rows = jnp.where(lane == j, picked[:, j * width : (j + 1) * width], rows)
    return rows.astype(jnp.bfloat16)


def _edge_kernel(fold, scalars, edge_ref, ids_ref, dst_row_ref, ext_ref, own_ref,
                 alpha_ref, beta_ref, gamma_ref, gain_ref, out_ref):
    step = pl.program_id(0)
    chunk, width = edge_ref.shape

    @pl.when(step == 0)
    def _():
        out_ref[...] = jnp.zeros_like(out_ref)

    edge = edge_ref[...]
    dst = ids_ref[1]
    sender = _fold_pick(ext_ref, ids_ref[0], fold)
    receiver = _fold_pick(own_ref, dst, fold)
    pre = jnp.dot(edge, alpha_ref[0:width], preferred_element_type=jnp.float32)
    pre = pre + jnp.dot(sender, alpha_ref[width : 2 * width], preferred_element_type=jnp.float32)
    pre = pre + jnp.dot(receiver, alpha_ref[2 * width :], preferred_element_type=jnp.float32)
    first = _silu(pre).astype(jnp.bfloat16)
    second = _silu(jnp.dot(first, beta_ref[...], preferred_element_type=jnp.float32)).astype(
        jnp.bfloat16
    )
    third = jnp.dot(second, gamma_ref[...], preferred_element_type=jnp.float32)
    row_mean = jnp.mean(third, axis=-1, keepdims=True)
    centred = third - row_mean
    row_var = jnp.mean(centred * centred, axis=-1, keepdims=True)
    normed = centred * lax.rsqrt(row_var + 1e-05) * gain_ref[...]
    edge_new = (edge.astype(jnp.float32) + normed).astype(jnp.bfloat16)
    position = scalars[1] + step * chunk + lax.broadcasted_iota(jnp.int32, (chunk, 1), 0)
    live = position < scalars[2]
    messages = jnp.where(live, edge_new, jnp.zeros_like(edge_new))
    lane = jnp.bitwise_and(dst, fold - 1)
    spread = jnp.concatenate(
        [jnp.where(lane == j, messages, jnp.zeros_like(messages)) for j in range(fold)], axis=1
    )
    groups = out_ref.shape[0]
    shift = fold.bit_length() - 1
    hot_t = (
        lax.broadcasted_iota(jnp.int32, (groups, chunk), 0)
        == lax.shift_right_logical(dst_row_ref[0], shift)
    ).astype(jnp.bfloat16)
    out_ref[...] += jnp.dot(hot_t, spread, preferred_element_type=jnp.float32)


def edge_messages(edges, send_ids, recv_ids, extended, own_rows, alpha, beta, gamma, gain,
                  first_row, share, tally, chunk=1024, fold=FOLD):
    slots, width = edges.shape
    nodes = own_rows.shape[0] * fold
    turns = share // chunk
    scalars = jnp.stack([first_row // chunk, first_row, tally]).astype(jnp.int32)
    both_ids = lax.dynamic_slice_in_dim(jnp.stack([send_ids, recv_ids]), first_row, share, 1)
    columns = both_ids.reshape(2, share, 1)
    recv_ids = both_ids[1]
    ext_wide = extended
    own_wide = own_rows
    full = lambda shape: pl.BlockSpec(shape, lambda i, s: (0,) * len(shape))
    grid_spec = pltpu.PrefetchScalarGridSpec(
        num_scalar_prefetch=1,
        grid=(turns,),
        in_specs=[
            pl.BlockSpec((chunk, width), lambda i, s: (s[0] + i, 0)),
            pl.BlockSpec((2, chunk, 1), lambda i, s: (0, i, 0)),
            pl.BlockSpec((1, 1, chunk), lambda i, s: (i, 0, 0)),
            full(ext_wide.shape),
            full(own_wide.shape),
            full(alpha.shape),
            full(beta.shape),
            full(gamma.shape),
            full((1, width)),
        ],
        out_specs=full((nodes // fold, fold * width)),
    )
    total = pl.pallas_call(
        functools.partial(_edge_kernel, fold),
        out_shape=jax.ShapeDtypeStruct((nodes // fold, fold * width), jnp.float32),
        grid_spec=grid_spec,
    )(
        scalars,
        edges,
        columns,
        recv_ids.reshape(turns, 1, chunk),
        ext_wide,
        own_wide,
        alpha,
        beta,
        gamma,
        gain.reshape(1, width).astype(jnp.float32),
    )
    return total


def psum_slices(numer, denom):
    joined = jnp.concatenate([numer.reshape(-1), denom.reshape(-1)])
    rows = -(-joined.shape[0] // 1024) * 8
    padded = jnp.zeros((rows * 128,), joined.dtype).at[: joined.shape[0]].set(joined)
    total = dom_sum(padded.reshape(rows, 128)).reshape(-1)
    numer_size = numer.size
    return (
        total[:numer_size].reshape(numer.shape),
        total[numer_size : numer_size + denom.size].reshape(denom.shape),
    )


def layer_norm(values, gain_row):
    row_mean = jnp.mean(values, axis=-1, keepdims=True)
    centred = values - row_mean
    row_var = jnp.mean(centred * centred, axis=-1, keepdims=True)
    return centred * lax.rsqrt(row_var + 1e-05) * gain_row


def node_section(
    own_rows,
    summed_b,
    vertex_layer_alpha,
    vertex_layer_beta,
    vertex_layer_gamma,
    vertex_scale_factor,
):
    feature_width = own_rows.shape[1]
    node_pre = jnp.dot(
        own_rows, vertex_layer_alpha[:feature_width], preferred_element_type=jnp.float32
    )
    node_pre = node_pre + jnp.dot(
        summed_b, vertex_layer_alpha[feature_width:], preferred_element_type=jnp.float32
    )
    node_one = jax.nn.silu(node_pre).astype(jnp.bfloat16)
    node_two = jax.nn.silu(
        jnp.dot(node_one, vertex_layer_beta, preferred_element_type=jnp.float32)
    ).astype(jnp.bfloat16)
    node_three = jnp.dot(node_two, vertex_layer_gamma, preferred_element_type=jnp.float32)
    return (own_rows.astype(jnp.float32) + layer_norm(node_three, vertex_scale_factor)).astype(
        jnp.bfloat16
    )


def slice_partial_terms(
    refreshed_vertices,
    focus_scale_factor,
    vertex_content_factor,
    cluster_affinity_factor,
    softness_level,
):
    count_of_rows = refreshed_vertices.shape[0]
    domain_channel_split = softness_level.shape[0]
    standardised_entries = layer_norm(
        refreshed_vertices.astype(jnp.float32), focus_scale_factor
    ).astype(jnp.bfloat16)
    values = jnp.dot(
        standardised_entries, vertex_content_factor, preferred_element_type=jnp.float32
    ).astype(jnp.bfloat16)
    cluster_affinities = jnp.dot(
        standardised_entries, cluster_affinity_factor, preferred_element_type=jnp.float32
    )
    cluster_affinities = (
        cluster_affinities.reshape(count_of_rows, domain_channel_split, GROUPS_PER_LANE)
        / softness_level[None, :, None]
    )
    weights = jax.nn.softmax(cluster_affinities, axis=-1)
    weights_b = weights.astype(jnp.bfloat16)
    numer = jnp.einsum(
        "nhs,nhc->hsc",
        weights_b,
        values.reshape(count_of_rows, domain_channel_split, HEAD_DIM),
        preferred_element_type=jnp.float32,
    )
    denom = jnp.sum(weights, axis=0)
    return (weights_b, numer, denom)


def slice_mixing(numer, denom, cluster_probe_lookup, cluster_content_linear):
    tokens = numer / denom[:, :, None]
    highest = lax.Precision.HIGHEST
    query = jnp.einsum("hsc,hcd->hsd", tokens, cluster_probe_lookup[0], precision=highest)
    keys = jnp.einsum("hsc,hcd->hsd", tokens, cluster_probe_lookup[1], precision=highest)
    carried = jnp.einsum("hsc,hcd->hsd", tokens, cluster_content_linear, precision=highest)
    scores = jnp.einsum("hsd,htd->hst", query, keys, precision=highest) / math.sqrt(HEAD_DIM)
    mixing = jax.nn.softmax(scores, axis=-1)
    return jnp.einsum("hst,htd->hsd", mixing, carried, precision=highest).astype(jnp.bfloat16)


def attend_rows(weights_b, slice_out):
    count_of_rows = weights_b.shape[0]
    domain_channel_split = weights_b.shape[1]
    attended = jnp.einsum("nhs,hsd->nhd", weights_b, slice_out, preferred_element_type=jnp.float32)
    return attended.reshape(count_of_rows, domain_channel_split * HEAD_DIM).astype(jnp.bfloat16)


def pick_rows(table, row_ids):
    table_ids = jnp.arange(table.shape[0], dtype=jnp.int32)
    selector = (row_ids[:, None] == table_ids[None, :]).astype(jnp.bfloat16)
    return jnp.dot(selector, table, preferred_element_type=jnp.float32).astype(jnp.bfloat16)


def gather_rows(table, row_ids, fold):
    count, width = table.shape
    wide = table.reshape(count // fold, fold * width)
    hot = (row_ids[:, None] // fold == jnp.arange(count // fold, dtype=jnp.int32)[None, :]).astype(
        jnp.bfloat16
    )
    picked = jnp.dot(hot, wide, preferred_element_type=jnp.float32)
    lane = row_ids % fold
    rows = picked[:, :width]
    for j in range(1, fold):
        rows = jnp.where((lane == j)[:, None], picked[:, j * width : (j + 1) * width], rows)
    return rows.astype(jnp.bfloat16)


def scatter_rows(messages, row_ids, count, fold):
    width = messages.shape[1]
    lane = row_ids % fold
    spread = jnp.concatenate(
        [jnp.where((lane == j)[:, None], messages, jnp.zeros_like(messages)) for j in range(fold)],
        axis=1,
    )
    hot = (row_ids[:, None] // fold == jnp.arange(count // fold, dtype=jnp.int32)[None, :]).astype(
        jnp.bfloat16
    )
    total = lax.dot_general(
        hot, spread, (((0,), (0,)), ((), ())), preferred_element_type=jnp.float32
    )
    return total.reshape(count, width)


def body(
    vertex_state,
    link_state_slotted,
    source_vertex_ids,
    target_vertex_ids,
    active_link_tally,
    halo_outgoing_ids,
    link_layer_alpha,
    link_layer_beta,
    link_layer_gamma,
    link_scale_factor,
    vertex_layer_alpha,
    vertex_layer_beta,
    vertex_layer_gamma,
    vertex_scale_factor,
    focus_scale_factor,
    vertex_content_factor,
    cluster_affinity_factor,
    softness_level,
    cluster_probe_lookup,
    cluster_content_linear,
    closing_linear_factor,
):
    node_count = vertex_state.shape[0]
    feature_width = vertex_state.shape[1]
    capacity = link_state_slotted.shape[0]
    offsets = (1, -1, 2, -2)
    own_wide = vertex_state.reshape(node_count // FOLD, FOLD * feature_width)
    picked_ids = halo_outgoing_ids[0].reshape(-1, FOLD)
    outgoing = jnp.concatenate(
        [gather_rows(vertex_state, picked_ids[:, j], FOLD) for j in range(FOLD)], axis=1
    )
    extended = exchange_halos(own_wide, outgoing, offsets)
    share = capacity // lax.axis_size("head")
    first_row = lax.axis_index("head") * share
    total = edge_messages(
        link_state_slotted,
        source_vertex_ids,
        target_vertex_ids,
        extended,
        own_wide,
        link_layer_alpha,
        link_layer_beta,
        link_layer_gamma,
        link_scale_factor,
        first_row,
        share,
        active_link_tally[0],
    )
    summed = sibling_sum(total, 2).astype(jnp.bfloat16).reshape(vertex_state.shape)
    refreshed_vertices = node_section(
        vertex_state,
        summed.astype(jnp.bfloat16),
        vertex_layer_alpha,
        vertex_layer_beta,
        vertex_layer_gamma,
        vertex_scale_factor,
    )
    weights_b, numer, denom = slice_partial_terms(
        refreshed_vertices,
        focus_scale_factor,
        vertex_content_factor,
        cluster_affinity_factor,
        softness_level,
    )
    numer, denom = psum_slices(numer, denom)
    slice_out = slice_mixing(numer, denom, cluster_probe_lookup, cluster_content_linear)
    attended = attend_rows(weights_b, slice_out)
    projected = sibling_sum(
        jnp.dot(attended, closing_linear_factor, preferred_element_type=jnp.float32).astype(
            jnp.bfloat16
        ),
        3,
    )
    return (refreshed_vertices.astype(jnp.float32) + projected.astype(jnp.float32)).astype(
        jnp.bfloat16
    )


def solution(mesh):
    in_specs = (
        P("dom", None),
        P("dom", None),
        P("dom"),
        P("dom"),
        P("dom"),
        P("dom", None, None),
        P(),
        P(),
        P(),
        P(),
        P(),
        P(),
        P(),
        P(),
        P(),
        P(None, "head"),
        P(None, "head"),
        P("head"),
        P(None, "head", None, None),
        P("head", None, None),
        P("head", None),
    )
    out_specs = P("dom", None)
    return jax.shard_map(body, mesh=mesh, in_specs=in_specs, out_specs=out_specs, check_vma=False)
```
